128 devices in a mesh: seq: 8 (over y, x_lo), fsdp: 16 (over z, x_hi, core).
Axes of the slice: x: 4 (x_hi: 2, x_lo: 2; x = x_hi * 2 + x_lo), y: 4, z: 4, core: 2. Of those that a mesh axis runs over, the one named last changes fastest.
Arguments:
- hidden_in: bfloat16 [16, 2048, 1024], P('fsdp', 'seq'), may hold values from -40 to 40
- norm_gain: bfloat16 [1024], P('fsdp'), may hold values from 0.5 to 1.5
- mixer_proj: bfloat16 [1024, 3352], P('fsdp'), may hold values from -0.1875 to 0.1875
- attn_proj: bfloat16 [1024, 768], P('fsdp'), may hold values from -8 to 8
- conv_kernel: bfloat16 [1792, 4], P('fsdp'), may hold values from -1.5 to 1.5
- conv_bias: bfloat16 [1792], P('fsdp'), may hold values from -1.5 to 1.5
- step_bias: float32 [24], replicated, may hold values from -4.6 to -2.3
- decay_log: float32 [24], replicated, may hold values from 0 to 2.77
- skip_gain: float32 [24], replicated, may hold values from 0.5 to 2
- gated_gain: bfloat16 [1536], P('fsdp'), may hold values from 0.5 to 1.5
- mixer_out: bfloat16 [1536, 1024], P('fsdp'), may hold values from -0.15625 to 0.15625
- attn_out: bfloat16 [512, 1024], P('fsdp'), may hold values from -0.75 to 0.75
- ffn_gain: bfloat16 [1024], P('fsdp'), may hold values from 0.5 to 1.5
- gate_up: bfloat16 [1024, 4096], P('fsdp'), may hold values from -0.1875 to 0.1875
- down_proj: bfloat16 [2048, 1024], P('fsdp'), may hold values from -0.125 to 0.125
- out_grad: bfloat16 [16, 2048, 1024], P('fsdp', 'seq'), may hold values from -6 to 6
Outputs:
- block_out: bfloat16 [16, 2048, 1024], P('fsdp', 'seq')
- input_grad: float32 [16, 2048, 1024], P('fsdp', 'seq')
- grad_norm: float32 [1024], P('fsdp')
- grad_mixer: float32 [1024, 3352], P('fsdp')
- grad_attn: float32 [1024, 768], P('fsdp')
- grad_kernel: float32 [1792, 4], P('fsdp')
- grad_convbias: float32 [1792], P('fsdp')
- grad_step: float32 [24], replicated
- grad_decay: float32 [24], replicated
- grad_skip: float32 [24], replicated
- grad_gated: float32 [1536], P('fsdp')
- grad_mixed: float32 [1536, 1024], P('fsdp')
- grad_attended: float32 [512, 1024], P('fsdp')
- grad_ffn: float32 [1024], P('fsdp')
- grad_gateup: float32 [1024, 4096], P('fsdp')
- grad_down: float32 [2048, 1024], P('fsdp')
The draws below stay inside these ranges and needn't reach their ends.
All inputs are finite; a program needn't handle non-finite values.
Results may differ from the reference program's by a relative error of at most 0.024.
Values may be sent and summed in bfloat16 or wider, within the bound.
A program may use at most 192 MiB of HBM per device.

```python
import math
import jax
import jax.numpy as jnp
from jax import lax

D = 1024
MH = 24
NST = 128
QH = 8
KVH = 2
AP = 64
FF = 2048
KCONV = 4
STRETCH = 256
SEQ_LEN = 2048
SEQS = 16
D_SSM = 1536
XBC = 1792
CIN = 3352
CA = 768


def draw_hidden_in(key, part):
    first, second, third = jax.random.split(key, 3)
    shape = (SEQS, SEQ_LEN, D)
    rows = jnp.exp(jax.random.uniform(second, (SEQS, SEQ_LEN, 1), minval=-1.15, maxval=1.15))
    columns = jnp.exp(jax.random.uniform(third, (1, 1, D), minval=-1.15, maxval=1.15))
    base = jnp.clip(jax.random.normal(first, shape), -4.0, 4.0)
    return (base * rows * columns).astype(jnp.bfloat16)


def draw_attn_proj(key, part):
    first = jax.random.fold_in(key, 0)
    base = jnp.clip(jax.random.normal(first, (D, CA)), -6.0, 6.0) / math.sqrt(D)
    return base.astype(jnp.bfloat16)


def level_of(rng, extent, pieces, low, top_value):
    level = 1.0
    for position, parts in pieces:
        draws = jax.random.uniform(jax.random.fold_in(jax.random.fold_in(rng, 6), position), (parts,), jnp.float32, low / len(pieces), top_value / len(pieces))
        level = level * jnp.repeat(jnp.exp(draws), extent[position] // parts).reshape((-1,) + (1,) * (len(extent) - 1 - position))
    return level


def gaussian(own_key, dims, scale, limit, shards=(), held_as=jnp.bfloat16):
    values = jax.random.normal(own_key, dims, jnp.float32) * scale
    if len(shards) > 0:
        values = level_of(own_key, dims, shards, -0.22, 0.18) * values
    return jnp.clip(values, min=-limit, max=limit).astype(held_as)


def setup_inputs(seed: int = 0) -> dict:
    key_list = jax.random.split(jax.random.key(seed), 17)
    return {
        "hidden_in": draw_hidden_in(jax.random.fold_in(key_list[16], 71), 0),
        "norm_gain": jnp.clip(1.0 + 0.1 * jax.random.normal(key_list[1], (D,), jnp.float32), 0.5, 1.5).astype(jnp.bfloat16),
        "mixer_proj": gaussian(key_list[2], (D, CIN), D ** -0.5, 0.1875, ((0, 16),)),
        "attn_proj": draw_attn_proj(jax.random.fold_in(key_list[16], 71), 0),
        "conv_kernel": gaussian(key_list[4], (XBC, KCONV), 0.5, 1.5, ((0, 16),)),
        "conv_bias": gaussian(key_list[5], (XBC,), 0.5, 1.5, ((0, 16),)),
        "step_bias": jnp.clip(jax.random.uniform(key_list[6], (MH,), jnp.float32, -4.6, -2.3), -4.6, -2.3),
        "decay_log": jnp.clip(jax.random.uniform(key_list[7], (MH,), jnp.float32, 0.0, 2.77), 0.0, 2.77),
        "skip_gain": jnp.clip(jax.random.uniform(key_list[8], (MH,), jnp.float32, 0.5, 2.0), 0.5, 2.0),
        "gated_gain": jnp.clip(1.0 + 0.1 * jax.random.normal(key_list[9], (D_SSM,), jnp.float32), 0.5, 1.5).astype(jnp.bfloat16),
        "mixer_out": gaussian(key_list[10], (D_SSM, D), D_SSM ** -0.5, 0.15625, ((0, 16),)),
        "attn_out": gaussian(key_list[11], (QH * AP, D), (QH * AP // 8) ** -0.5, 0.75, ((0, 16),)),
        "ffn_gain": jnp.clip(1.0 + 0.1 * jax.random.normal(key_list[12], (D,), jnp.float32), 0.5, 1.5).astype(jnp.bfloat16),
        "gate_up": gaussian(key_list[13], (D, 2 * FF), D ** -0.5, 0.1875, ((0, 16),)),
        "down_proj": gaussian(key_list[14], (FF, D), FF ** -0.5, 0.125, ((0, 16),)),
        "out_grad": gaussian(key_list[15], (SEQS, SEQ_LEN, D), 1.0, 6.0, ((0, 16), (1, 8))),
    }


EPSILON = 1e-05
THETA = 10000.0
HIGHEST = lax.Precision.HIGHEST

def silu_slope(value):
    sigma = jax.nn.sigmoid(value)
    return sigma * (1.0 + value * (1.0 - sigma))

def rms_scale(value):
    return lax.rsqrt(lax.optimization_barrier(jnp.mean(value * value, axis=1, keepdims=True)) + EPSILON)

def rms_back(grad_normed, normed, scale):
    return scale * (grad_normed - normed * lax.optimization_barrier(jnp.mean(grad_normed * normed, axis=1, keepdims=True)))

def rope_tables(length, width):
    half = width // 2
    inverse = THETA ** (-2.0 * jnp.arange(half).astype(jnp.float32) / width)
    angles = jnp.arange(length).astype(jnp.float32)[:, None] * inverse[None, :]
    return (jnp.cos(angles), jnp.sin(angles))

def rotate(value, cosine, sine):
    half = value.shape[-1] // 2
    first = value[..., :half]
    second = value[..., half:]
    return jnp.concatenate([first * cosine - second * sine, second * cosine + first * sine], axis=-1)

def unrotate(grad, cosine, sine):
    half = grad.shape[-1] // 2
    first = grad[..., :half]
    second = grad[..., half:]
    return jnp.concatenate([first * cosine + second * sine, second * cosine - first * sine], axis=-1)

def conv_apply(signal, kernel, offset):
    length = signal.shape[0]
    taps = kernel.shape[1]
    padded = jnp.pad(signal, ((taps - 1, 0), (0, 0)))
    result = offset[None, :] + jnp.zeros_like(signal)
    for lag in range(taps):
        result = result + kernel[:, lag][None, :] * padded[lag:lag + length]
    return result

def ssd_scan(xinput, delta, decay, bmatrix, cmatrix, skip):
    length, heads, width = xinput.shape
    nstate = bmatrix.shape[1]
    count = length // STRETCH
    xblocks = xinput.reshape(count, STRETCH, heads, width)
    dblocks = delta.reshape(count, STRETCH, heads)
    bblocks = bmatrix.reshape(count, STRETCH, nstate)
    cblocks = cmatrix.reshape(count, STRETCH, nstate)
    cumul = jnp.cumsum(dblocks * decay[None, None, :], axis=1)
    places = jnp.arange(STRETCH)
    lower = places[:, None] >= places[None, :]
    spread = cumul[:, :, None, :] - cumul[:, None, :, :]
    fading = jnp.exp(jnp.where(lower[None, :, :, None], spread, -jnp.inf))
    inner = jnp.einsum('cin,cjn->cij', cblocks, bblocks, precision=HIGHEST)
    mixing = inner[..., None] * fading * dblocks[:, None, :, :]
    y_inner = jnp.einsum('cijh,cjhp->cihp', mixing, xblocks, precision=HIGHEST)
    tails = jnp.exp(cumul[:, -1:, :] - cumul) * dblocks
    fresh = jnp.einsum('cjn,cjh,cjhp->chpn', bblocks, tails, xblocks, precision=HIGHEST)
    totals = jnp.exp(cumul[:, -1, :])

    def advance(state, pair):
        fade, added = pair
        return (fade[:, None, None] * state + added, state)
    _, starts = lax.scan(advance, jnp.zeros((heads, width, nstate), xinput.dtype), (totals, fresh))
    y_outer = jnp.einsum('cin,chpn->cihp', cblocks, starts, precision=HIGHEST) * jnp.exp(cumul)[..., None]
    output = y_inner + y_outer + skip[None, None, :, None] * xblocks
    return output.reshape(length, heads, width)

def mamba_heads(xpart, bcpart, kernel_x, kernel_bc, bias_x, bias_bc, steps_raw, step_bias, decay_log, skip_gain):
    heads = steps_raw.shape[1]
    length = xpart.shape[0]
    nstate = bcpart.shape[1] // 2
    conv_x = jax.nn.silu(conv_apply(xpart, kernel_x, bias_x))
    conv_bc = jax.nn.silu(conv_apply(bcpart, kernel_bc, bias_bc))
    delta = jax.nn.softplus(steps_raw + step_bias[None, :])
    decay = -jnp.exp(decay_log)
    output = ssd_scan(conv_x.reshape(length, heads, -1), delta, decay, conv_bc[:, :nstate], conv_bc[:, nstate:], skip_gain)
    return output.reshape(length, -1)

def attend(query, keys, values, qpos, kpos, scale):
    scores = jnp.dot(query, keys.T, preferred_element_type=jnp.float32) * scale
    scores = jnp.where(kpos[None, :] <= qpos[:, None], scores, -jnp.inf)
    top = lax.optimization_barrier(jnp.max(scores, axis=1, keepdims=True))
    expo = jnp.exp(scores - top)
    total = lax.optimization_barrier(jnp.sum(expo, axis=1, keepdims=True))
    probs = (expo / total).astype(jnp.bfloat16)
    output = jnp.dot(probs, values, preferred_element_type=jnp.float32).astype(jnp.bfloat16)
    return (output, (top + jnp.log(total))[:, 0])

def attend_back(query, keys, values, output, logsum, grad_out, qpos, kpos, scale):
    scores = jnp.dot(query, keys.T, preferred_element_type=jnp.float32) * scale
    scores = jnp.where(kpos[None, :] <= qpos[:, None], scores, -jnp.inf)
    probs = jnp.exp(scores - logsum[:, None])
    grad_values = jnp.dot(probs.astype(jnp.bfloat16).T, grad_out, preferred_element_type=jnp.float32)
    grad_probs = jnp.dot(grad_out, values.T, preferred_element_type=jnp.float32)
    centre = lax.optimization_barrier(jnp.sum(grad_out.astype(jnp.float32) * output.astype(jnp.float32), axis=1, keepdims=True))
    grad_scores = (probs * (grad_probs - centre)).astype(jnp.bfloat16)
    grad_query = jnp.dot(grad_scores, keys, preferred_element_type=jnp.float32) * scale
    grad_keys = jnp.dot(grad_scores.T, query, preferred_element_type=jnp.float32) * scale
    return (grad_query, grad_keys, grad_values)

def token_front(hidden, norm_gain, mixer_proj, attn_proj):
    resid = hidden.astype(jnp.float32)
    scale_one = rms_scale(resid)
    normed_one = resid * scale_one
    normed_in = (normed_one * norm_gain.astype(jnp.float32)).astype(jnp.bfloat16)
    projection = jnp.dot(normed_in, mixer_proj, preferred_element_type=jnp.float32)
    gate_pre = projection[:, :D_SSM]
    xpart = projection[:, D_SSM:2 * D_SSM].astype(jnp.bfloat16)
    bcpart = projection[:, 2 * D_SSM:2 * D_SSM + 2 * NST].astype(jnp.bfloat16)
    steps_raw = projection[:, 2 * D_SSM + 2 * NST:].astype(jnp.bfloat16)
    attend_pre = jnp.dot(normed_in, attn_proj, preferred_element_type=jnp.float32)
    queries = attend_pre[:, :QH * AP].astype(jnp.bfloat16)
    keyvals = attend_pre[:, QH * AP:].astype(jnp.bfloat16)
    return (resid, scale_one, normed_one, normed_in, gate_pre, xpart, bcpart, steps_raw, queries, keyvals)

def token_tail(resid, mixed_y, attn_tok, gate_pre, gated_gain, mixer_out, attn_out, ffn_gain, gate_up, down_proj):
    gated = mixed_y.astype(jnp.float32) * jax.nn.silu(gate_pre)
    scale_two = rms_scale(gated)
    normed_two = gated * scale_two
    normed_mix = (normed_two * gated_gain.astype(jnp.float32)).astype(jnp.bfloat16)
    branch = jnp.dot(normed_mix, mixer_out, preferred_element_type=jnp.float32)
    branch = branch + jnp.dot(attn_tok, attn_out, preferred_element_type=jnp.float32)
    middle = resid + branch
    scale_three = rms_scale(middle)
    normed_three = middle * scale_three
    normed_ffn = (normed_three * ffn_gain.astype(jnp.float32)).astype(jnp.bfloat16)
    gates = jnp.dot(normed_ffn, gate_up, preferred_element_type=jnp.float32)
    gate_half = gates[:, :FF]
    up_half = gates[:, FF:]
    activ = (jax.nn.silu(gate_half) * up_half).astype(jnp.bfloat16)
    block_out = (middle + jnp.dot(activ, down_proj, preferred_element_type=jnp.float32)).astype(jnp.bfloat16)
    saved = (scale_two, normed_two, normed_mix, scale_three, normed_three, normed_ffn, gate_half, up_half, activ)
    return (block_out, saved)

def token_back_tail(out_grad, saved, mixed_y, attn_tok, gate_pre, gated_gain, mixer_out, attn_out, ffn_gain, gate_up, down_proj, layout):
    scale_two, normed_two, normed_mix, scale_three, normed_three, normed_ffn, gate_half, up_half, activ = saved
    grad_activ = jnp.dot(out_grad, down_proj.T, preferred_element_type=jnp.float32)
    grad_down = jnp.dot(layout(activ, 1).T, out_grad, preferred_element_type=jnp.float32)
    grad_gates = jnp.concatenate([grad_activ * up_half * silu_slope(gate_half), grad_activ * jax.nn.silu(gate_half)], axis=1).astype(jnp.bfloat16)
    grad_gateup = jnp.dot(layout(normed_ffn, 1).T, grad_gates, preferred_element_type=jnp.float32)
    grad_nffn = jnp.dot(grad_gates, gate_up.T, preferred_element_type=jnp.float32)
    grad_ffn = lax.optimization_barrier(jnp.sum(grad_nffn * normed_three, axis=0))
    grad_middle = out_grad.astype(jnp.float32) + rms_back(grad_nffn * ffn_gain.astype(jnp.float32), normed_three, scale_three)
    middle_bf = grad_middle.astype(jnp.bfloat16)
    grad_mixed = jnp.dot(layout(normed_mix, 1).T, middle_bf, preferred_element_type=jnp.float32)
    grad_attended = jnp.dot(layout(attn_tok, 1).T, middle_bf, preferred_element_type=jnp.float32)
    grad_nmix = jnp.dot(middle_bf, mixer_out.T, preferred_element_type=jnp.float32)
    grad_otok = jnp.dot(middle_bf, attn_out.T, preferred_element_type=jnp.float32).astype(jnp.bfloat16)
    grad_gated = lax.optimization_barrier(jnp.sum(grad_nmix * normed_two, axis=0))
    grad_gz = rms_back(grad_nmix * gated_gain.astype(jnp.float32), normed_two, scale_two)
    grad_ymix = (grad_gz * jax.nn.silu(gate_pre)).astype(jnp.bfloat16)
    grad_gate = grad_gz * mixed_y.astype(jnp.float32) * silu_slope(gate_pre)
    late = (grad_gated, grad_mixed, grad_attended, grad_ffn, grad_gateup, grad_down)
    return (grad_middle, grad_ymix, grad_otok, grad_gate, late)

def token_back_front(grad_middle, grad_gate, xgrad, bcgrad, stepgrad, qgrad, kvgrad, normed_in, normed_one, scale_one, norm_gain, mixer_proj, attn_proj, layout):
    grad_proj = jnp.concatenate([grad_gate.astype(jnp.bfloat16), xgrad, bcgrad.astype(jnp.bfloat16), stepgrad], axis=1)
    grad_aproj = jnp.concatenate([qgrad, kvgrad.astype(jnp.bfloat16)], axis=1)
    ordered = layout(normed_in, 1).T
    grad_mixer = jnp.dot(ordered, grad_proj, preferred_element_type=jnp.float32)
    grad_attn = jnp.dot(ordered, grad_aproj, preferred_element_type=jnp.float32)
    grad_nin = jnp.dot(grad_proj, mixer_proj.T, preferred_element_type=jnp.float32)
    grad_nin = grad_nin + jnp.dot(grad_aproj, attn_proj.T, preferred_element_type=jnp.float32)
    grad_norm = lax.optimization_barrier(jnp.sum(grad_nin * normed_one, axis=0))
    input_grad = grad_middle + rms_back(grad_nin * norm_gain.astype(jnp.float32), normed_one, scale_one)
    return (input_grad, grad_norm, grad_mixer, grad_attn)

def identity_layout(value, axis):
    return value

def sequence_pass(seq_in, seq_grad, weights, step_bias, decay_log, skip_gain):
    norm_gain, mixer_proj, attn_proj, conv_kernel, conv_bias, gated_gain, mixer_out, attn_out, ffn_gain, gate_up, down_proj = weights
    resid, scale_one, normed_one, normed_in, gate_pre, xpart, bcpart, steps_raw, queries, keyvals = token_front(seq_in, norm_gain, mixer_proj, attn_proj)
    length = seq_in.shape[0]
    mamba_args = (xpart.astype(jnp.float32), bcpart.astype(jnp.float32), conv_kernel[:D_SSM].astype(jnp.float32), conv_kernel[D_SSM:].astype(jnp.float32), conv_bias[:D_SSM].astype(jnp.float32), conv_bias[D_SSM:].astype(jnp.float32), steps_raw.astype(jnp.float32), step_bias, decay_log, skip_gain)
    mamba_y, pullback = jax.vjp(mamba_heads, *mamba_args)
    mixed_y = mamba_y.astype(jnp.bfloat16)
    cosine, sine = rope_tables(length, AP)
    query_rot = rotate(queries.reshape(length, QH, AP).astype(jnp.float32), cosine[:, None, :], sine[:, None, :]).astype(jnp.bfloat16)
    key_rot = rotate(keyvals[:, :KVH * AP].reshape(length, KVH, AP).astype(jnp.float32), cosine[:, None, :], sine[:, None, :]).astype(jnp.bfloat16)
    value_heads = keyvals[:, KVH * AP:].reshape(length, KVH, AP)
    group = QH // KVH
    key_rep = jnp.repeat(key_rot, group, axis=1).transpose(1, 0, 2)
    value_rep = jnp.repeat(value_heads, group, axis=1).transpose(1, 0, 2)
    query_heads = query_rot.transpose(1, 0, 2)
    positions = jnp.arange(length)
    scale = 1.0 / math.sqrt(AP)

    def head_forward(item):
        return attend(item[0], item[1], item[2], positions, positions, scale)
    head_outs, head_lse = lax.map(head_forward, (query_heads, key_rep, value_rep))
    attn_tok = head_outs.transpose(1, 0, 2).reshape(length, QH * AP)
    block_out, saved = token_tail(resid, mixed_y, attn_tok, gate_pre, gated_gain, mixer_out, attn_out, ffn_gain, gate_up, down_proj)
    grad_middle, grad_ymix, grad_otok, grad_gate, late = token_back_tail(seq_grad, saved, mixed_y, attn_tok, gate_pre, gated_gain, mixer_out, attn_out, ffn_gain, gate_up, down_proj, identity_layout)
    xg, bcg, kxg, kbcg, bxg, bbcg, stepg, stepbg, decayg, skipg = pullback(grad_ymix.astype(jnp.float32))
    grad_oheads = grad_otok.reshape(length, QH, AP).transpose(1, 0, 2)

    def head_backward(item):
        return attend_back(item[0], item[1], item[2], item[3], item[4], item[5], positions, positions, scale)
    dquery, dkeys, dvals = lax.map(head_backward, (query_heads, key_rep, value_rep, head_outs, head_lse, grad_oheads))
    qgrad = unrotate(dquery.transpose(1, 0, 2), cosine[:, None, :], sine[:, None, :]).reshape(length, QH * AP).astype(jnp.bfloat16)
    kgrad = unrotate(dkeys.transpose(1, 0, 2), cosine[:, None, :], sine[:, None, :]).reshape(length, KVH, group, AP).sum(axis=2)
    vgrad = dvals.transpose(1, 0, 2).reshape(length, KVH, group, AP).sum(axis=2)
    kvgrad = jnp.concatenate([kgrad.reshape(length, KVH * AP), vgrad.reshape(length, KVH * AP)], axis=1)
    input_grad, grad_norm, grad_mixer, grad_attn = token_back_front(grad_middle, grad_gate, xg.astype(jnp.bfloat16), bcg, stepg.astype(jnp.bfloat16), qgrad, kvgrad, normed_in, normed_one, scale_one, norm_gain, mixer_proj, attn_proj, identity_layout)
    grad_kernel = jnp.concatenate([kxg, kbcg], axis=0)
    grad_convbias = jnp.concatenate([bxg, bbcg], axis=0)
    grads = (grad_norm, grad_mixer, grad_attn, grad_kernel, grad_convbias) + late + (stepbg, decayg, skipg)
    return (block_out, input_grad, grads)

def reference(hidden_in, norm_gain, mixer_proj, attn_proj, conv_kernel, conv_bias, step_bias, decay_log, skip_gain, gated_gain, mixer_out, attn_out, ffn_gain, gate_up, down_proj, out_grad):
    weights = (norm_gain, mixer_proj, attn_proj, conv_kernel, conv_bias, gated_gain, mixer_out, attn_out, ffn_gain, gate_up, down_proj)
    zeros = tuple((jnp.zeros(weight.shape, jnp.float32) for weight in weights))
    zeros = zeros + (jnp.zeros((MH,), jnp.float32), jnp.zeros((MH,), jnp.float32), jnp.zeros((MH,), jnp.float32))

    def one_sequence(carry, item):
        block_out, input_grad, grads = sequence_pass(item[0], item[1], weights, step_bias, decay_log, skip_gain)
        carry = jax.tree.map(lambda total, extra: total + extra, carry, grads)
        return (carry, (block_out, input_grad))
    totals, (outputs, in_grads) = lax.scan(one_sequence, zeros, (hidden_in, out_grad))
    return (outputs, in_grads, totals[0], totals[1], totals[2], totals[3], totals[4], totals[11], totals[12], totals[13], totals[5], totals[6], totals[7], totals[8], totals[9], totals[10])
```

```python
import functools
import math

import jax
import jax.numpy as jnp
from jax import lax
from jax.experimental import pallas as pl
from jax.experimental.pallas import tpu as pltpu
from jax.sharding import PartitionSpec as P

MH = 24
NST = 128
QH = 8
KVH = 2
AP = 64
FF = 2048
D_SSM = 1536
XBC = 1792
CIN = 3352
FRONT = 4224
EPSILON = 1e-05
THETA = 10000.0
HIGHEST = lax.Precision.HIGHEST
F32 = jnp.float32
BF = jnp.bfloat16
NT = (((1,), (1,)), ((), ()))
TN = (((0,), (0,)), ((), ()))


def dot(a, b, dims=(((1,), (0,)), ((), ())), precision=None):
    return lax.dot_general(a, b, dims, preferred_element_type=F32, precision=precision)


def silu_slope(value):
    sigma = jax.nn.sigmoid(value)
    return sigma * (1.0 + value * (1.0 - sigma))


def rms_scale(value):
    return lax.rsqrt(jnp.mean(value * value, axis=1, keepdims=True) + EPSILON)


def rms_back(grad_normed, normed, scale):
    return scale * (grad_normed - normed * jnp.mean(grad_normed * normed, axis=1, keepdims=True))


def head_selector(rows, cols):
    channel = lax.broadcasted_iota(jnp.int32, (rows, cols), 0)
    head = lax.broadcasted_iota(jnp.int32, (rows, cols), 1)
    return jnp.where((channel >= head * AP) & (channel < head * AP + AP), 1.0, 0.0).astype(F32)


def spread_heads(value):
    head = lax.broadcasted_iota(jnp.int32, (128, D_SSM), 0)
    channel = lax.broadcasted_iota(jnp.int32, (128, D_SSM), 1)
    select = jnp.where((channel >= head * AP) & (channel < head * AP + AP), 1.0, 0.0).astype(F32)
    return dot(value, select, precision=HIGHEST)


def gather_heads(value):
    return dot(value, head_selector(D_SSM, 128), precision=HIGHEST)


def conv_pre(ext, taps, bias, length):
    result = bias[...] + taps[3:4, :] * ext[8 : 8 + length, :]
    for lag in range(3):
        result = result + taps[lag : lag + 1, :] * ext[pl.ds(5 + lag, length), :]
    return result


def mamba_first(xbc, halo, steps, taps, bias, sbias, dlog, act_ref, dt_ref, cum_ref, fresh_ref, ext):
    length = xbc.shape[0]
    ext[0:8, :] = halo[...].astype(F32)
    ext[8 : 8 + length, :] = xbc[...].astype(F32)
    conv = conv_pre(ext, taps, bias, length)
    act = conv * jax.nn.sigmoid(conv)
    act_ref[...] = act
    lane = lax.broadcasted_iota(jnp.int32, (length, 128), 1)
    raw = steps[...].astype(F32) + sbias[...]
    dt = jnp.maximum(raw, 0.0) + jnp.log1p(jnp.exp(-jnp.abs(raw)))
    dt = jnp.where(lane < MH, dt, 0.0)
    dt_ref[...] = dt
    row = lax.broadcasted_iota(jnp.int32, (length, length), 0)
    col = lax.broadcasted_iota(jnp.int32, (length, length), 1)
    lower = jnp.where(row >= col, 1.0, 0.0).astype(F32)
    cum = dot(lower, dt * (-jnp.exp(dlog[...])), precision=HIGHEST)
    cum_ref[...] = cum
    weight = spread_heads(jnp.exp(cum[length - 1 : length, :] - cum) * dt)
    scaled = (act[:, :D_SSM] * weight).astype(BF)
    fresh_ref[...] = dot(scaled, act[:, D_SSM : D_SSM + NST].astype(BF), TN).astype(BF)


def mamba_second(act, dt, cum, starts, skip, y_ref):
    length = act.shape[0]
    cumv = cum[...]
    cum_t = cumv.T
    bmat = act[:, D_SSM : D_SSM + NST].astype(BF)
    cmat = act[:, D_SSM + NST :].astype(BF)
    inner = dot(cmat, bmat, NT)
    row = lax.broadcasted_iota(jnp.int32, (length, length), 0)
    col = lax.broadcasted_iota(jnp.int32, (length, length), 1)
    inner = jnp.where(row >= col, inner, 0.0)
    x = act[:, :D_SSM]
    scaled = (x * spread_heads(dt[...])).astype(BF)
    outer = dot(cmat, starts[...], NT) * spread_heads(jnp.exp(cumv))
    base = outer + spread_heads(skip[...]) * x
    for pair in range(MH // 2):
        parts = []
        for h in (2 * pair, 2 * pair + 1):
            fade = jnp.exp(jnp.minimum(cumv[:, h : h + 1] - cum_t[h : h + 1, :], 0.0))
            parts.append(dot((inner * fade).astype(BF), scaled[:, h * AP : h * AP + AP]))
        lanes = slice(pair * 128, pair * 128 + 128)
        y_ref[:, lanes] = (base[:, lanes] + jnp.concatenate(parts, axis=1)).astype(BF)


def mamba_back_first(gy, act, cum, dstart_ref):
    rise = spread_heads(jnp.exp(cum[...]))
    cmat = act[:, D_SSM + NST :].astype(BF)
    dstart_ref[...] = dot((gy[...].astype(F32) * rise).astype(BF), cmat, TN).astype(BF)


def mamba_back_second(
    gy, xbc, halo, act, dt, cum, starts, dends, steps, taps, bias, sbias, dlog, skip,
    dconv_ref, dtaps_ref, dbias_ref, dsteps_ref, dhead_ref, ext, dact,
):
    length = act.shape[0]
    cumv = cum[...]
    dtv = dt[...]
    cum_t = cumv.T
    lane = lax.broadcasted_iota(jnp.int32, (length, 128), 1)
    bmat = act[:, D_SSM : D_SSM + NST].astype(BF)
    cmat = act[:, D_SSM + NST :].astype(BF)
    row = lax.broadcasted_iota(jnp.int32, (length, length), 0)
    col = lax.broadcasted_iota(jnp.int32, (length, length), 1)
    inner_t = jnp.where(col >= row, dot(bmat, cmat, NT), 0.0)
    x = act[:, :D_SSM]
    gyb = gy[...]
    gyf = gyb.astype(F32)
    dt_full = spread_heads(dtv)
    tail = spread_heads(jnp.exp(cumv[length - 1 : length, :] - cumv))
    rise = spread_heads(jnp.exp(cumv))
    xs = x * dt_full
    xsb = xs.astype(BF)
    ginner = jnp.zeros((length, length), F32)
    qcols = jnp.zeros((length, 128), F32)
    rrows = []
    for pair in range(MH // 2):
        parts = []
        for h in (2 * pair, 2 * pair + 1):
            lanes = slice(h * AP, h * AP + AP)
            fade = jnp.exp(jnp.minimum(cum_t[h : h + 1, :] - cumv[:, h : h + 1], 0.0))
            graded = dot(xsb[:, lanes], gyb[:, lanes], NT) * fade
            ginner = ginner + graded
            weighed = graded * inner_t
            rrows.append(jnp.sum(weighed, axis=0, keepdims=True))
            qcols = jnp.where(lane == h, jnp.sum(weighed, axis=1, keepdims=True), qcols)
            parts.append(dot((inner_t * fade).astype(BF), gyb[:, lanes]))
        dact[:, pair * 128 : pair * 128 + 128] = jnp.concatenate(parts, axis=1)
    ginner = jnp.where(col >= row, ginner, 0.0).astype(BF)
    rrows = jnp.concatenate(rrows + [jnp.zeros((128 - MH, length), F32)], axis=0).T
    endb = dends[...]
    startb = starts[...]
    from_end = dot(bmat, endb, NT) * tail
    dxs = dact[:, :D_SSM] + from_end
    reach = gather_heads(xs * from_end)
    outer = dot(cmat, startb, NT) * rise
    dcum = rrows - qcols + gather_heads(gyf * outer) - reach
    total = jnp.exp(cumv[length - 1 : length, :])
    carried = gather_heads_rows(startb, endb) * total + jnp.sum(reach, axis=0, keepdims=True)
    last = lax.broadcasted_iota(jnp.int32, (length, 128), 0) == length - 1
    dcum = dcum + jnp.where(last, carried, 0.0)
    upper = jnp.where(col >= row, 1.0, 0.0).astype(F32)
    rest = dot(upper, dcum, precision=HIGHEST)
    decay = -jnp.exp(dlog[...])
    ddt = gather_heads(x * dxs) + decay * rest
    ddecay = jnp.sum(dtv * rest, axis=0, keepdims=True) * decay
    raw = steps[...].astype(F32) + sbias[...]
    dsteps = jnp.where(lane < MH, ddt * jax.nn.sigmoid(raw), 0.0)
    dsteps_ref[...] = dsteps.astype(BF)
    dskip = gather_heads(jnp.sum(x * gyf, axis=0, keepdims=True))
    dhead_ref[0:1, :] = jnp.sum(dsteps, axis=0, keepdims=True)
    dhead_ref[1:2, :] = ddecay
    dhead_ref[2:3, :] = dskip
    dhead_ref[3:8, :] = jnp.zeros((5, 128), F32)
    dact[:, :D_SSM] = dt_full * dxs + spread_heads(skip[...]) * gyf
    dact[:, D_SSM : D_SSM + NST] = dot((xs * tail).astype(BF), endb) + dot(ginner, cmat)
    dact[:, D_SSM + NST :] = dot((gyf * rise).astype(BF), startb) + dot(ginner, bmat, TN)
    ext[0:8, :] = halo[...].astype(F32)
    ext[8 : 8 + length, :] = xbc[...].astype(F32)
    conv = conv_pre(ext, taps, bias, length)
    dconv = dact[...] * silu_slope(conv)
    dconv_ref[...] = dconv
    dbias_ref[...] = jnp.broadcast_to(jnp.sum(dconv, axis=0, keepdims=True), (8, XBC))
    for lag in range(4):
        dtaps_ref[lag : lag + 1, :] = jnp.sum(
            dconv * ext[pl.ds(5 + lag, length), :], axis=0, keepdims=True
        )
    dtaps_ref[4:8, :] = jnp.zeros((4, XBC), F32)


def gather_heads_rows(a, b):
    product = a.astype(F32) * b.astype(F32)
    per_row = dot(jnp.ones((8, NST), F32), product, NT, precision=HIGHEST)
    return gather_heads(per_row)[0:1, :]


def attend_forward(axis, q, kv, o_ref, lse_ref, acc, top, total):
    me = lax.axis_index(axis)
    block = q.shape[0]
    scale = 1.0 / math.sqrt(AP)
    acc[...] = jnp.zeros_like(acc)
    top[...] = jnp.full(top.shape, -jnp.inf, F32)
    total[...] = jnp.zeros_like(total)
    key_at = lax.broadcasted_iota(jnp.int32, (block, block), 0)
    query_at = lax.broadcasted_iota(jnp.int32, (block, block), 1)

    def step(j, carry):
        rows = pl.ds(pl.multiple_of(j * block, block), block)
        allowed = (key_at + j * block) <= (query_at + me * block)
        for h in range(QH):
            g = h // (QH // KVH)
            keys = kv[rows, g * AP : g * AP + AP]
            values = kv[rows, KVH * AP + g * AP : KVH * AP + g * AP + AP]
            s = dot(keys, q[:, h * AP : h * AP + AP], NT) * scale
            s = jnp.where(allowed, s, -1e30)
            old = top[h : h + 1, :]
            new = jnp.maximum(old, jnp.max(s, axis=0, keepdims=True))
            p = jnp.exp(s - new)
            fix = jnp.exp(old - new)
            top[h : h + 1, :] = new
            total[h : h + 1, :] = total[h : h + 1, :] * fix + jnp.sum(p, axis=0, keepdims=True)
            band = slice(h * AP, h * AP + AP)
            acc[band, :] = acc[band, :] * fix + dot(values, p.astype(BF), TN)
        return carry

    lax.fori_loop(0, me + 1, step, 0)
    lse_ref[...] = top[...] + jnp.log(total[...])
    for pair in range(QH // 2):
        parts = []
        for h in (2 * pair, 2 * pair + 1):
            parts.append(acc[h * AP : h * AP + AP, :] / total[h : h + 1, :])
        o_ref[:, pair * 128 : pair * 128 + 128] = jnp.concatenate(parts, axis=0).T.astype(BF)


def attend_backward(axis, q, kv, o, lse, go, dq_ref, dkv_ref):
    me = lax.axis_index(axis)
    block = q.shape[0]
    scale = 1.0 / math.sqrt(AP)
    dq_ref[...] = jnp.zeros_like(dq_ref)
    dkv_ref[...] = jnp.zeros_like(dkv_ref)
    key_at = lax.broadcasted_iota(jnp.int32, (block, block), 0)
    query_at = lax.broadcasted_iota(jnp.int32, (block, block), 1)
    centred = go[...].astype(F32) * o[...].astype(F32)
    pick_h = lax.broadcasted_iota(jnp.int32, (8, QH * AP), 0)
    pick_c = lax.broadcasted_iota(jnp.int32, (8, QH * AP), 1)
    pick = jnp.where((pick_c >= pick_h * AP) & (pick_c < pick_h * AP + AP), 1.0, 0.0).astype(F32)
    centre = dot(pick, centred, NT, precision=HIGHEST)

    def step(j, carry):
        rows = pl.ds(pl.multiple_of(j * block, block), block)
        allowed = (key_at + j * block) <= (query_at + me * block)
        sums = []
        for g in range(KVH):
            keys = kv[rows, g * AP : g * AP + AP]
            values = kv[rows, KVH * AP + g * AP : KVH * AP + g * AP + AP]
            dk = jnp.zeros((block, AP), F32)
            dv = jnp.zeros((block, AP), F32)
            for h in range(g * (QH // KVH), (g + 1) * (QH // KVH)):
                band = slice(h * AP, h * AP + AP)
                qh = q[:, band]
                gh = go[:, band]
                s = dot(keys, qh, NT) * scale
                p = jnp.exp(jnp.where(allowed, s - lse[h : h + 1, :], -1e30))
                dv = dv + dot(p.astype(BF), gh)
                dp = dot(values, gh, NT)
                ds = (p * (dp - centre[h : h + 1, :])).astype(BF)
                dk = dk + dot(ds, qh)
                dq_ref[:, band] += dot(ds, keys, TN) * scale
            sums.append((dk * scale, dv))
        dkv_ref[rows, 0:128] = jnp.concatenate([sums[0][0], sums[1][0]], axis=1).astype(BF)
        dkv_ref[rows, 128:256] = jnp.concatenate([sums[0][1], sums[1][1]], axis=1).astype(BF)
        return carry

    lax.fori_loop(0, me + 1, step, 0)


def call(kernel, outs, *args, scratch=(), limit=48):
    spec = pl.BlockSpec(memory_space=pltpu.VMEM)
    return pl.pallas_call(
        kernel,
        out_shape=[jax.ShapeDtypeStruct(shape, dtype) for shape, dtype in outs],
        in_specs=[spec] * len(args),
        out_specs=[spec] * len(outs),
        scratch_shapes=list(scratch),
        compiler_params=pltpu.CompilerParams(vmem_limit_bytes=limit << 20),
    )(*args)


def rope_parts(length, start):
    half = AP // 2
    inverse = THETA ** (-2.0 * jnp.arange(half).astype(F32) / AP)
    angles = (start + jnp.arange(length)).astype(F32)[:, None] * inverse[None, :]
    cosine = jnp.cos(angles)
    sine = jnp.sin(angles)
    return jnp.concatenate([cosine, cosine], axis=1), jnp.concatenate([-sine, sine], axis=1)


def swap_halves(value):
    rows, cols = value.shape
    parts = value.reshape(rows, cols // AP, 2, AP // 2)
    return parts[:, :, ::-1, :].reshape(rows, cols)


def pad_lanes(value):
    return jnp.pad(value.astype(F32), (0, 128 - value.shape[0]))[None, :]


def state_scan(packed, seqs):
    states = packed[:, :, :AP, :].astype(F32)
    logs = packed[:, :, AP, 0].astype(F32) + packed[:, :, AP + 1, 0].astype(F32)
    return states, jnp.exp(logs)


def per_device(
    seqs, hidden_in, norm_gain, mixer_proj, attn_proj, conv_kernel, conv_bias, step_bias, decay_log,
    skip_gain, gated_gain, mixer_out, attn_out, ffn_gain, gate_up, down_proj, out_grad,
):
    T = hidden_in.shape[1]
    width = norm_gain.shape[0]
    shards = 1024 // width
    me = lax.axis_index("seq")
    mix_rows, att_rows, down_rows = mixer_out.shape[0], attn_out.shape[0], down_proj.shape[0]

    small = jnp.concatenate(
        [norm_gain, ffn_gain, gated_gain, conv_bias, conv_kernel.T.reshape(-1)]
    )
    slots = width * 104
    small = jnp.pad(small, (0, slots - small.shape[0])).reshape(width, 104)
    front_shard = jnp.concatenate(
        [mixer_proj[:, : D_SSM + XBC], attn_proj, mixer_proj[:, D_SSM + XBC :], small], axis=1
    )
    front = lax.all_gather(front_shard, "fsdp", axis=0, tiled=True)
    tail_shard = jnp.concatenate(
        [
            gate_up[:, :FF],
            gate_up[:, FF:],
            jnp.concatenate([jnp.concatenate([mixer_out, attn_out], axis=0), down_proj], axis=1),
        ],
        axis=0,
    )
    tail_shard, _ = lax.optimization_barrier((tail_shard, front_shard))
    tail = lax.all_gather(tail_shard, "fsdp", axis=0, tiled=False)
    smalls = front.reshape(shards, width, FRONT)[:, :, 4120:].reshape(shards, slots)
    cuts = []
    at = 0
    for size in (width, width, gated_gain.shape[0], conv_bias.shape[0]):
        cuts.append(smalls[:, at : at + size].reshape(1, -1).astype(F32))
        at += size
    gain_one, gain_ffn, gain_gated, bias_all = cuts
    kernel_size = conv_kernel.shape[0]
    taps = smalls[:, at : at + 4 * kernel_size].reshape(shards, 4, kernel_size)
    taps = taps.transpose(1, 0, 2).reshape(4, XBC).astype(F32)
    taps = jnp.pad(taps, ((0, 4), (0, 0)))

    resid = hidden_in[0].astype(F32)
    scale_one = rms_scale(resid)
    normed_one = resid * scale_one
    normed_in = (normed_one * gain_one).astype(BF)
    projection = dot(normed_in, front)
    gate_pre = projection[:, :D_SSM]
    xbc = projection[:, D_SSM : D_SSM + XBC].astype(BF)
    queries = projection[:, 3328:3840].astype(BF)
    keyvals = projection[:, 3840:4096].astype(BF)
    steps = projection[:, 4096:].astype(BF)
    cosine, sine = rope_parts(T, me * T)
    cos_q, sin_q = jnp.tile(cosine, (1, QH)), jnp.tile(sine, (1, QH))
    cos_k, sin_k = jnp.tile(cosine, (1, KVH)), jnp.tile(sine, (1, KVH))
    query_rot = queries.astype(F32)
    query_rot = (query_rot * cos_q + swap_halves(query_rot) * sin_q).astype(BF)
    keys = keyvals[:, : KVH * AP].astype(F32)
    key_rot = (keys * cos_k + swap_halves(keys) * sin_k).astype(BF)
    kv_own = jnp.concatenate([key_rot, keyvals[:, KVH * AP :]], axis=1)
    halo = lax.ppermute(xbc[-8:], "seq", [(i, i + 1) for i in range(seqs - 1)])
    kv_all = lax.all_gather(kv_own, "seq", axis=0, tiled=True)
    sbias, dlog, skip = pad_lanes(step_bias), pad_lanes(decay_log), pad_lanes(skip_gain)
    act, dt, cum, fresh = call(
        mamba_first,
        [((T, XBC), F32), ((T, 128), F32), ((T, 128), F32), ((D_SSM, NST), BF)],
        xbc, halo, steps, taps, bias_all, sbias, dlog,
        scratch=[pltpu.VMEM((T + 8, XBC), F32)],
    )
    heads = MH // seqs
    ends = cum[T - 1, :MH]
    high = ends.astype(BF)
    low = (ends - high.astype(F32)).astype(BF)
    extra = jnp.concatenate([high[:, None, None], low[:, None, None]], axis=1)
    extra = jnp.broadcast_to(jnp.pad(extra, ((0, 0), (0, 14), (0, 0))), (MH, 16, NST))
    packed = jnp.concatenate([fresh.reshape(MH, AP, NST), extra], axis=1)
    packed = lax.all_to_all(
        packed.reshape(seqs, heads, AP + 16, NST), "seq", split_axis=0, concat_axis=0, tiled=True
    )
    states, totals = state_scan(packed, seqs)
    running = jnp.zeros_like(states[0])
    starts = []
    for c in range(seqs):
        starts.append(running.astype(BF))
        running = running * totals[c][:, None, None] + states[c]
    starts = lax.all_to_all(
        jnp.stack(starts), "seq", split_axis=0, concat_axis=0, tiled=True
    ).reshape(D_SSM, NST)
    attn_tok, lse = call(
        functools.partial(attend_forward, "seq"),
        [((T, QH * AP), BF), ((QH, T), F32)],
        query_rot, kv_all,
        scratch=[pltpu.VMEM((QH * AP, T), F32), pltpu.VMEM((QH, T), F32), pltpu.VMEM((QH, T), F32)],
    )
    (mixed_y,) = call(mamba_second, [((T, D_SSM), BF)], act, dt, cum, starts, skip)

    proj_gate = tail[:, :width].reshape(-1, FF)
    proj_up = tail[:, width : 2 * width].reshape(-1, FF)
    low_rows = 2 * width
    out_mixer = tail[:, low_rows : low_rows + mix_rows, :1024].reshape(-1, 1024)
    out_attn = tail[:, low_rows + mix_rows :, :1024].reshape(-1, 1024)
    proj_down = tail[:, low_rows:, 1024:].reshape(-1, 1024)
    mixed = mixed_y.astype(F32)
    gated = mixed * jax.nn.silu(gate_pre)
    scale_two = rms_scale(gated)
    normed_two = gated * scale_two
    normed_mix = (normed_two * gain_gated).astype(BF)
    middle = resid + dot(normed_mix, out_mixer) + dot(attn_tok, out_attn)
    scale_three = rms_scale(middle)
    normed_three = middle * scale_three
    normed_ffn = (normed_three * gain_ffn).astype(BF)
    gate_half = dot(normed_ffn, proj_gate)
    up_half = dot(normed_ffn, proj_up)
    activ = (jax.nn.silu(gate_half) * up_half).astype(BF)
    block_out = (middle + dot(activ, proj_down)).astype(BF)

    ograd = out_grad[0]
    grad_activ = dot(ograd, proj_down, NT)
    grad_down = dot(activ, ograd, TN).astype(BF)
    grad_g = (grad_activ * up_half * silu_slope(gate_half)).astype(BF)
    grad_u = (grad_activ * jax.nn.silu(gate_half)).astype(BF)
    grad_gw = dot(normed_ffn, grad_g, TN).astype(BF)
    grad_uw = dot(normed_ffn, grad_u, TN).astype(BF)
    grad_nffn = dot(grad_g, proj_gate, NT) + dot(grad_u, proj_up, NT)
    grad_ffn = jnp.sum(grad_nffn * normed_three, axis=0)
    grad_middle = ograd.astype(F32) + rms_back(grad_nffn * gain_ffn, normed_three, scale_three)
    middle_bf = grad_middle.astype(BF)
    grad_mixed = dot(normed_mix, middle_bf, TN).astype(BF)
    grad_attended = dot(attn_tok, middle_bf, TN).astype(BF)
    grad_nmix = dot(middle_bf, out_mixer, NT)
    grad_otok = dot(middle_bf, out_attn, NT).astype(BF)
    grad_gated = jnp.sum(grad_nmix * normed_two, axis=0)
    grad_gz = rms_back(grad_nmix * gain_gated, normed_two, scale_two)
    grad_ymix = (grad_gz * jax.nn.silu(gate_pre)).astype(BF)
    grad_gate = (grad_gz * mixed * silu_slope(gate_pre)).astype(BF)
    tail_grad = jnp.concatenate(
        [
            grad_gw.reshape(shards, width, FF),
            grad_uw.reshape(shards, width, FF),
            jnp.concatenate(
                [
                    jnp.concatenate(
                        [
                            grad_mixed.reshape(shards, mix_rows, 1024),
                            grad_attended.reshape(shards, att_rows, 1024),
                        ],
                        axis=1,
                    ),
                    grad_down.reshape(shards, down_rows, 1024),
                ],
                axis=2,
            ),
        ],
        axis=1,
    )
    tail_piece = lax.psum_scatter(tail_grad, "fsdp", scatter_dimension=0, tiled=True)[0]

    (dstart,) = call(mamba_back_first, [((D_SSM, NST), BF)], grad_ymix, act, cum)
    dstarts = lax.all_to_all(
        dstart.reshape(seqs, heads, AP, NST), "seq", split_axis=0, concat_axis=0, tiled=True
    ).astype(F32)
    running = jnp.zeros_like(dstarts[0])
    dends = [None] * seqs
    for c in reversed(range(seqs)):
        dends[c] = running.astype(BF)
        running = running * totals[c][:, None, None] + dstarts[c]
    dends = lax.all_to_all(
        jnp.stack(dends), "seq", split_axis=0, concat_axis=0, tiled=True
    ).reshape(D_SSM, NST)
    dq, dkv = call(
        functools.partial(attend_backward, "seq"),
        [((T, QH * AP), F32), ((kv_all.shape[0], 2 * KVH * AP), BF)],
        query_rot, kv_all, attn_tok, lse, grad_otok,
    )
    dkv = lax.psum_scatter(dkv, "seq", scatter_dimension=0, tiled=True)
    qgrad = (dq * cos_q - swap_halves(dq) * sin_q).astype(BF)
    dk = dkv[:, : KVH * AP].astype(F32)
    kgrad = (dk * cos_k - swap_halves(dk) * sin_k).astype(BF)
    dconv, dtaps, dbias, dsteps, dhead = call(
        mamba_back_second,
        [((T, XBC), F32), ((8, XBC), F32), ((8, XBC), F32), ((T, 128), BF), ((8, 128), F32)],
        grad_ymix, xbc, halo, act, dt, cum, starts, dends, steps, taps, bias_all, sbias, dlog, skip,
        scratch=[pltpu.VMEM((T + 8, XBC), F32), pltpu.VMEM((T, XBC), F32)],
    )
    ahead = lax.ppermute(dconv[:8].astype(BF), "seq", [(i + 1, i) for i in range(seqs - 1)])
    later = jnp.concatenate([dconv, ahead.astype(F32)], axis=0)
    du = taps[3:4] * dconv
    for lag in range(3):
        du = du + taps[lag : lag + 1] * later[3 - lag : 3 - lag + T]
    grad_proj = jnp.concatenate(
        [grad_gate, du.astype(BF), qgrad, kgrad, dkv[:, KVH * AP :], dsteps], axis=1
    )

    grad_front = dot(normed_in, grad_proj, TN).astype(BF)
    grad_nin = dot(grad_proj, front, NT)
    grad_norm = jnp.sum(grad_nin * normed_one, axis=0)
    input_grad = grad_middle + rms_back(grad_nin * gain_one, normed_one, scale_one)
    front_piece = lax.psum_scatter(grad_front, "fsdp", scatter_dimension=0, tiled=True)
    front_sum, tail_sum = lax.psum((front_piece, tail_piece), "seq")
    vectors = jnp.concatenate(
        [
            grad_norm, grad_ffn, grad_gated, dbias[0], dtaps[:4].reshape(-1),
            dhead[0, :MH], dhead[1, :MH], dhead[2, :MH],
        ]
    )
    vectors = lax.psum(vectors, ("seq", "fsdp"))
    pos = lax.axis_index("fsdp")

    def own(start, size, full):
        return lax.dynamic_slice_in_dim(vectors[start : start + full], pos * size, size, 0)

    at = 0
    owned = []
    for size, full in ((width, 1024), (width, 1024), (gated_gain.shape[0], D_SSM), (kernel_size, XBC)):
        owned.append(own(at, size, full))
        at += full
    own_taps = jnp.stack([own(at + lag * XBC, kernel_size, XBC) for lag in range(4)], axis=1)
    at += 4 * XBC
    tail_sum = tail_sum.astype(F32)
    front_sum = front_sum.astype(F32)
    return (
        block_out[None],
        input_grad[None],
        owned[0],
        jnp.concatenate([front_sum[:, : D_SSM + XBC], front_sum[:, 4096:4120]], axis=1),
        front_sum[:, 3328:4096],
        own_taps,
        owned[3],
        vectors[at : at + MH],
        vectors[at + MH : at + 2 * MH],
        vectors[at + 2 * MH : at + 3 * MH],
        owned[2],
        tail_sum[low_rows : low_rows + mix_rows, :1024],
        tail_sum[low_rows + mix_rows :, :1024],
        owned[1],
        jnp.concatenate([tail_sum[:width], tail_sum[width : 2 * width]], axis=1),
        tail_sum[low_rows:, 1024:],
    )


def solution(mesh):
    tokens = P("fsdp", "seq", None)
    vector = P("fsdp")
    matrix = P("fsdp", None)
    in_specs = (
        tokens, vector, matrix, matrix, matrix, vector, P(), P(), P(), vector, matrix, matrix, vector,
        matrix, matrix, tokens,
    )
    out_specs = (
        tokens, tokens, vector, matrix, matrix, matrix, vector, P(), P(), P(), vector, matrix, matrix,
        vector, matrix, matrix,
    )
    return jax.shard_map(
        functools.partial(per_device, mesh.shape["seq"]),
        mesh=mesh, in_specs=in_specs, out_specs=out_specs, check_vma=False,
    )
```

```python
import functools
import math

import jax
import jax.numpy as jnp
from jax import lax
from jax.experimental import pallas as pl
from jax.experimental.pallas import tpu as pltpu
from jax.sharding import PartitionSpec as P

MH = 24
NST = 128
QH = 8
KVH = 2
AP = 64
FF = 2048
D_SSM = 1536
XBC = 1792
CIN = 3352
FRONT = 4224
EPSILON = 1e-05
THETA = 10000.0
HIGHEST = lax.Precision.HIGHEST
F32 = jnp.float32
BF = jnp.bfloat16
NT = (((1,), (1,)), ((), ()))
TN = (((0,), (0,)), ((), ()))


def dot(a, b, dims=(((1,), (0,)), ((), ())), precision=None):
    return lax.dot_general(a, b, dims, preferred_element_type=F32, precision=precision)


def silu_slope(value):
    sigma = jax.nn.sigmoid(value)
    return sigma * (1.0 + value * (1.0 - sigma))


def rms_scale(value):
    return lax.rsqrt(jnp.mean(value * value, axis=1, keepdims=True) + EPSILON)


def rms_back(grad_normed, normed, scale):
    return scale * (grad_normed - normed * jnp.mean(grad_normed * normed, axis=1, keepdims=True))


def head_selector(rows, cols):
    channel = lax.broadcasted_iota(jnp.int32, (rows, cols), 0)
    head = lax.broadcasted_iota(jnp.int32, (rows, cols), 1)
    return jnp.where((channel >= head * AP) & (channel < head * AP + AP), 1.0, 0.0).astype(F32)


def spread_heads(value):
    head = lax.broadcasted_iota(jnp.int32, (128, D_SSM), 0)
    channel = lax.broadcasted_iota(jnp.int32, (128, D_SSM), 1)
    select = jnp.where((channel >= head * AP) & (channel < head * AP + AP), 1.0, 0.0).astype(F32)
    return dot(value, select, precision=HIGHEST)


def gather_heads(value):
    return dot(value, head_selector(D_SSM, 128), precision=HIGHEST)


def conv_pre(ext, taps, bias, length):
    result = bias[...] + taps[3:4, :] * ext[8 : 8 + length, :]
    for lag in range(3):
        result = result + taps[lag : lag + 1, :] * ext[pl.ds(5 + lag, length), :]
    return result


def mamba_first(xbc, halo, steps, taps, bias, sbias, dlog, act_ref, dt_ref, cum_ref, fresh_ref, ext):
    length = xbc.shape[0]
    ext[0:8, :] = halo[...].astype(F32)
    ext[8 : 8 + length, :] = xbc[...].astype(F32)
    conv = conv_pre(ext, taps, bias, length)
    act = conv * jax.nn.sigmoid(conv)
    act_ref[...] = act
    lane = lax.broadcasted_iota(jnp.int32, (length, 128), 1)
    raw = steps[...].astype(F32) + sbias[...]
    dt = jnp.maximum(raw, 0.0) + jnp.log1p(jnp.exp(-jnp.abs(raw)))
    dt = jnp.where(lane < MH, dt, 0.0)
    dt_ref[...] = dt
    row = lax.broadcasted_iota(jnp.int32, (length, length), 0)
    col = lax.broadcasted_iota(jnp.int32, (length, length), 1)
    lower = jnp.where(row >= col, 1.0, 0.0).astype(F32)
    cum = dot(lower, dt * (-jnp.exp(dlog[...])), precision=HIGHEST)
    cum_ref[...] = cum
    weight = spread_heads(jnp.exp(cum[length - 1 : length, :] - cum) * dt)
    scaled = (act[:, :D_SSM] * weight).astype(BF)
    fresh_ref[...] = dot(scaled, act[:, D_SSM : D_SSM + NST].astype(BF), TN).astype(BF)


def mamba_second(act, dt, cum, starts, skip, y_ref):
    length = act.shape[0]
    cumv = cum[...]
    cum_t = cumv.T
    bmat = act[:, D_SSM : D_SSM + NST].astype(BF)
    cmat = act[:, D_SSM + NST :].astype(BF)
    inner = dot(cmat, bmat, NT)
    row = lax.broadcasted_iota(jnp.int32, (length, length), 0)
    col = lax.broadcasted_iota(jnp.int32, (length, length), 1)
    inner = jnp.where(row >= col, inner, 0.0)
    x = act[:, :D_SSM]
    scaled = (x * spread_heads(dt[...])).astype(BF)
    outer = dot(cmat, starts[...], NT) * spread_heads(jnp.exp(cumv))
    base = outer + spread_heads(skip[...]) * x
    for pair in range(MH // 2):
        parts = []
        for h in (2 * pair, 2 * pair + 1):
            fade = jnp.exp(jnp.minimum(cumv[:, h : h + 1] - cum_t[h : h + 1, :], 0.0))
            parts.append(dot((inner * fade).astype(BF), scaled[:, h * AP : h * AP + AP]))
        lanes = slice(pair * 128, pair * 128 + 128)
        y_ref[:, lanes] = (base[:, lanes] + jnp.concatenate(parts, axis=1)).astype(BF)


def mamba_back_first(gy, act, cum, dstart_ref):
    rise = spread_heads(jnp.exp(cum[...]))
    cmat = act[:, D_SSM + NST :].astype(BF)
    dstart_ref[...] = dot((gy[...].astype(F32) * rise).astype(BF), cmat, TN).astype(BF)


def mamba_back_second(
    gy, xbc, halo, act, dt, cum, starts, dends, steps, taps, bias, sbias, dlog, skip,
    dconv_ref, dtaps_ref, dbias_ref, dsteps_ref, dhead_ref, ext, dact,
):
    length = act.shape[0]
    cumv = cum[...]
    dtv = dt[...]
    cum_t = cumv.T
    lane = lax.broadcasted_iota(jnp.int32, (length, 128), 1)
    bmat = act[:, D_SSM : D_SSM + NST].astype(BF)
    cmat = act[:, D_SSM + NST :].astype(BF)
    row = lax.broadcasted_iota(jnp.int32, (length, length), 0)
    col = lax.broadcasted_iota(jnp.int32, (length, length), 1)
    inner_t = jnp.where(col >= row, dot(bmat, cmat, NT), 0.0)
    x = act[:, :D_SSM]
    gyb = gy[...]
    gyf = gyb.astype(F32)
    dt_full = spread_heads(dtv)
    tail = spread_heads(jnp.exp(cumv[length - 1 : length, :] - cumv))
    rise = spread_heads(jnp.exp(cumv))
    xs = x * dt_full
    xsb = xs.astype(BF)
    ginner = jnp.zeros((length, length), F32)
    qcols = jnp.zeros((length, 128), F32)
    rrows = []
    for pair in range(MH // 2):
        parts = []
        for h in (2 * pair, 2 * pair + 1):
            lanes = slice(h * AP, h * AP + AP)
            fade = jnp.exp(jnp.minimum(cum_t[h : h + 1, :] - cumv[:, h : h + 1], 0.0))
            graded = dot(xsb[:, lanes], gyb[:, lanes], NT) * fade
            ginner = ginner + graded
            weighed = graded * inner_t
            rrows.append(jnp.sum(weighed, axis=0, keepdims=True))
            qcols = jnp.where(lane == h, jnp.sum(weighed, axis=1, keepdims=True), qcols)
            parts.append(dot((inner_t * fade).astype(BF), gyb[:, lanes]))
        dact[:, pair * 128 : pair * 128 + 128] = jnp.concatenate(parts, axis=1)
    ginner = jnp.where(col >= row, ginner, 0.0).astype(BF)
    rrows = jnp.concatenate(rrows + [jnp.zeros((128 - MH, length), F32)], axis=0).T
    endb = dends[...]
    startb = starts[...]
    from_end = dot(bmat, endb, NT) * tail
    dxs = dact[:, :D_SSM] + from_end
    reach = gather_heads(xs * from_end)
    outer = dot(cmat, startb, NT) * rise
    dcum = rrows - qcols + gather_heads(gyf * outer) - reach
    total = jnp.exp(cumv[length - 1 : length, :])
    carried = gather_heads_rows(startb, endb) * total + jnp.sum(reach, axis=0, keepdims=True)
    last = lax.broadcasted_iota(jnp.int32, (length, 128), 0) == length - 1
    dcum = dcum + jnp.where(last, carried, 0.0)
    upper = jnp.where(col >= row, 1.0, 0.0).astype(F32)
    rest = dot(upper, dcum, precision=HIGHEST)
    decay = -jnp.exp(dlog[...])
    ddt = gather_heads(x * dxs) + decay * rest
    ddecay = jnp.sum(dtv * rest, axis=0, keepdims=True) * decay
    raw = steps[...].astype(F32) + sbias[...]
    dsteps = jnp.where(lane < MH, ddt * jax.nn.sigmoid(raw), 0.0)
    dsteps_ref[...] = dsteps.astype(BF)
    dskip = gather_heads(jnp.sum(x * gyf, axis=0, keepdims=True))
    dhead_ref[0:1, :] = jnp.sum(dsteps, axis=0, keepdims=True)
    dhead_ref[1:2, :] = ddecay
    dhead_ref[2:3, :] = dskip
    dhead_ref[3:8, :] = jnp.zeros((5, 128), F32)
    dact[:, :D_SSM] = dt_full * dxs + spread_heads(skip[...]) * gyf
    dact[:, D_SSM : D_SSM + NST] = dot((xs * tail).astype(BF), endb) + dot(ginner, cmat)
    dact[:, D_SSM + NST :] = dot((gyf * rise).astype(BF), startb) + dot(ginner, bmat, TN)
    ext[0:8, :] = halo[...].astype(F32)
    ext[8 : 8 + length, :] = xbc[...].astype(F32)
    conv = conv_pre(ext, taps, bias, length)
    dconv = dact[...] * silu_slope(conv)
    dconv_ref[...] = dconv
    dbias_ref[...] = jnp.broadcast_to(jnp.sum(dconv, axis=0, keepdims=True), (8, XBC))
    for lag in range(4):
        dtaps_ref[lag : lag + 1, :] = jnp.sum(
            dconv * ext[pl.ds(5 + lag, length), :], axis=0, keepdims=True
        )
    dtaps_ref[4:8, :] = jnp.zeros((4, XBC), F32)


def gather_heads_rows(a, b):
    product = a.astype(F32) * b.astype(F32)
    per_row = dot(jnp.ones((8, NST), F32), product, NT, precision=HIGHEST)
    return gather_heads(per_row)[0:1, :]


def attend_forward(axis, q, kv, o_ref, lse_ref, acc, top, total):
    me = lax.axis_index(axis)
    block = q.shape[0]
    scale = 1.0 / math.sqrt(AP)
    acc[...] = jnp.zeros_like(acc)
    top[...] = jnp.full(top.shape, -jnp.inf, F32)
    total[...] = jnp.zeros_like(total)
    key_at = lax.broadcasted_iota(jnp.int32, (block, block), 0)
    query_at = lax.broadcasted_iota(jnp.int32, (block, block), 1)

    def step(j, carry):
        rows = pl.ds(pl.multiple_of(j * block, block), block)
        allowed = (key_at + j * block) <= (query_at + me * block)
        for h in range(QH):
            g = h // (QH // KVH)
            keys = kv[rows, g * AP : g * AP + AP]
            values = kv[rows, KVH * AP + g * AP : KVH * AP + g * AP + AP]
            s = dot(keys, q[:, h * AP : h * AP + AP], NT) * scale
            s = jnp.where(allowed, s, -1e30)
            old = top[h : h + 1, :]
            new = jnp.maximum(old, jnp.max(s, axis=0, keepdims=True))
            p = jnp.exp(s - new)
            fix = jnp.exp(old - new)
            top[h : h + 1, :] = new
            total[h : h + 1, :] = total[h : h + 1, :] * fix + jnp.sum(p, axis=0, keepdims=True)
            band = slice(h * AP, h * AP + AP)
            acc[band, :] = acc[band, :] * fix + dot(values, p.astype(BF), TN)
        return carry

    lax.fori_loop(0, me + 1, step, 0)
    lse_ref[...] = top[...] + jnp.log(total[...])
    for pair in range(QH // 2):
        parts = []
        for h in (2 * pair, 2 * pair + 1):
            parts.append(acc[h * AP : h * AP + AP, :] / total[h : h + 1, :])
        o_ref[:, pair * 128 : pair * 128 + 128] = jnp.concatenate(parts, axis=0).T.astype(BF)


def attend_backward(axis, q, kv, o, lse, go, dq_ref, dkv_ref):
    me = lax.axis_index(axis)
    block = q.shape[0]
    scale = 1.0 / math.sqrt(AP)
    dq_ref[...] = jnp.zeros_like(dq_ref)
    dkv_ref[...] = jnp.zeros_like(dkv_ref)
    key_at = lax.broadcasted_iota(jnp.int32, (block, block), 0)
    query_at = lax.broadcasted_iota(jnp.int32, (block, block), 1)
    centred = go[...].astype(F32) * o[...].astype(F32)
    pick_h = lax.broadcasted_iota(jnp.int32, (8, QH * AP), 0)
    pick_c = lax.broadcasted_iota(jnp.int32, (8, QH * AP), 1)
    pick = jnp.where((pick_c >= pick_h * AP) & (pick_c < pick_h * AP + AP), 1.0, 0.0).astype(F32)
    centre = dot(pick, centred, NT, precision=HIGHEST)

    def step(j, carry):
        rows = pl.ds(pl.multiple_of(j * block, block), block)
        allowed = (key_at + j * block) <= (query_at + me * block)
        sums = []
        for g in range(KVH):
            keys = kv[rows, g * AP : g * AP + AP]
            values = kv[rows, KVH * AP + g * AP : KVH * AP + g * AP + AP]
            dk = jnp.zeros((block, AP), F32)
            dv = jnp.zeros((block, AP), F32)
            for h in range(g * (QH // KVH), (g + 1) * (QH // KVH)):
                band = slice(h * AP, h * AP + AP)
                qh = q[:, band]
                gh = go[:, band]
                s = dot(keys, qh, NT) * scale
                p = jnp.exp(jnp.where(allowed, s - lse[h : h + 1, :], -1e30))
                dv = dv + dot(p.astype(BF), gh)
                dp = dot(values, gh, NT)
                ds = (p * (dp - centre[h : h + 1, :])).astype(BF)
                dk = dk + dot(ds, qh)
                dq_ref[:, band] += dot(ds, keys, TN) * scale
            sums.append((dk * scale, dv))
        dkv_ref[rows, 0:128] = jnp.concatenate([sums[0][0], sums[1][0]], axis=1).astype(BF)
        dkv_ref[rows, 128:256] = jnp.concatenate([sums[0][1], sums[1][1]], axis=1).astype(BF)
        return carry

    lax.fori_loop(0, me + 1, step, 0)


def call(kernel, outs, *args, scratch=(), limit=48):
    spec = pl.BlockSpec(memory_space=pltpu.VMEM)
    return pl.pallas_call(
        kernel,
        out_shape=[jax.ShapeDtypeStruct(shape, dtype) for shape, dtype in outs],
        in_specs=[spec] * len(args),
        out_specs=[spec] * len(outs),
        scratch_shapes=list(scratch),
        compiler_params=pltpu.CompilerParams(vmem_limit_bytes=limit << 20),
    )(*args)


def rope_parts(length, start):
    half = AP // 2
    inverse = THETA ** (-2.0 * jnp.arange(half).astype(F32) / AP)
    angles = (start + jnp.arange(length)).astype(F32)[:, None] * inverse[None, :]
    cosine = jnp.cos(angles)
    sine = jnp.sin(angles)
    return jnp.concatenate([cosine, cosine], axis=1), jnp.concatenate([-sine, sine], axis=1)


def swap_halves(value):
    rows, cols = value.shape
    parts = value.reshape(rows, cols // AP, 2, AP // 2)
    return parts[:, :, ::-1, :].reshape(rows, cols)


def pad_lanes(value):
    return jnp.pad(value.astype(F32), (0, 128 - value.shape[0]))[None, :]


def exchange(value):
    return lax.all_to_all(value, "seq", split_axis=0, concat_axis=0, tiled=True)


def share(value, seqs):
    return exchange(jnp.broadcast_to(value[None], (seqs,) + value.shape))


def sum_over(value, seqs):
    rows, cols = value.shape
    parts = exchange(value.reshape(seqs, rows // seqs, cols))
    return share(jnp.sum(parts.astype(F32), axis=0).astype(BF), seqs).reshape(rows, cols)


def state_scan(packed, seqs):
    states = packed[:, :, :AP, :].astype(F32)
    logs = packed[:, :, AP, 0].astype(F32) + packed[:, :, AP + 1, 0].astype(F32)
    return states, jnp.exp(logs)


def per_device(
    seqs, hidden_in, norm_gain, mixer_proj, attn_proj, conv_kernel, conv_bias, step_bias, decay_log,
    skip_gain, gated_gain, mixer_out, attn_out, ffn_gain, gate_up, down_proj, out_grad,
):
    T = hidden_in.shape[1]
    width = norm_gain.shape[0]
    shards = 1024 // width
    me = lax.axis_index("seq")
    mix_rows, att_rows, down_rows = mixer_out.shape[0], attn_out.shape[0], down_proj.shape[0]

    small = jnp.concatenate(
        [norm_gain, ffn_gain, gated_gain, conv_bias, conv_kernel.T.reshape(-1)]
    )
    slots = width * 104
    small = jnp.pad(small, (0, slots - small.shape[0])).reshape(width, 104)
    front_shard = jnp.concatenate(
        [mixer_proj[:, : D_SSM + XBC], attn_proj, mixer_proj[:, D_SSM + XBC :], small], axis=1
    )
    front = lax.all_gather(front_shard, "fsdp", axis=0, tiled=True)
    tail_shard = jnp.concatenate(
        [
            gate_up[:, :FF],
            gate_up[:, FF:],
            jnp.concatenate([jnp.concatenate([mixer_out, attn_out], axis=0), down_proj], axis=1),
        ],
        axis=0,
    )
    tail_shard, _ = lax.optimization_barrier((tail_shard, front_shard))
    tail = lax.all_gather(tail_shard, "fsdp", axis=0, tiled=False)
    smalls = front.reshape(shards, width, FRONT)[:, :, 4120:].reshape(shards, slots)
    cuts = []
    at = 0
    for size in (width, width, gated_gain.shape[0], conv_bias.shape[0]):
        cuts.append(smalls[:, at : at + size].reshape(1, -1).astype(F32))
        at += size
    gain_one, gain_ffn, gain_gated, bias_all = cuts
    kernel_size = conv_kernel.shape[0]
    taps = smalls[:, at : at + 4 * kernel_size].reshape(shards, 4, kernel_size)
    taps = taps.transpose(1, 0, 2).reshape(4, XBC).astype(F32)
    taps = jnp.pad(taps, ((0, 4), (0, 0)))

    resid = hidden_in[0].astype(F32)
    scale_one = rms_scale(resid)
    normed_one = resid * scale_one
    normed_in = (normed_one * gain_one).astype(BF)
    projection = dot(normed_in, front)
    gate_pre = projection[:, :D_SSM]
    xbc = projection[:, D_SSM : D_SSM + XBC].astype(BF)
    queries = projection[:, 3328:3840].astype(BF)
    keyvals = projection[:, 3840:4096].astype(BF)
    steps = projection[:, 4096:].astype(BF)
    cosine, sine = rope_parts(T, me * T)
    cos_q, sin_q = jnp.tile(cosine, (1, QH)), jnp.tile(sine, (1, QH))
    cos_k, sin_k = jnp.tile(cosine, (1, KVH)), jnp.tile(sine, (1, KVH))
    query_rot = queries.astype(F32)
    query_rot = (query_rot * cos_q + swap_halves(query_rot) * sin_q).astype(BF)
    keys = keyvals[:, : KVH * AP].astype(F32)
    key_rot = (keys * cos_k + swap_halves(keys) * sin_k).astype(BF)
    kv_own = jnp.concatenate([key_rot, keyvals[:, KVH * AP :]], axis=1)
    halo = lax.ppermute(xbc[-8:], "seq", [(i, i + 1) for i in range(seqs - 1)])
    kv_all = share(kv_own, seqs).reshape(seqs * T, 2 * KVH * AP)
    sbias, dlog, skip = pad_lanes(step_bias), pad_lanes(decay_log), pad_lanes(skip_gain)
    act, dt, cum, fresh = call(
        mamba_first,
        [((T, XBC), F32), ((T, 128), F32), ((T, 128), F32), ((D_SSM, NST), BF)],
        xbc, halo, steps, taps, bias_all, sbias, dlog,
        scratch=[pltpu.VMEM((T + 8, XBC), F32)],
    )
    heads = MH // seqs
    ends = cum[T - 1, :MH]
    high = ends.astype(BF)
    low = (ends - high.astype(F32)).astype(BF)
    extra = jnp.concatenate([high[:, None, None], low[:, None, None]], axis=1)
    extra = jnp.broadcast_to(jnp.pad(extra, ((0, 0), (0, 14), (0, 0))), (MH, 16, NST))
    packed = jnp.concatenate([fresh.reshape(MH, AP, NST), extra], axis=1)
    packed = lax.all_to_all(
        packed.reshape(seqs, heads, AP + 16, NST), "seq", split_axis=0, concat_axis=0, tiled=True
    )
    states, totals = state_scan(packed, seqs)
    running = jnp.zeros_like(states[0])
    starts = []
    for c in range(seqs):
        starts.append(running.astype(BF))
        running = running * totals[c][:, None, None] + states[c]
    starts = lax.all_to_all(
        jnp.stack(starts), "seq", split_axis=0, concat_axis=0, tiled=True
    ).reshape(D_SSM, NST)
    attn_tok, lse = call(
        functools.partial(attend_forward, "seq"),
        [((T, QH * AP), BF), ((QH, T), F32)],
        query_rot, kv_all,
        scratch=[pltpu.VMEM((QH * AP, T), F32), pltpu.VMEM((QH, T), F32), pltpu.VMEM((QH, T), F32)],
    )
    (mixed_y,) = call(mamba_second, [((T, D_SSM), BF)], act, dt, cum, starts, skip)

    proj_gate = tail[:, :width].reshape(-1, FF)
    proj_up = tail[:, width : 2 * width].reshape(-1, FF)
    low_rows = 2 * width
    out_mixer = tail[:, low_rows : low_rows + mix_rows, :1024].reshape(-1, 1024)
    out_attn = tail[:, low_rows + mix_rows :, :1024].reshape(-1, 1024)
    proj_down = tail[:, low_rows:, 1024:].reshape(-1, 1024)
    mixed = mixed_y.astype(F32)
    gated = mixed * jax.nn.silu(gate_pre)
    scale_two = rms_scale(gated)
    normed_two = gated * scale_two
    normed_mix = (normed_two * gain_gated).astype(BF)
    middle = resid + dot(normed_mix, out_mixer) + dot(attn_tok, out_attn)
    scale_three = rms_scale(middle)
    normed_three = middle * scale_three
    normed_ffn = (normed_three * gain_ffn).astype(BF)
    gate_half = dot(normed_ffn, proj_gate)
    up_half = dot(normed_ffn, proj_up)
    activ = (jax.nn.silu(gate_half) * up_half).astype(BF)
    block_out = (middle + dot(activ, proj_down)).astype(BF)

    ograd = out_grad[0]
    grad_activ = dot(ograd, proj_down, NT)
    grad_down = dot(activ, ograd, TN).astype(BF)
    grad_g = (grad_activ * up_half * silu_slope(gate_half)).astype(BF)
    grad_u = (grad_activ * jax.nn.silu(gate_half)).astype(BF)
    grad_gw = dot(normed_ffn, grad_g, TN).astype(BF)
    grad_uw = dot(normed_ffn, grad_u, TN).astype(BF)
    grad_nffn = dot(grad_g, proj_gate, NT) + dot(grad_u, proj_up, NT)
    grad_ffn = jnp.sum(grad_nffn * normed_three, axis=0)
    grad_middle = ograd.astype(F32) + rms_back(grad_nffn * gain_ffn, normed_three, scale_three)
    middle_bf = grad_middle.astype(BF)
    grad_mixed = dot(normed_mix, middle_bf, TN).astype(BF)
    grad_attended = dot(attn_tok, middle_bf, TN).astype(BF)
    grad_nmix = dot(middle_bf, out_mixer, NT)
    grad_otok = dot(middle_bf, out_attn, NT).astype(BF)
    grad_gated = jnp.sum(grad_nmix * normed_two, axis=0)
    grad_gz = rms_back(grad_nmix * gain_gated, normed_two, scale_two)
    grad_ymix = (grad_gz * jax.nn.silu(gate_pre)).astype(BF)
    grad_gate = (grad_gz * mixed * silu_slope(gate_pre)).astype(BF)
    tail_grad = jnp.concatenate(
        [
            grad_gw.reshape(shards, width, FF),
            grad_uw.reshape(shards, width, FF),
            jnp.concatenate(
                [
                    jnp.concatenate(
                        [
                            grad_mixed.reshape(shards, mix_rows, 1024),
                            grad_attended.reshape(shards, att_rows, 1024),
                        ],
                        axis=1,
                    ),
                    grad_down.reshape(shards, down_rows, 1024),
                ],
                axis=2,
            ),
        ],
        axis=1,
    )
    tail_piece = lax.psum_scatter(tail_grad, "fsdp", scatter_dimension=0, tiled=True)[0]

    (dstart,) = call(mamba_back_first, [((D_SSM, NST), BF)], grad_ymix, act, cum)
    dstarts = lax.all_to_all(
        dstart.reshape(seqs, heads, AP, NST), "seq", split_axis=0, concat_axis=0, tiled=True
    ).astype(F32)
    running = jnp.zeros_like(dstarts[0])
    dends = [None] * seqs
    for c in reversed(range(seqs)):
        dends[c] = running.astype(BF)
        running = running * totals[c][:, None, None] + dstarts[c]
    dends = lax.all_to_all(
        jnp.stack(dends), "seq", split_axis=0, concat_axis=0, tiled=True
    ).reshape(D_SSM, NST)
    dq, dkv = call(
        functools.partial(attend_backward, "seq"),
        [((T, QH * AP), F32), ((kv_all.shape[0], 2 * KVH * AP), BF)],
        query_rot, kv_all, attn_tok, lse, grad_otok,
    )
    dkv = exchange(dkv.reshape(seqs, T, 2 * KVH * AP))
    dkv = jnp.sum(dkv.astype(F32), axis=0).astype(BF)
    qgrad = (dq * cos_q - swap_halves(dq) * sin_q).astype(BF)
    dk = dkv[:, : KVH * AP].astype(F32)
    kgrad = (dk * cos_k - swap_halves(dk) * sin_k).astype(BF)
    dconv, dtaps, dbias, dsteps, dhead = call(
        mamba_back_second,
        [((T, XBC), F32), ((8, XBC), F32), ((8, XBC), F32), ((T, 128), BF), ((8, 128), F32)],
        grad_ymix, xbc, halo, act, dt, cum, starts, dends, steps, taps, bias_all, sbias, dlog, skip,
        scratch=[pltpu.VMEM((T + 8, XBC), F32), pltpu.VMEM((T, XBC), F32)],
    )
    ahead = lax.ppermute(dconv[:8].astype(BF), "seq", [(i + 1, i) for i in range(seqs - 1)])
    later = jnp.concatenate([dconv, ahead.astype(F32)], axis=0)
    du = taps[3:4] * dconv
    for lag in range(3):
        du = du + taps[lag : lag + 1] * later[3 - lag : 3 - lag + T]
    grad_proj = jnp.concatenate(
        [grad_gate, du.astype(BF), qgrad, kgrad, dkv[:, KVH * AP :], dsteps], axis=1
    )

    grad_front = dot(normed_in, grad_proj, TN).astype(BF)
    grad_nin = dot(grad_proj, front, NT)
    grad_norm = jnp.sum(grad_nin * normed_one, axis=0)
    input_grad = grad_middle + rms_back(grad_nin * gain_one, normed_one, scale_one)
    grad_front, tail_piece = lax.optimization_barrier((grad_front, tail_piece))
    front_piece = lax.psum_scatter(grad_front, "fsdp", scatter_dimension=0, tiled=True)
    front_sum, tail_sum = sum_over(front_piece, seqs), sum_over(tail_piece, seqs)
    vectors = jnp.concatenate(
        [
            grad_norm, grad_ffn, grad_gated, dbias[0], dtaps[:4].reshape(-1),
            dhead[0, :MH], dhead[1, :MH], dhead[2, :MH],
        ]
    )
    vectors = lax.psum(vectors, ("seq", "fsdp"))
    pos = lax.axis_index("fsdp")

    def own(start, size, full):
        return lax.dynamic_slice_in_dim(vectors[start : start + full], pos * size, size, 0)

    at = 0
    owned = []
    for size, full in ((width, 1024), (width, 1024), (gated_gain.shape[0], D_SSM), (kernel_size, XBC)):
        owned.append(own(at, size, full))
        at += full
    own_taps = jnp.stack([own(at + lag * XBC, kernel_size, XBC) for lag in range(4)], axis=1)
    at += 4 * XBC
    tail_sum = tail_sum.astype(F32)
    front_sum = front_sum.astype(F32)
    return (
        block_out[None],
        input_grad[None],
        owned[0],
        jnp.concatenate([front_sum[:, : D_SSM + XBC], front_sum[:, 4096:4120]], axis=1),
        front_sum[:, 3328:4096],
        own_taps,
        owned[3],
        vectors[at : at + MH],
        vectors[at + MH : at + 2 * MH],
        vectors[at + 2 * MH : at + 3 * MH],
        owned[2],
        tail_sum[low_rows : low_rows + mix_rows, :1024],
        tail_sum[low_rows + mix_rows :, :1024],
        owned[1],
        jnp.concatenate([tail_sum[:width], tail_sum[width : 2 * width]], axis=1),
        tail_sum[low_rows:, 1024:],
    )


def solution(mesh):
    tokens = P("fsdp", "seq", None)
    vector = P("fsdp")
    matrix = P("fsdp", None)
    in_specs = (
        tokens, vector, matrix, matrix, matrix, vector, P(), P(), P(), vector, matrix, matrix, vector,
        matrix, matrix, tokens,
    )
    out_specs = (
        tokens, tokens, vector, matrix, matrix, matrix, vector, P(), P(), P(), vector, matrix, matrix,
        vector, matrix, matrix,
    )
    return jax.shard_map(
        functools.partial(per_device, mesh.shape["seq"]),
        mesh=mesh, in_specs=in_specs, out_specs=out_specs, check_vma=False,
    )
```

```python
import functools
import math

import jax
import jax.numpy as jnp
from jax import lax
from jax.experimental import pallas as pl
from jax.experimental.pallas import tpu as pltpu
from jax.sharding import PartitionSpec as P

MH = 24
NST = 128
QH = 8
KVH = 2
AP = 64
FF = 2048
D_SSM = 1536
XBC = 1792
CIN = 3352
FRONT = 4224
EPSILON = 1e-05
THETA = 10000.0
HIGHEST = lax.Precision.HIGHEST
F32 = jnp.float32
BF = jnp.bfloat16
NT = (((1,), (1,)), ((), ()))
TN = (((0,), (0,)), ((), ()))


def dot(a, b, dims=(((1,), (0,)), ((), ())), precision=None):
    return lax.dot_general(a, b, dims, preferred_element_type=F32, precision=precision)


def silu_slope(value):
    sigma = jax.nn.sigmoid(value)
    return sigma * (1.0 + value * (1.0 - sigma))


def rms_scale(value):
    return lax.rsqrt(jnp.mean(value * value, axis=1, keepdims=True) + EPSILON)


def rms_back(grad_normed, normed, scale):
    return scale * (grad_normed - normed * jnp.mean(grad_normed * normed, axis=1, keepdims=True))


def head_selector(rows, cols):
    channel = lax.broadcasted_iota(jnp.int32, (rows, cols), 0)
    head = lax.broadcasted_iota(jnp.int32, (rows, cols), 1)
    return jnp.where((channel >= head * AP) & (channel < head * AP + AP), 1.0, 0.0).astype(F32)


def spread_heads(value):
    head = lax.broadcasted_iota(jnp.int32, (128, D_SSM), 0)
    channel = lax.broadcasted_iota(jnp.int32, (128, D_SSM), 1)
    select = jnp.where((channel >= head * AP) & (channel < head * AP + AP), 1.0, 0.0).astype(F32)
    return dot(value, select, precision=HIGHEST)


def gather_heads(value):
    return dot(value, head_selector(D_SSM, 128), precision=HIGHEST)


def conv_pre(ext, taps, bias, length):
    result = bias[...] + taps[3:4, :] * ext[8 : 8 + length, :]
    for lag in range(3):
        result = result + taps[lag : lag + 1, :] * ext[pl.ds(5 + lag, length), :]
    return result


def mamba_first(xbc, halo, steps, taps, bias, sbias, dlog, act_ref, dt_ref, cum_ref, fresh_ref, ext):
    length = xbc.shape[0]
    ext[0:8, :] = halo[...].astype(F32)
    ext[8 : 8 + length, :] = xbc[...].astype(F32)
    conv = conv_pre(ext, taps, bias, length)
    act = conv * jax.nn.sigmoid(conv)
    act_ref[...] = act
    lane = lax.broadcasted_iota(jnp.int32, (length, 128), 1)
    raw = steps[...].astype(F32) + sbias[...]
    dt = jnp.maximum(raw, 0.0) + jnp.log1p(jnp.exp(-jnp.abs(raw)))
    dt = jnp.where(lane < MH, dt, 0.0)
    dt_ref[...] = dt
    row = lax.broadcasted_iota(jnp.int32, (length, length), 0)
    col = lax.broadcasted_iota(jnp.int32, (length, length), 1)
    lower = jnp.where(row >= col, 1.0, 0.0).astype(F32)
    cum = dot(lower, dt * (-jnp.exp(dlog[...])), precision=HIGHEST)
    cum_ref[...] = cum
    weight = spread_heads(jnp.exp(cum[length - 1 : length, :] - cum) * dt)
    scaled = (act[:, :D_SSM] * weight).astype(BF)
    fresh_ref[...] = dot(scaled, act[:, D_SSM : D_SSM + NST].astype(BF), TN).astype(BF)


def mamba_second(act, dt, cum, starts, skip, y_ref):
    length = act.shape[0]
    cumv = cum[...]
    cum_t = cumv.T
    bmat = act[:, D_SSM : D_SSM + NST].astype(BF)
    cmat = act[:, D_SSM + NST :].astype(BF)
    inner = dot(cmat, bmat, NT)
    row = lax.broadcasted_iota(jnp.int32, (length, length), 0)
    col = lax.broadcasted_iota(jnp.int32, (length, length), 1)
    inner = jnp.where(row >= col, inner, 0.0)
    x = act[:, :D_SSM]
    scaled = (x * spread_heads(dt[...])).astype(BF)
    outer = dot(cmat, starts[...], NT) * spread_heads(jnp.exp(cumv))
    base = outer + spread_heads(skip[...]) * x
    for pair in range(MH // 2):
        parts = []
        for h in (2 * pair, 2 * pair + 1):
            fade = jnp.exp(jnp.minimum(cumv[:, h : h + 1] - cum_t[h : h + 1, :], 0.0))
            parts.append(dot((inner * fade).astype(BF), scaled[:, h * AP : h * AP + AP]))
        lanes = slice(pair * 128, pair * 128 + 128)
        y_ref[:, lanes] = (base[:, lanes] + jnp.concatenate(parts, axis=1)).astype(BF)


def mamba_back_first(gy, act, cum, dstart_ref):
    rise = spread_heads(jnp.exp(cum[...]))
    cmat = act[:, D_SSM + NST :].astype(BF)
    dstart_ref[...] = dot((gy[...].astype(F32) * rise).astype(BF), cmat, TN).astype(BF)


def mamba_back_second(
    gy, xbc, halo, act, dt, cum, starts, dends, steps, taps, bias, sbias, dlog, skip,
    dconv_ref, dtaps_ref, dbias_ref, dsteps_ref, dhead_ref, ext, dact,
):
    length = act.shape[0]
    cumv = cum[...]
    dtv = dt[...]
    cum_t = cumv.T
    lane = lax.broadcasted_iota(jnp.int32, (length, 128), 1)
    bmat = act[:, D_SSM : D_SSM + NST].astype(BF)
    cmat = act[:, D_SSM + NST :].astype(BF)
    row = lax.broadcasted_iota(jnp.int32, (length, length), 0)
    col = lax.broadcasted_iota(jnp.int32, (length, length), 1)
    inner_t = jnp.where(col >= row, dot(bmat, cmat, NT), 0.0)
    x = act[:, :D_SSM]
    gyb = gy[...]
    gyf = gyb.astype(F32)
    dt_full = spread_heads(dtv)
    tail = spread_heads(jnp.exp(cumv[length - 1 : length, :] - cumv))
    rise = spread_heads(jnp.exp(cumv))
    xs = x * dt_full
    xsb = xs.astype(BF)
    ginner = jnp.zeros((length, length), F32)
    qcols = jnp.zeros((length, 128), F32)
    rrows = []
    for pair in range(MH // 2):
        parts = []
        for h in (2 * pair, 2 * pair + 1):
            lanes = slice(h * AP, h * AP + AP)
            fade = jnp.exp(jnp.minimum(cum_t[h : h + 1, :] - cumv[:, h : h + 1], 0.0))
            graded = dot(xsb[:, lanes], gyb[:, lanes], NT) * fade
            ginner = ginner + graded
            weighed = graded * inner_t
            rrows.append(jnp.sum(weighed, axis=0, keepdims=True))
            qcols = jnp.where(lane == h, jnp.sum(weighed, axis=1, keepdims=True), qcols)
            parts.append(dot((inner_t * fade).astype(BF), gyb[:, lanes]))
        dact[:, pair * 128 : pair * 128 + 128] = jnp.concatenate(parts, axis=1)
    ginner = jnp.where(col >= row, ginner, 0.0).astype(BF)
    rrows = jnp.concatenate(rrows + [jnp.zeros((128 - MH, length), F32)], axis=0).T
    endb = dends[...]
    startb = starts[...]
    from_end = dot(bmat, endb, NT) * tail
    dxs = dact[:, :D_SSM] + from_end
    reach = gather_heads(xs * from_end)
    outer = dot(cmat, startb, NT) * rise
    dcum = rrows - qcols + gather_heads(gyf * outer) - reach
    total = jnp.exp(cumv[length - 1 : length, :])
    carried = gather_heads_rows(startb, endb) * total + jnp.sum(reach, axis=0, keepdims=True)
    last = lax.broadcasted_iota(jnp.int32, (length, 128), 0) == length - 1
    dcum = dcum + jnp.where(last, carried, 0.0)
    upper = jnp.where(col >= row, 1.0, 0.0).astype(F32)
    rest = dot(upper, dcum, precision=HIGHEST)
    decay = -jnp.exp(dlog[...])
    ddt = gather_heads(x * dxs) + decay * rest
    ddecay = jnp.sum(dtv * rest, axis=0, keepdims=True) * decay
    raw = steps[...].astype(F32) + sbias[...]
    dsteps = jnp.where(lane < MH, ddt * jax.nn.sigmoid(raw), 0.0)
    dsteps_ref[...] = dsteps.astype(BF)
    dskip = gather_heads(jnp.sum(x * gyf, axis=0, keepdims=True))
    dhead_ref[0:1, :] = jnp.sum(dsteps, axis=0, keepdims=True)
    dhead_ref[1:2, :] = ddecay
    dhead_ref[2:3, :] = dskip
    dhead_ref[3:8, :] = jnp.zeros((5, 128), F32)
    dact[:, :D_SSM] = dt_full * dxs + spread_heads(skip[...]) * gyf
    dact[:, D_SSM : D_SSM + NST] = dot((xs * tail).astype(BF), endb) + dot(ginner, cmat)
    dact[:, D_SSM + NST :] = dot((gyf * rise).astype(BF), startb) + dot(ginner, bmat, TN)
    ext[0:8, :] = halo[...].astype(F32)
    ext[8 : 8 + length, :] = xbc[...].astype(F32)
    conv = conv_pre(ext, taps, bias, length)
    dconv = dact[...] * silu_slope(conv)
    dconv_ref[...] = dconv
    dbias_ref[...] = jnp.broadcast_to(jnp.sum(dconv, axis=0, keepdims=True), (8, XBC))
    for lag in range(4):
        dtaps_ref[lag : lag + 1, :] = jnp.sum(
            dconv * ext[pl.ds(5 + lag, length), :], axis=0, keepdims=True
        )
    dtaps_ref[4:8, :] = jnp.zeros((4, XBC), F32)


def gather_heads_rows(a, b):
    product = a.astype(F32) * b.astype(F32)
    per_row = dot(jnp.ones((8, NST), F32), product, NT, precision=HIGHEST)
    return gather_heads(per_row)[0:1, :]


def attend_forward(axis, q, kv, o_ref, lse_ref, acc, top, total):
    me = lax.axis_index(axis)
    block = q.shape[0]
    scale = 1.0 / math.sqrt(AP)
    acc[...] = jnp.zeros_like(acc)
    top[...] = jnp.full(top.shape, -jnp.inf, F32)
    total[...] = jnp.zeros_like(total)
    key_at = lax.broadcasted_iota(jnp.int32, (block, block), 0)
    query_at = lax.broadcasted_iota(jnp.int32, (block, block), 1)

    def step(j, carry):
        rows = pl.ds(pl.multiple_of(j * block, block), block)
        allowed = (key_at + j * block) <= (query_at + me * block)
        for h in range(QH):
            g = h // (QH // KVH)
            keys = kv[rows, g * AP : g * AP + AP]
            values = kv[rows, KVH * AP + g * AP : KVH * AP + g * AP + AP]
            s = dot(keys, q[:, h * AP : h * AP + AP], NT) * scale
            s = jnp.where(allowed, s, -1e30)
            old = top[h : h + 1, :]
            new = jnp.maximum(old, jnp.max(s, axis=0, keepdims=True))
            p = jnp.exp(s - new)
            fix = jnp.exp(old - new)
            top[h : h + 1, :] = new
            total[h : h + 1, :] = total[h : h + 1, :] * fix + jnp.sum(p, axis=0, keepdims=True)
            band = slice(h * AP, h * AP + AP)
            acc[band, :] = acc[band, :] * fix + dot(values, p.astype(BF), TN)
        return carry

    lax.fori_loop(0, me + 1, step, 0)
    lse_ref[...] = top[...] + jnp.log(total[...])
    for pair in range(QH // 2):
        parts = []
        for h in (2 * pair, 2 * pair + 1):
            parts.append(acc[h * AP : h * AP + AP, :] / total[h : h + 1, :])
        o_ref[:, pair * 128 : pair * 128 + 128] = jnp.concatenate(parts, axis=0).T.astype(BF)


def attend_backward(axis, q, kv, o, lse, go, dq_ref, dkv_ref):
    me = lax.axis_index(axis)
    block = q.shape[0]
    scale = 1.0 / math.sqrt(AP)
    dq_ref[...] = jnp.zeros_like(dq_ref)
    dkv_ref[...] = jnp.zeros_like(dkv_ref)
    key_at = lax.broadcasted_iota(jnp.int32, (block, block), 0)
    query_at = lax.broadcasted_iota(jnp.int32, (block, block), 1)
    centred = go[...].astype(F32) * o[...].astype(F32)
    pick_h = lax.broadcasted_iota(jnp.int32, (8, QH * AP), 0)
    pick_c = lax.broadcasted_iota(jnp.int32, (8, QH * AP), 1)
    pick = jnp.where((pick_c >= pick_h * AP) & (pick_c < pick_h * AP + AP), 1.0, 0.0).astype(F32)
    centre = dot(pick, centred, NT, precision=HIGHEST)

    def step(j, carry):
        rows = pl.ds(pl.multiple_of(j * block, block), block)
        allowed = (key_at + j * block) <= (query_at + me * block)
        sums = []
        for g in range(KVH):
            keys = kv[rows, g * AP : g * AP + AP]
            values = kv[rows, KVH * AP + g * AP : KVH * AP + g * AP + AP]
            dk = jnp.zeros((block, AP), F32)
            dv = jnp.zeros((block, AP), F32)
            for h in range(g * (QH // KVH), (g + 1) * (QH // KVH)):
                band = slice(h * AP, h * AP + AP)
                qh = q[:, band]
                gh = go[:, band]
                s = dot(keys, qh, NT) * scale
                p = jnp.exp(jnp.where(allowed, s - lse[h : h + 1, :], -1e30))
                dv = dv + dot(p.astype(BF), gh)
                dp = dot(values, gh, NT)
                ds = (p * (dp - centre[h : h + 1, :])).astype(BF)
                dk = dk + dot(ds, qh)
                dq_ref[:, band] += dot(ds, keys, TN) * scale
            sums.append((dk * scale, dv))
        dkv_ref[rows, 0:128] = jnp.concatenate([sums[0][0], sums[1][0]], axis=1).astype(BF)
        dkv_ref[rows, 128:256] = jnp.concatenate([sums[0][1], sums[1][1]], axis=1).astype(BF)
        return carry

    lax.fori_loop(0, me + 1, step, 0)


def call(kernel, outs, *args, scratch=(), limit=48):
    spec = pl.BlockSpec(memory_space=pltpu.VMEM)
    return pl.pallas_call(
        kernel,
        out_shape=[jax.ShapeDtypeStruct(shape, dtype) for shape, dtype in outs],
        in_specs=[spec] * len(args),
        out_specs=[spec] * len(outs),
        scratch_shapes=list(scratch),
        compiler_params=pltpu.CompilerParams(vmem_limit_bytes=limit << 20),
    )(*args)


def places():
    s, f = lax.axis_index("seq"), lax.axis_index("fsdp")
    return s // 2, s % 2, f // 4, (f // 2) % 2, f % 2


def at_place(y, x_lo, z, x_hi, core):
    return {"seq": y * 2 + x_lo, "fsdp": z * 4 + x_hi * 2 + core}


def greet(others):
    barrier = pltpu.get_barrier_semaphore()
    for other in others:
        pl.semaphore_signal(barrier, inc=1, device_id=other, device_id_type=pl.DeviceIdType.MESH)
    pl.semaphore_wait(barrier, len(others))


WIDTHS = (1024, 1024, 1024, 1152)


def reduce_kernel(g, out, *refs):
    n = len(WIDTHS)
    groups = [refs[i * 10 : i * 10 + 10] for i in range(n)]
    gathered, send, recv, local = refs[n * 10 :]
    y, x_lo, z, x_hi, core = places()
    yn, yp, yo = (y + 1) % 4, (y + 3) % 4, (y + 2) % 4
    zn, zp, zo = (z + 1) % 4, (z + 3) % 4, (z + 2) % 4
    y_next, y_prev = at_place(yn, x_lo, z, x_hi, core), at_place(yp, x_lo, z, x_hi, core)
    y_far = at_place(yo, x_lo, z, x_hi, core)
    z_next, z_prev = at_place(y, x_lo, zn, x_hi, core), at_place(y, x_lo, zp, x_hi, core)
    across = at_place(y, 1 - x_lo, z, 1 - x_hi, core)
    beside = at_place(y, 1 - x_lo, z, x_hi, core)
    twin = at_place(y, x_lo, z, x_hi, 1 - core)
    greet((y_next, y_prev, y_far, z_next, z_prev, across, beside, twin))

    def copy(c, slot, source, target, device):
        return pltpu.make_async_remote_copy(
            src_ref=source, dst_ref=target, send_sem=send.at[c, slot], recv_sem=recv.at[c, slot],
            device_id=device, device_id_type=pl.DeviceIdType.MESH,
        )

    started = []

    def go(c, slot, source, target, device):
        item = copy(c, slot, source, target, device)
        item.start()
        started.append(item)
        return item

    def lanes(c):
        return pl.ds(sum(WIDTHS[:c]), WIDTHS[c])

    first = [[None] * 16 for _ in range(n)]
    loads = []
    for c in range(n):
        acc, twin_buf = groups[c][0], groups[c][1]
        first[c][0] = go(c, 0, g.at[:, :, 1 - core, :, :, lanes(c)], twin_buf, twin)
        load = pltpu.make_async_copy(g.at[:, :, core, :, :, lanes(c)], acc, local.at[c])
        load.start()
        loads.append(load)

    def add(target, source):
        target[...] = target[...] + source[...]

    def stage(c, step):
        acc, twin_buf, p1, m1, p2, m2, q1, r1, q2, r2 = groups[c][:10]
        kept = first[c]
        y_first = c % 2 == 0
        if step == 0:
            loads[c].wait()
            kept[0].wait_recv()

            def body(i, carry):
                a, b, d = i // 8, (i // 4) % 2, i % 4
                add(acc.at[a, b, d], twin_buf.at[a, b, d])
                return carry

            lax.fori_loop(0, 32, body, 0)
            if y_first:
                kept[1] = go(c, 1, acc.at[:, 0, yo], p1, y_next)
                kept[2] = go(c, 2, acc.at[:, 1, yo], m1, y_prev)
            else:
                kept[1] = go(c, 1, acc.at[zo, 0], p1, z_next)
                kept[2] = go(c, 2, acc.at[zo, 1], m1, z_prev)
        elif step == 1:
            kept[1].wait_recv()
            kept[2].wait_recv()

            def body(i, carry):
                if y_first:
                    add(acc.at[i, 0, yn], p1.at[i])
                    add(acc.at[i, 1, yp], m1.at[i])
                else:
                    add(acc.at[zn, 0, i], p1.at[i])
                    add(acc.at[zp, 1, i], m1.at[i])
                return carry

            lax.fori_loop(0, 4, body, 0)
            if y_first:
                kept[3] = go(c, 3, acc.at[:, :, yn], p2, y_next)
                kept[4] = go(c, 4, acc.at[:, :, yp], m2, y_prev)
            else:
                kept[3] = go(c, 3, acc.at[zn], p2, z_next)
                kept[4] = go(c, 4, acc.at[zp], m2, z_prev)
        elif step == 2:
            kept[3].wait_recv()
            kept[4].wait_recv()

            def body(i, carry):
                if y_first:
                    a, b = i // 2, i % 2
                    add(acc.at[a, b, y], p2.at[a, b])
                    add(acc.at[a, b, y], m2.at[a, b])
                else:
                    a, b = i // 4, i % 4
                    add(acc.at[z, a, b], p2.at[a, b])
                    add(acc.at[z, a, b], m2.at[a, b])
                return carry

            lax.fori_loop(0, 8, body, 0)
            if y_first:
                kept[5] = go(c, 5, acc.at[zo, 0, y], q1, z_next)
                kept[6] = go(c, 6, acc.at[zo, 1, y], r1, z_prev)
            else:
                kept[5] = go(c, 5, acc.at[z, 0, yo], q1, y_next)
                kept[6] = go(c, 6, acc.at[z, 1, yo], r1, y_prev)
        elif step == 3:
            kept[5].wait_recv()
            kept[6].wait_recv()
            if y_first:
                add(acc.at[zn, 0, y], q1)
                add(acc.at[zp, 1, y], r1)
                kept[7] = go(c, 7, acc.at[zn, :, y], q2, z_next)
                kept[8] = go(c, 8, acc.at[zp, :, y], r2, z_prev)
            else:
                add(acc.at[z, 0, yn], q1)
                add(acc.at[z, 1, yp], r1)
                kept[7] = go(c, 7, acc.at[z, :, yn], q2, y_next)
                kept[8] = go(c, 8, acc.at[z, :, yp], r2, y_prev)
        elif step == 4:
            kept[7].wait_recv()
            kept[8].wait_recv()
            for b in range(2):
                add(acc.at[z, b, y], q2.at[b])
                add(acc.at[z, b, y], r2.at[b])
            kept[9] = go(c, 9, acc.at[z, 1 - x_hi, y], gathered.at[4, :, lanes(c)], across)
        elif step == 5:
            kept[9].wait_recv()
            acc[z, x_hi, y] = acc[z, x_hi, y] + gathered[4, :, lanes(c)]
            kept[10] = go(c, 10, acc.at[z, x_hi, y], gathered.at[5, :, lanes(c)], beside)
        elif step == 6:
            kept[10].wait_recv()
            gathered[y, :, lanes(c)] = acc[z, x_hi, y] + gathered[5, :, lanes(c)]
            mine = gathered.at[y, :, lanes(c)]
            kept[11] = go(c, 11, mine, mine, y_next)
            kept[12] = go(c, 12, mine, mine, y_prev)
            kept[13] = go(c, 13, mine, mine, y_far)
        else:
            for slot in (11, 12, 13):
                kept[slot].wait_recv()

    for step in range(8):
        for c in range(n):
            stage(c, step)
    for i in range(4):
        out[i] = gathered[i].astype(F32)
    for item in started:
        item.wait_send()


def reduce_all(g):
    cols = g.shape[1]
    scratch = []
    for c, w in enumerate(WIDTHS):
        scratch += [pltpu.VMEM((4, 2, 4, 16, w), BF)] * 2 + [pltpu.VMEM((4, 16, w), BF)] * 2
        scratch += [pltpu.VMEM((4, 2, 16, w) if c % 2 == 0 else (2, 4, 16, w), BF)] * 2
        scratch += [pltpu.VMEM((16, w), BF)] * 2 + [pltpu.VMEM((2, 16, w), BF)] * 2
    n = len(WIDTHS)
    scratch += [
        pltpu.VMEM((6, 16, cols), BF), pltpu.SemaphoreType.DMA((n, 14)), pltpu.SemaphoreType.DMA((n, 14)),
        pltpu.SemaphoreType.DMA((n,)),
    ]
    out = pl.pallas_call(
        reduce_kernel,
        out_shape=jax.ShapeDtypeStruct((4, 16, cols), F32),
        in_specs=[pl.BlockSpec(memory_space=pl.ANY)],
        out_specs=pl.BlockSpec(memory_space=pltpu.VMEM),
        scratch_shapes=scratch,
        compiler_params=pltpu.CompilerParams(
            collective_id=1, has_side_effects=True, vmem_limit_bytes=48 << 20
        ),
        cost_estimate=pl.CostEstimate(flops=10**8, bytes_accessed=10**8, transcendentals=0),
    )(g.reshape(4, 2, 2, 4, 16, cols))
    return out.reshape(64, cols)


def gather_kernel(own, out, send, recv, local):
    n = len(WIDTHS)
    y, x_lo, z, x_hi, core = places()
    yn, yp, yo = (y + 1) % 4, (y + 3) % 4, (y + 2) % 4
    zn, zp, zo = (z + 1) % 4, (z + 3) % 4, (z + 2) % 4
    y_next, y_prev = at_place(yn, x_lo, z, x_hi, core), at_place(yp, x_lo, z, x_hi, core)
    z_next, z_prev = at_place(y, x_lo, zn, x_hi, core), at_place(y, x_lo, zp, x_hi, core)
    across = at_place(y, 1 - x_lo, z, 1 - x_hi, core)
    twin = at_place(y, x_lo, z, x_hi, 1 - core)
    greet((y_next, y_prev, z_next, z_prev, across, twin))
    started = []

    def lanes(c):
        return pl.ds(sum(WIDTHS[:c]), WIDTHS[c])

    def go(c, slot, source, target, device):
        item = pltpu.make_async_remote_copy(
            src_ref=source, dst_ref=target, send_sem=send.at[c, slot], recv_sem=recv.at[c, slot],
            device_id=device, device_id_type=pl.DeviceIdType.MESH,
        )
        item.start()
        started.append(item)
        return item

    held = [[None] * 10 for _ in range(n)]
    loads = []

    def stage(c, step):
        kept = held[c]
        cols = lanes(c)
        split = c % 2 == 0
        rows = pl.ds(y, 1) if split else pl.ds(0, 4)

        def part(a, b, d):
            return out.at[a, b, core, d, :, cols]

        def pass_on(slot, source, device):
            kept[slot] = go(c, slot, source, source, device)

        if step == 0:
            kept[0] = go(c, 0, own.at[rows, :, cols], part(z, x_hi, rows), across)
            load = pltpu.make_async_copy(own.at[rows, :, cols], part(z, x_hi, rows), local.at[c])
            load.start()
            loads.append(load)
        elif step == 1:
            loads[c].wait()
            kept[0].wait_recv()
            pass_on(1, part(z, slice(None), rows), z_next)
            pass_on(2, part(z, slice(None), rows), z_prev)
        elif step == 2:
            kept[1].wait_recv()
            kept[2].wait_recv()
            pass_on(3, part(zp, 0, rows), z_next)
            pass_on(4, part(zn, 1, rows), z_prev)
        elif step == 3:
            kept[3].wait_recv()
            kept[4].wait_recv()
            if split:
                pass_on(5, part(slice(None), slice(None), rows), y_next)
                pass_on(6, part(slice(None), slice(None), rows), y_prev)
            else:
                pass_on(9, part(slice(None), slice(None), rows), twin)
        elif step == 4 and split:
            kept[5].wait_recv()
            kept[6].wait_recv()
            pass_on(7, part(slice(None), 0, pl.ds(yp, 1)), y_next)
            pass_on(8, part(slice(None), 1, pl.ds(yn, 1)), y_prev)
        elif step == 5 and split:
            kept[7].wait_recv()
            kept[8].wait_recv()
            pass_on(9, part(slice(None), slice(None), slice(None)), twin)
        elif step == 6:
            kept[9].wait_recv()

    for step in range(7):
        for c in range(n):
            stage(c, step)
    for item in started:
        item.wait_send()


def gather_all(own):
    cols = own.shape[1]
    n = len(WIDTHS)
    out = pl.pallas_call(
        gather_kernel,
        out_shape=jax.ShapeDtypeStruct((4, 2, 2, 4, 16, cols), BF),
        in_specs=[pl.BlockSpec(memory_space=pl.ANY)],
        out_specs=pl.BlockSpec(memory_space=pl.ANY),
        scratch_shapes=[
            pltpu.SemaphoreType.DMA((n, 10)), pltpu.SemaphoreType.DMA((n, 10)), pltpu.SemaphoreType.DMA((n,))
        ],
        compiler_params=pltpu.CompilerParams(collective_id=2, has_side_effects=True),
        cost_estimate=pl.CostEstimate(flops=10**8, bytes_accessed=10**8, transcendentals=0),
    )(own.reshape(4, 16, cols))
    return out.reshape(1024, cols)


def rope_parts(length, start):
    half = AP // 2
    inverse = THETA ** (-2.0 * jnp.arange(half).astype(F32) / AP)
    angles = (start + jnp.arange(length)).astype(F32)[:, None] * inverse[None, :]
    cosine = jnp.cos(angles)
    sine = jnp.sin(angles)
    return jnp.concatenate([cosine, cosine], axis=1), jnp.concatenate([-sine, sine], axis=1)


def swap_halves(value):
    rows, cols = value.shape
    parts = value.reshape(rows, cols // AP, 2, AP // 2)
    return parts[:, :, ::-1, :].reshape(rows, cols)


def pad_lanes(value):
    return jnp.pad(value.astype(F32), (0, 128 - value.shape[0]))[None, :]


def exchange(value):
    return lax.all_to_all(value, "seq", split_axis=0, concat_axis=0, tiled=True)


def share(value, seqs):
    return exchange(jnp.broadcast_to(value[None], (seqs,) + value.shape))


def sum_over(value, seqs):
    rows, cols = value.shape
    parts = exchange(value.reshape(seqs, rows // seqs, cols))
    return share(jnp.sum(parts.astype(F32), axis=0).astype(BF), seqs).reshape(rows, cols)


def state_scan(packed, seqs):
    states = packed[:, :, :AP, :].astype(F32)
    logs = packed[:, :, AP, 0].astype(F32) + packed[:, :, AP + 1, 0].astype(F32)
    return states, jnp.exp(logs)


def per_device(
    seqs, hidden_in, norm_gain, mixer_proj, attn_proj, conv_kernel, conv_bias, step_bias, decay_log,
    skip_gain, gated_gain, mixer_out, attn_out, ffn_gain, gate_up, down_proj, out_grad,
):
    T = hidden_in.shape[1]
    width = norm_gain.shape[0]
    shards = 1024 // width
    me = lax.axis_index("seq")
    mix_rows, att_rows, down_rows = mixer_out.shape[0], attn_out.shape[0], down_proj.shape[0]

    small = jnp.concatenate(
        [norm_gain, ffn_gain, gated_gain, conv_bias, conv_kernel.T.reshape(-1)]
    )
    slots = width * 104
    small = jnp.pad(small, (0, slots - small.shape[0])).reshape(width, 104)
    front_shard = jnp.concatenate(
        [mixer_proj[:, : D_SSM + XBC], attn_proj, mixer_proj[:, D_SSM + XBC :], small], axis=1
    )
    front = gather_all(front_shard)
    tail_shard = jnp.concatenate(
        [
            gate_up[:, :FF],
            gate_up[:, FF:],
            jnp.concatenate([jnp.concatenate([mixer_out, attn_out], axis=0), down_proj], axis=1),
        ],
        axis=0,
    )
    tail = lax.all_gather(tail_shard, "fsdp", axis=0, tiled=False)
    smalls = front.reshape(shards, width, FRONT)[:, :, 4120:].reshape(shards, slots)
    cuts = []
    at = 0
    for size in (width, width, gated_gain.shape[0], conv_bias.shape[0]):
        cuts.append(smalls[:, at : at + size].reshape(1, -1).astype(F32))
        at += size
    gain_one, gain_ffn, gain_gated, bias_all = cuts
    kernel_size = conv_kernel.shape[0]
    taps = smalls[:, at : at + 4 * kernel_size].reshape(shards, 4, kernel_size)
    taps = taps.transpose(1, 0, 2).reshape(4, XBC).astype(F32)
    taps = jnp.pad(taps, ((0, 4), (0, 0)))

    resid = hidden_in[0].astype(F32)
    scale_one = rms_scale(resid)
    normed_one = resid * scale_one
    normed_in = (normed_one * gain_one).astype(BF)
    projection = dot(normed_in, front)
    gate_pre = projection[:, :D_SSM]
    xbc = projection[:, D_SSM : D_SSM + XBC].astype(BF)
    queries = projection[:, 3328:3840].astype(BF)
    keyvals = projection[:, 3840:4096].astype(BF)
    steps = projection[:, 4096:].astype(BF)
    cosine, sine = rope_parts(T, me * T)
    cos_q, sin_q = jnp.tile(cosine, (1, QH)), jnp.tile(sine, (1, QH))
    cos_k, sin_k = jnp.tile(cosine, (1, KVH)), jnp.tile(sine, (1, KVH))
    query_rot = queries.astype(F32)
    query_rot = (query_rot * cos_q + swap_halves(query_rot) * sin_q).astype(BF)
    keys = keyvals[:, : KVH * AP].astype(F32)
    key_rot = (keys * cos_k + swap_halves(keys) * sin_k).astype(BF)
    kv_own = jnp.concatenate([key_rot, keyvals[:, KVH * AP :]], axis=1)
    halo = lax.ppermute(xbc[-8:], "seq", [(i, i + 1) for i in range(seqs - 1)])
    kv_all = share(kv_own, seqs).reshape(seqs * T, 2 * KVH * AP)
    sbias, dlog, skip = pad_lanes(step_bias), pad_lanes(decay_log), pad_lanes(skip_gain)
    act, dt, cum, fresh = call(
        mamba_first,
        [((T, XBC), F32), ((T, 128), F32), ((T, 128), F32), ((D_SSM, NST), BF)],
        xbc, halo, steps, taps, bias_all, sbias, dlog,
        scratch=[pltpu.VMEM((T + 8, XBC), F32)],
    )
    heads = MH // seqs
    ends = cum[T - 1, :MH]
    high = ends.astype(BF)
    low = (ends - high.astype(F32)).astype(BF)
    extra = jnp.concatenate([high[:, None, None], low[:, None, None]], axis=1)
    extra = jnp.broadcast_to(jnp.pad(extra, ((0, 0), (0, 14), (0, 0))), (MH, 16, NST))
    packed = jnp.concatenate([fresh.reshape(MH, AP, NST), extra], axis=1)
    packed = lax.all_to_all(
        packed.reshape(seqs, heads, AP + 16, NST), "seq", split_axis=0, concat_axis=0, tiled=True
    )
    states, totals = state_scan(packed, seqs)
    running = jnp.zeros_like(states[0])
    starts = []
    for c in range(seqs):
        starts.append(running.astype(BF))
        running = running * totals[c][:, None, None] + states[c]
    starts = lax.all_to_all(
        jnp.stack(starts), "seq", split_axis=0, concat_axis=0, tiled=True
    ).reshape(D_SSM, NST)
    attn_tok, lse = call(
        functools.partial(attend_forward, "seq"),
        [((T, QH * AP), BF), ((QH, T), F32)],
        query_rot, kv_all,
        scratch=[pltpu.VMEM((QH * AP, T), F32), pltpu.VMEM((QH, T), F32), pltpu.VMEM((QH, T), F32)],
    )
    (mixed_y,) = call(mamba_second, [((T, D_SSM), BF)], act, dt, cum, starts, skip)

    proj_gate = tail[:, :width].reshape(-1, FF)
    proj_up = tail[:, width : 2 * width].reshape(-1, FF)
    low_rows = 2 * width
    out_mixer = tail[:, low_rows : low_rows + mix_rows, :1024].reshape(-1, 1024)
    out_attn = tail[:, low_rows + mix_rows :, :1024].reshape(-1, 1024)
    proj_down = tail[:, low_rows:, 1024:].reshape(-1, 1024)
    mixed = mixed_y.astype(F32)
    gated = mixed * jax.nn.silu(gate_pre)
    scale_two = rms_scale(gated)
    normed_two = gated * scale_two
    normed_mix = (normed_two * gain_gated).astype(BF)
    middle = resid + dot(normed_mix, out_mixer) + dot(attn_tok, out_attn)
    scale_three = rms_scale(middle)
    normed_three = middle * scale_three
    normed_ffn = (normed_three * gain_ffn).astype(BF)
    gate_half = dot(normed_ffn, proj_gate)
    up_half = dot(normed_ffn, proj_up)
    activ = (jax.nn.silu(gate_half) * up_half).astype(BF)
    block_out = (middle + dot(activ, proj_down)).astype(BF)

    ograd = out_grad[0]
    grad_activ = dot(ograd, proj_down, NT)
    grad_down = dot(activ, ograd, TN).astype(BF)
    grad_g = (grad_activ * up_half * silu_slope(gate_half)).astype(BF)
    grad_u = (grad_activ * jax.nn.silu(gate_half)).astype(BF)
    grad_gw = dot(normed_ffn, grad_g, TN).astype(BF)
    grad_uw = dot(normed_ffn, grad_u, TN).astype(BF)
    grad_nffn = dot(grad_g, proj_gate, NT) + dot(grad_u, proj_up, NT)
    grad_ffn = jnp.sum(grad_nffn * normed_three, axis=0)
    grad_middle = ograd.astype(F32) + rms_back(grad_nffn * gain_ffn, normed_three, scale_three)
    middle_bf = grad_middle.astype(BF)
    grad_mixed = dot(normed_mix, middle_bf, TN).astype(BF)
    grad_attended = dot(attn_tok, middle_bf, TN).astype(BF)
    grad_nmix = dot(middle_bf, out_mixer, NT)
    grad_otok = dot(middle_bf, out_attn, NT).astype(BF)
    grad_gated = jnp.sum(grad_nmix * normed_two, axis=0)
    grad_gz = rms_back(grad_nmix * gain_gated, normed_two, scale_two)
    grad_ymix = (grad_gz * jax.nn.silu(gate_pre)).astype(BF)
    grad_gate = (grad_gz * mixed * silu_slope(gate_pre)).astype(BF)
    tail_grad = jnp.concatenate(
        [
            grad_gw.reshape(shards, width, FF),
            grad_uw.reshape(shards, width, FF),
            jnp.concatenate(
                [
                    jnp.concatenate(
                        [
                            grad_mixed.reshape(shards, mix_rows, 1024),
                            grad_attended.reshape(shards, att_rows, 1024),
                        ],
                        axis=1,
                    ),
                    grad_down.reshape(shards, down_rows, 1024),
                ],
                axis=2,
            ),
        ],
        axis=1,
    )
    tail_piece = lax.psum_scatter(tail_grad, "fsdp", scatter_dimension=0, tiled=True)[0]

    (dstart,) = call(mamba_back_first, [((D_SSM, NST), BF)], grad_ymix, act, cum)
    dstarts = lax.all_to_all(
        dstart.reshape(seqs, heads, AP, NST), "seq", split_axis=0, concat_axis=0, tiled=True
    ).astype(F32)
    running = jnp.zeros_like(dstarts[0])
    dends = [None] * seqs
    for c in reversed(range(seqs)):
        dends[c] = running.astype(BF)
        running = running * totals[c][:, None, None] + dstarts[c]
    dends = lax.all_to_all(
        jnp.stack(dends), "seq", split_axis=0, concat_axis=0, tiled=True
    ).reshape(D_SSM, NST)
    dq, dkv = call(
        functools.partial(attend_backward, "seq"),
        [((T, QH * AP), F32), ((kv_all.shape[0], 2 * KVH * AP), BF)],
        query_rot, kv_all, attn_tok, lse, grad_otok,
    )
    dkv = exchange(dkv.reshape(seqs, T, 2 * KVH * AP))
    dkv = jnp.sum(dkv.astype(F32), axis=0).astype(BF)
    qgrad = (dq * cos_q - swap_halves(dq) * sin_q).astype(BF)
    dk = dkv[:, : KVH * AP].astype(F32)
    kgrad = (dk * cos_k - swap_halves(dk) * sin_k).astype(BF)
    dconv, dtaps, dbias, dsteps, dhead = call(
        mamba_back_second,
        [((T, XBC), F32), ((8, XBC), F32), ((8, XBC), F32), ((T, 128), BF), ((8, 128), F32)],
        grad_ymix, xbc, halo, act, dt, cum, starts, dends, steps, taps, bias_all, sbias, dlog, skip,
        scratch=[pltpu.VMEM((T + 8, XBC), F32), pltpu.VMEM((T, XBC), F32)],
    )
    ahead = lax.ppermute(dconv[:8].astype(BF), "seq", [(i + 1, i) for i in range(seqs - 1)])
    later = jnp.concatenate([dconv, ahead.astype(F32)], axis=0)
    du = taps[3:4] * dconv
    for lag in range(3):
        du = du + taps[lag : lag + 1] * later[3 - lag : 3 - lag + T]
    grad_proj = jnp.concatenate(
        [grad_gate, du.astype(BF), qgrad, kgrad, dkv[:, KVH * AP :], dsteps], axis=1
    )

    grad_front = dot(normed_in, grad_proj, TN).astype(BF)
    grad_nin = dot(grad_proj, front, NT)
    grad_norm = jnp.sum(grad_nin * normed_one, axis=0)
    input_grad = grad_middle + rms_back(grad_nin * gain_one, normed_one, scale_one)
    vectors = [grad_norm, grad_ffn, grad_gated, dbias[0]] + [dtaps[lag] for lag in range(4)]
    vectors = [value.reshape(shards, -1) for value in vectors]
    vectors.append(jnp.broadcast_to(dhead[:3, :MH].reshape(1, 3 * MH), (shards, 3 * MH)))
    vectors = jnp.concatenate(vectors, axis=1)
    vectors = jnp.pad(vectors, ((0, 0), (0, slots - vectors.shape[1]))).astype(BF)
    last = jnp.concatenate([grad_front[:, 4096:4120], vectors.reshape(-1, 104)], axis=1)
    front_sum = reduce_all(lax.dynamic_update_slice(grad_front, last, (0, 4096)))
    front_sum, tail_piece = lax.optimization_barrier((front_sum, tail_piece))
    tail_sum = sum_over(tail_piece, seqs)
    vectors = front_sum[:, 4120:].reshape(-1)
    owned = []
    at = 0
    for size in [width, width, gated_gain.shape[0], kernel_size] + [kernel_size] * 4 + [MH] * 3:
        owned.append(vectors[at : at + size])
        at += size
    own_taps = jnp.stack(owned[4:8], axis=1)
    tail_sum = tail_sum.astype(F32)
    return (
        block_out[None],
        input_grad[None],
        owned[0],
        jnp.concatenate([front_sum[:, : D_SSM + XBC], front_sum[:, 4096:4120]], axis=1),
        front_sum[:, 3328:4096],
        own_taps,
        owned[3],
        owned[8],
        owned[9],
        owned[10],
        owned[2],
        tail_sum[low_rows : low_rows + mix_rows, :1024],
        tail_sum[low_rows + mix_rows :, :1024],
        owned[1],
        jnp.concatenate([tail_sum[:width], tail_sum[width : 2 * width]], axis=1),
        tail_sum[low_rows:, 1024:],
    )


def solution(mesh):
    tokens = P("fsdp", "seq", None)
    vector = P("fsdp")
    matrix = P("fsdp", None)
    in_specs = (
        tokens, vector, matrix, matrix, matrix, vector, P(), P(), P(), vector, matrix, matrix, vector,
        matrix, matrix, tokens,
    )
    out_specs = (
        tokens, tokens, vector, matrix, matrix, matrix, vector, P(), P(), P(), vector, matrix, matrix,
        vector, matrix, matrix,
    )
    return jax.shard_map(
        functools.partial(per_device, mesh.shape["seq"]),
        mesh=mesh, in_specs=in_specs, out_specs=out_specs, check_vma=False,
    )
```

```python
import functools
import math

import jax
import jax.numpy as jnp
from jax import lax
from jax.experimental import pallas as pl
from jax.experimental.pallas import tpu as pltpu
from jax.sharding import PartitionSpec as P

MH = 24
NST = 128
QH = 8
KVH = 2
AP = 64
FF = 2048
D_SSM = 1536
XBC = 1792
CIN = 3352
FRONT = 4224
EPSILON = 1e-05
THETA = 10000.0
HIGHEST = lax.Precision.HIGHEST
F32 = jnp.float32
BF = jnp.bfloat16
NT = (((1,), (1,)), ((), ()))
TN = (((0,), (0,)), ((), ()))


def dot(a, b, dims=(((1,), (0,)), ((), ())), precision=None):
    return lax.dot_general(a, b, dims, preferred_element_type=F32, precision=precision)


def silu_slope(value):
    sigma = jax.nn.sigmoid(value)
    return sigma * (1.0 + value * (1.0 - sigma))


def rms_scale(value):
    return lax.rsqrt(jnp.mean(value * value, axis=1, keepdims=True) + EPSILON)


def rms_back(grad_normed, normed, scale):
    return scale * (grad_normed - normed * jnp.mean(grad_normed * normed, axis=1, keepdims=True))


def head_selector(rows, cols):
    channel = lax.broadcasted_iota(jnp.int32, (rows, cols), 0)
    head = lax.broadcasted_iota(jnp.int32, (rows, cols), 1)
    return jnp.where((channel >= head * AP) & (channel < head * AP + AP), 1.0, 0.0).astype(F32)


def spread_heads(value):
    head = lax.broadcasted_iota(jnp.int32, (128, D_SSM), 0)
    channel = lax.broadcasted_iota(jnp.int32, (128, D_SSM), 1)
    select = jnp.where((channel >= head * AP) & (channel < head * AP + AP), 1.0, 0.0).astype(F32)
    return dot(value, select, precision=HIGHEST)


def gather_heads(value):
    return dot(value, head_selector(D_SSM, 128), precision=HIGHEST)


def conv_pre(ext, taps, bias, length):
    result = bias[...] + taps[3:4, :] * ext[8 : 8 + length, :]
    for lag in range(3):
        result = result + taps[lag : lag + 1, :] * ext[pl.ds(5 + lag, length), :]
    return result


def mamba_first(xbc, halo, steps, taps, bias, sbias, dlog, act_ref, dt_ref, cum_ref, fresh_ref, ext):
    length = xbc.shape[0]
    ext[0:8, :] = halo[...].astype(F32)
    ext[8 : 8 + length, :] = xbc[...].astype(F32)
    conv = conv_pre(ext, taps, bias, length)
    act = conv * jax.nn.sigmoid(conv)
    act_ref[...] = act
    lane = lax.broadcasted_iota(jnp.int32, (length, 128), 1)
    raw = steps[...].astype(F32) + sbias[...]
    dt = jnp.maximum(raw, 0.0) + jnp.log1p(jnp.exp(-jnp.abs(raw)))
    dt = jnp.where(lane < MH, dt, 0.0)
    dt_ref[...] = dt
    row = lax.broadcasted_iota(jnp.int32, (length, length), 0)
    col = lax.broadcasted_iota(jnp.int32, (length, length), 1)
    lower = jnp.where(row >= col, 1.0, 0.0).astype(F32)
    cum = dot(lower, dt * (-jnp.exp(dlog[...])), precision=HIGHEST)
    cum_ref[...] = cum
    weight = spread_heads(jnp.exp(cum[length - 1 : length, :] - cum) * dt)
    scaled = (act[:, :D_SSM] * weight).astype(BF)
    fresh_ref[...] = dot(scaled, act[:, D_SSM : D_SSM + NST].astype(BF), TN).astype(BF)


def mamba_second(act, dt, cum, starts, skip, y_ref):
    length = act.shape[0]
    cumv = cum[...]
    cum_t = cumv.T
    bmat = act[:, D_SSM : D_SSM + NST].astype(BF)
    cmat = act[:, D_SSM + NST :].astype(BF)
    inner = dot(cmat, bmat, NT)
    row = lax.broadcasted_iota(jnp.int32, (length, length), 0)
    col = lax.broadcasted_iota(jnp.int32, (length, length), 1)
    inner = jnp.where(row >= col, inner, 0.0)
    x = act[:, :D_SSM]
    scaled = (x * spread_heads(dt[...])).astype(BF)
    outer = dot(cmat, starts[...], NT) * spread_heads(jnp.exp(cumv))
    base = outer + spread_heads(skip[...]) * x
    for pair in range(MH // 2):
        parts = []
        for h in (2 * pair, 2 * pair + 1):
            fade = jnp.exp(jnp.minimum(cumv[:, h : h + 1] - cum_t[h : h + 1, :], 0.0))
            parts.append(dot((inner * fade).astype(BF), scaled[:, h * AP : h * AP + AP]))
        lanes = slice(pair * 128, pair * 128 + 128)
        y_ref[:, lanes] = (base[:, lanes] + jnp.concatenate(parts, axis=1)).astype(BF)


def mamba_back_first(gy, act, cum, dstart_ref):
    rise = spread_heads(jnp.exp(cum[...]))
    cmat = act[:, D_SSM + NST :].astype(BF)
    dstart_ref[...] = dot((gy[...].astype(F32) * rise).astype(BF), cmat, TN).astype(BF)


def mamba_back_second(
    gy, xbc, halo, act, dt, cum, starts, dends, steps, taps, bias, sbias, dlog, skip,
    dconv_ref, dtaps_ref, dbias_ref, dsteps_ref, dhead_ref, ext, dact,
):
    length = act.shape[0]
    cumv = cum[...]
    dtv = dt[...]
    cum_t = cumv.T
    lane = lax.broadcasted_iota(jnp.int32, (length, 128), 1)
    bmat = act[:, D_SSM : D_SSM + NST].astype(BF)
    cmat = act[:, D_SSM + NST :].astype(BF)
    row = lax.broadcasted_iota(jnp.int32, (length, length), 0)
    col = lax.broadcasted_iota(jnp.int32, (length, length), 1)
    inner_t = jnp.where(col >= row, dot(bmat, cmat, NT), 0.0)
    x = act[:, :D_SSM]
    gyb = gy[...]
    gyf = gyb.astype(F32)
    dt_full = spread_heads(dtv)
    tail = spread_heads(jnp.exp(cumv[length - 1 : length, :] - cumv))
    rise = spread_heads(jnp.exp(cumv))
    xs = x * dt_full
    xsb = xs.astype(BF)
    ginner = jnp.zeros((length, length), F32)
    qcols = jnp.zeros((length, 128), F32)
    rrows = []
    for pair in range(MH // 2):
        parts = []
        for h in (2 * pair, 2 * pair + 1):
            lanes = slice(h * AP, h * AP + AP)
            fade = jnp.exp(jnp.minimum(cum_t[h : h + 1, :] - cumv[:, h : h + 1], 0.0))
            graded = dot(xsb[:, lanes], gyb[:, lanes], NT) * fade
            ginner = ginner + graded
            weighed = graded * inner_t
            rrows.append(jnp.sum(weighed, axis=0, keepdims=True))
            qcols = jnp.where(lane == h, jnp.sum(weighed, axis=1, keepdims=True), qcols)
            parts.append(dot((inner_t * fade).astype(BF), gyb[:, lanes]))
        dact[:, pair * 128 : pair * 128 + 128] = jnp.concatenate(parts, axis=1)
    ginner = jnp.where(col >= row, ginner, 0.0).astype(BF)
    rrows = jnp.concatenate(rrows + [jnp.zeros((128 - MH, length), F32)], axis=0).T
    endb = dends[...]
    startb = starts[...]
    from_end = dot(bmat, endb, NT) * tail
    dxs = dact[:, :D_SSM] + from_end
    reach = gather_heads(xs * from_end)
    outer = dot(cmat, startb, NT) * rise
    dcum = rrows - qcols + gather_heads(gyf * outer) - reach
    total = jnp.exp(cumv[length - 1 : length, :])
    carried = gather_heads_rows(startb, endb) * total + jnp.sum(reach, axis=0, keepdims=True)
    last = lax.broadcasted_iota(jnp.int32, (length, 128), 0) == length - 1
    dcum = dcum + jnp.where(last, carried, 0.0)
    upper = jnp.where(col >= row, 1.0, 0.0).astype(F32)
    rest = dot(upper, dcum, precision=HIGHEST)
    decay = -jnp.exp(dlog[...])
    ddt = gather_heads(x * dxs) + decay * rest
    ddecay = jnp.sum(dtv * rest, axis=0, keepdims=True) * decay
    raw = steps[...].astype(F32) + sbias[...]
    dsteps = jnp.where(lane < MH, ddt * jax.nn.sigmoid(raw), 0.0)
    dsteps_ref[...] = dsteps.astype(BF)
    dskip = gather_heads(jnp.sum(x * gyf, axis=0, keepdims=True))
    dhead_ref[0:1, :] = jnp.sum(dsteps, axis=0, keepdims=True)
    dhead_ref[1:2, :] = ddecay
    dhead_ref[2:3, :] = dskip
    dhead_ref[3:8, :] = jnp.zeros((5, 128), F32)
    dact[:, :D_SSM] = dt_full * dxs + spread_heads(skip[...]) * gyf
    dact[:, D_SSM : D_SSM + NST] = dot((xs * tail).astype(BF), endb) + dot(ginner, cmat)
    dact[:, D_SSM + NST :] = dot((gyf * rise).astype(BF), startb) + dot(ginner, bmat, TN)
    ext[0:8, :] = halo[...].astype(F32)
    ext[8 : 8 + length, :] = xbc[...].astype(F32)
    conv = conv_pre(ext, taps, bias, length)
    dconv = dact[...] * silu_slope(conv)
    dconv_ref[...] = dconv
    dbias_ref[...] = jnp.broadcast_to(jnp.sum(dconv, axis=0, keepdims=True), (8, XBC))
    for lag in range(4):
        dtaps_ref[lag : lag + 1, :] = jnp.sum(
            dconv * ext[pl.ds(5 + lag, length), :], axis=0, keepdims=True
        )
    dtaps_ref[4:8, :] = jnp.zeros((4, XBC), F32)


def gather_heads_rows(a, b):
    product = a.astype(F32) * b.astype(F32)
    per_row = dot(jnp.ones((8, NST), F32), product, NT, precision=HIGHEST)
    return gather_heads(per_row)[0:1, :]


def attend_forward(axis, q, kv, o_ref, lse_ref, acc, top, total):
    me = lax.axis_index(axis)
    block = q.shape[0]
    scale = 1.0 / math.sqrt(AP)
    acc[...] = jnp.zeros_like(acc)
    top[...] = jnp.full(top.shape, -jnp.inf, F32)
    total[...] = jnp.zeros_like(total)
    key_at = lax.broadcasted_iota(jnp.int32, (block, block), 0)
    query_at = lax.broadcasted_iota(jnp.int32, (block, block), 1)

    def step(j, carry):
        rows = pl.ds(pl.multiple_of(j * block, block), block)
        allowed = (key_at + j * block) <= (query_at + me * block)
        for h in range(QH):
            g = h // (QH // KVH)
            keys = kv[rows, g * AP : g * AP + AP]
            values = kv[rows, KVH * AP + g * AP : KVH * AP + g * AP + AP]
            s = dot(keys, q[:, h * AP : h * AP + AP], NT) * scale
            s = jnp.where(allowed, s, -1e30)
            old = top[h : h + 1, :]
            new = jnp.maximum(old, jnp.max(s, axis=0, keepdims=True))
            p = jnp.exp(s - new)
            fix = jnp.exp(old - new)
            top[h : h + 1, :] = new
            total[h : h + 1, :] = total[h : h + 1, :] * fix + jnp.sum(p, axis=0, keepdims=True)
            band = slice(h * AP, h * AP + AP)
            acc[band, :] = acc[band, :] * fix + dot(values, p.astype(BF), TN)
        return carry

    lax.fori_loop(0, me + 1, step, 0)
    lse_ref[...] = top[...] + jnp.log(total[...])
    for pair in range(QH // 2):
        parts = []
        for h in (2 * pair, 2 * pair + 1):
            parts.append(acc[h * AP : h * AP + AP, :] / total[h : h + 1, :])
        o_ref[:, pair * 128 : pair * 128 + 128] = jnp.concatenate(parts, axis=0).T.astype(BF)


def attend_backward(axis, q, kv, o, lse, go, dq_ref, dkv_ref):
    me = lax.axis_index(axis)
    block = q.shape[0]
    scale = 1.0 / math.sqrt(AP)
    dq_ref[...] = jnp.zeros_like(dq_ref)
    dkv_ref[...] = jnp.zeros_like(dkv_ref)
    key_at = lax.broadcasted_iota(jnp.int32, (block, block), 0)
    query_at = lax.broadcasted_iota(jnp.int32, (block, block), 1)
    centred = go[...].astype(F32) * o[...].astype(F32)
    pick_h = lax.broadcasted_iota(jnp.int32, (8, QH * AP), 0)
    pick_c = lax.broadcasted_iota(jnp.int32, (8, QH * AP), 1)
    pick = jnp.where((pick_c >= pick_h * AP) & (pick_c < pick_h * AP + AP), 1.0, 0.0).astype(F32)
    centre = dot(pick, centred, NT, precision=HIGHEST)

    def step(j, carry):
        rows = pl.ds(pl.multiple_of(j * block, block), block)
        allowed = (key_at + j * block) <= (query_at + me * block)
        sums = []
        for g in range(KVH):
            keys = kv[rows, g * AP : g * AP + AP]
            values = kv[rows, KVH * AP + g * AP : KVH * AP + g * AP + AP]
            dk = jnp.zeros((block, AP), F32)
            dv = jnp.zeros((block, AP), F32)
            for h in range(g * (QH // KVH), (g + 1) * (QH // KVH)):
                band = slice(h * AP, h * AP + AP)
                qh = q[:, band]
                gh = go[:, band]
                s = dot(keys, qh, NT) * scale
                p = jnp.exp(jnp.where(allowed, s - lse[h : h + 1, :], -1e30))
                dv = dv + dot(p.astype(BF), gh)
                dp = dot(values, gh, NT)
                ds = (p * (dp - centre[h : h + 1, :])).astype(BF)
                dk = dk + dot(ds, qh)
                dq_ref[:, band] += dot(ds, keys, TN) * scale
            sums.append((dk * scale, dv))
        dkv_ref[rows, 0:128] = jnp.concatenate([sums[0][0], sums[1][0]], axis=1).astype(BF)
        dkv_ref[rows, 128:256] = jnp.concatenate([sums[0][1], sums[1][1]], axis=1).astype(BF)
        return carry

    lax.fori_loop(0, me + 1, step, 0)


def call(kernel, outs, *args, scratch=(), limit=20):
    spec = pl.BlockSpec(memory_space=pltpu.VMEM)
    return pl.pallas_call(
        kernel,
        out_shape=[jax.ShapeDtypeStruct(shape, dtype) for shape, dtype in outs],
        in_specs=[spec] * len(args),
        out_specs=[spec] * len(outs),
        scratch_shapes=list(scratch),
        compiler_params=pltpu.CompilerParams(vmem_limit_bytes=limit << 20),
    )(*args)


def places():
    s, f = lax.axis_index("seq"), lax.axis_index("fsdp")
    return s // 2, s % 2, f // 4, (f // 2) % 2, f % 2


def at_place(y, x_lo, z, x_hi, core):
    return {"seq": y * 2 + x_lo, "fsdp": z * 4 + x_hi * 2 + core}


def greet(others):
    barrier = pltpu.get_barrier_semaphore()
    for other in others:
        pl.semaphore_signal(barrier, inc=1, device_id=other, device_id_type=pl.DeviceIdType.MESH)
    pl.semaphore_wait(barrier, len(others))


WIDTHS = (1024, 1024, 1024, 1152)


def reduce_kernel(chunks, *refs):
    n = len(chunks)
    count = max(chunk[0] for chunk in chunks) + 1
    inputs, outs, refs = refs[:count], refs[count : 2 * count], refs[2 * count :]
    groups = [refs[i * 10 : i * 10 + 10] for i in range(n)]
    refs = refs[n * 10 :]
    pieces, (send, recv, local) = refs[:count], refs[count:]
    y, x_lo, z, x_hi, core = places()
    yn, yp, yo = (y + 1) % 4, (y + 3) % 4, (y + 2) % 4
    zn, zp, zo = (z + 1) % 4, (z + 3) % 4, (z + 2) % 4
    y_next, y_prev = at_place(yn, x_lo, z, x_hi, core), at_place(yp, x_lo, z, x_hi, core)
    y_far = at_place(yo, x_lo, z, x_hi, core)
    z_next, z_prev = at_place(y, x_lo, zn, x_hi, core), at_place(y, x_lo, zp, x_hi, core)
    across = at_place(y, 1 - x_lo, z, 1 - x_hi, core)
    beside = at_place(y, 1 - x_lo, z, x_hi, core)
    twin = at_place(y, x_lo, z, x_hi, 1 - core)
    greet((y_next, y_prev, y_far, z_next, z_prev, across, beside, twin))

    def copy(c, slot, source, target, device):
        return pltpu.make_async_remote_copy(
            src_ref=source, dst_ref=target, send_sem=send.at[c, slot], recv_sem=recv.at[c, slot],
            device_id=device, device_id_type=pl.DeviceIdType.MESH,
        )

    started = []

    def go(c, slot, source, target, device):
        item = copy(c, slot, source, target, device)
        item.start()
        started.append(item)
        return item

    def lanes(c):
        return pl.ds(chunks[c][1], chunks[c][2])

    first = [[None] * 16 for _ in range(n)]
    loads = []
    for c in range(n):
        acc, twin_buf = groups[c][0], groups[c][1]
        g = inputs[chunks[c][0]]
        first[c][0] = go(c, 0, g.at[:, :, 1 - core, :, :, lanes(c)], twin_buf, twin)
        load = pltpu.make_async_copy(g.at[:, :, core, :, :, lanes(c)], acc, local.at[c])
        load.start()
        loads.append(load)

    def add(target, source):
        target[...] = target[...] + source[...]

    def stage(c, step):
        acc, twin_buf, p1, m1, p2, m2, q1, r1, q2, r2 = groups[c][:10]
        kept = first[c]
        gathered = pieces[chunks[c][0]]
        y_first = c % 2 == 0
        if step == 0:
            loads[c].wait()
            kept[0].wait_recv()

            def body(i, carry):
                a, b, d = i // 8, (i // 4) % 2, i % 4
                add(acc.at[a, b, d], twin_buf.at[a, b, d])
                return carry

            lax.fori_loop(0, 32, body, 0)
            if y_first:
                kept[1] = go(c, 1, acc.at[:, 0, yo], p1, y_next)
                kept[2] = go(c, 2, acc.at[:, 1, yo], m1, y_prev)
            else:
                kept[1] = go(c, 1, acc.at[zo, 0], p1, z_next)
                kept[2] = go(c, 2, acc.at[zo, 1], m1, z_prev)
        elif step == 1:
            kept[1].wait_recv()
            kept[2].wait_recv()

            def body(i, carry):
                if y_first:
                    add(acc.at[i, 0, yn], p1.at[i])
                    add(acc.at[i, 1, yp], m1.at[i])
                else:
                    add(acc.at[zn, 0, i], p1.at[i])
                    add(acc.at[zp, 1, i], m1.at[i])
                return carry

            lax.fori_loop(0, 4, body, 0)
            if y_first:
                kept[3] = go(c, 3, acc.at[:, :, yn], p2, y_next)
                kept[4] = go(c, 4, acc.at[:, :, yp], m2, y_prev)
            else:
                kept[3] = go(c, 3, acc.at[zn], p2, z_next)
                kept[4] = go(c, 4, acc.at[zp], m2, z_prev)
        elif step == 2:
            kept[3].wait_recv()
            kept[4].wait_recv()

            def body(i, carry):
                if y_first:
                    a, b = i // 2, i % 2
                    add(acc.at[a, b, y], p2.at[a, b])
                    add(acc.at[a, b, y], m2.at[a, b])
                else:
                    a, b = i // 4, i % 4
                    add(acc.at[z, a, b], p2.at[a, b])
                    add(acc.at[z, a, b], m2.at[a, b])
                return carry

            lax.fori_loop(0, 8, body, 0)
            if y_first:
                kept[5] = go(c, 5, acc.at[zo, 0, y], q1, z_next)
                kept[6] = go(c, 6, acc.at[zo, 1, y], r1, z_prev)
            else:
                kept[5] = go(c, 5, acc.at[z, 0, yo], q1, y_next)
                kept[6] = go(c, 6, acc.at[z, 1, yo], r1, y_prev)
        elif step == 3:
            kept[5].wait_recv()
            kept[6].wait_recv()
            if y_first:
                add(acc.at[zn, 0, y], q1)
                add(acc.at[zp, 1, y], r1)
                kept[7] = go(c, 7, acc.at[zn, :, y], q2, z_next)
                kept[8] = go(c, 8, acc.at[zp, :, y], r2, z_prev)
            else:
                add(acc.at[z, 0, yn], q1)
                add(acc.at[z, 1, yp], r1)
                kept[7] = go(c, 7, acc.at[z, :, yn], q2, y_next)
                kept[8] = go(c, 8, acc.at[z, :, yp], r2, y_prev)
        elif step == 4:
            kept[7].wait_recv()
            kept[8].wait_recv()
            for b in range(2):
                add(acc.at[z, b, y], q2.at[b])
                add(acc.at[z, b, y], r2.at[b])
            kept[9] = go(c, 9, acc.at[z, 1 - x_hi, y], gathered.at[4, :, lanes(c)], across)
        elif step == 5:
            kept[9].wait_recv()
            acc[z, x_hi, y] = acc[z, x_hi, y] + gathered[4, :, lanes(c)]
            kept[10] = go(c, 10, acc.at[z, x_hi, y], gathered.at[5, :, lanes(c)], beside)
        elif step == 6:
            kept[10].wait_recv()
            gathered[y, :, lanes(c)] = acc[z, x_hi, y] + gathered[5, :, lanes(c)]
            mine = gathered.at[y, :, lanes(c)]
            kept[11] = go(c, 11, mine, mine, y_next)
            kept[12] = go(c, 12, mine, mine, y_prev)
            kept[13] = go(c, 13, mine, mine, y_far)
        else:
            for slot in (11, 12, 13):
                kept[slot].wait_recv()

    for step in range(8):
        for c in range(n):
            stage(c, step)
    for out, gathered in zip(outs, pieces):
        for i in range(4):
            out[i] = gathered[i].astype(F32)
    for item in started:
        item.wait_send()


def reduce_all(values, chunks):
    shapes = [(value.shape[0] // 64, value.shape[1]) for value in values]
    scratch = []
    for c, (which, _, w) in enumerate(chunks):
        r = shapes[which][0]
        scratch += [pltpu.VMEM((4, 2, 4, r, w), BF)] * 2 + [pltpu.VMEM((4, r, w), BF)] * 2
        scratch += [pltpu.VMEM((4, 2, r, w) if c % 2 == 0 else (2, 4, r, w), BF)] * 2
        scratch += [pltpu.VMEM((r, w), BF)] * 2 + [pltpu.VMEM((2, r, w), BF)] * 2
    n = len(chunks)
    scratch += [pltpu.VMEM((6,) + shape, BF) for shape in shapes]
    scratch += [pltpu.SemaphoreType.DMA((n, 14)), pltpu.SemaphoreType.DMA((n, 14)), pltpu.SemaphoreType.DMA((n,))]
    outs = pl.pallas_call(
        functools.partial(reduce_kernel, chunks),
        out_shape=[jax.ShapeDtypeStruct((4,) + shape, F32) for shape in shapes],
        in_specs=[pl.BlockSpec(memory_space=pl.ANY)] * len(values),
        out_specs=[pl.BlockSpec(memory_space=pltpu.VMEM)] * len(values),
        scratch_shapes=scratch,
        compiler_params=pltpu.CompilerParams(
            collective_id=1, has_side_effects=True, vmem_limit_bytes=60 << 20
        ),
        cost_estimate=pl.CostEstimate(flops=10**8, bytes_accessed=10**8, transcendentals=0),
    )(*[value.reshape((4, 2, 2, 4) + shape) for value, shape in zip(values, shapes)])
    return [out.reshape(4 * shape[0], shape[1]) for out, shape in zip(outs, shapes)]


REDUCED = (
    (1, 0, 1408), (1, 1408, 1408), (2, 0, 1024), (3, 0, 1024), (1, 2816, 1280), (0, 0, 1408), (0, 1408, 1408),
    (0, 2816, 1408),
)


def seq_group(s, send, recv):
    group = [{"seq": (s + d) % 8} for d in range(1, 8)]
    started = []

    def go(slot, d, source, target):
        item = pltpu.make_async_remote_copy(
            src_ref=source, dst_ref=target, send_sem=send.at[slot, d], recv_sem=recv.at[slot, d],
            device_id=group[d - 1], device_id_type=pl.DeviceIdType.MESH,
        )
        item.start()
        started.append(item)
        return item

    return group, started, go


def fade_of(ends, c, head):
    lane = lax.broadcasted_iota(jnp.int32, (1, 128), 1)
    row = ends[c][7:8, :]
    return jnp.exp(jnp.sum(jnp.where(lane == head, row, 0.0), axis=1, keepdims=True))


def share_forward(fresh, last, kv, starts_out, kv_out, ends_out, got, made, back, kv_all, ends, send, recv):
    s = lax.axis_index("seq")
    group, started, go = seq_group(s, send, recv)
    greet(group)
    waits = [[], [], [], []]
    for d in range(1, 8):
        waits[0].append(go(0, d, fresh.at[(s + d) % 8], got.at[s]))
        waits[1].append(go(1, d, last, ends.at[s]))
    for d in range(1, 8):
        waits[2].append(go(2, d, kv, kv_all.at[s]))
    got[s] = fresh[s]
    ends[s] = last[...]
    kv_all[s] = kv[...]
    for item in waits[0] + waits[1]:
        item.wait_recv()
    heads = fresh.shape[1] // AP
    for k in range(heads):
        rows = slice(k * AP, k * AP + AP)
        running = jnp.zeros((AP, NST), F32)
        for c in range(8):
            made[c, rows, :] = running.astype(BF)
            if c < 7:
                running = running * fade_of(ends, c, s * heads + k) + got[c, rows, :].astype(F32)
    for d in range(1, 8):
        waits[3].append(go(3, d, made.at[(s + d) % 8], back.at[s]))
    back[s] = made[s]
    for item in waits[3] + waits[2]:
        item.wait_recv()
    starts_out[...] = back[...]
    kv_out[...] = kv_all[...]
    ends_out[...] = ends[...]
    for item in started:
        item.wait_send()


def share_backward(dstart, ends, dkv, dends_out, dkv_out, got, made, back, kv_all, send, recv):
    s = lax.axis_index("seq")
    group, started, go = seq_group(s, send, recv)
    greet(group)
    waits = [[], [], []]
    for d in range(1, 8):
        waits[0].append(go(0, d, dstart.at[(s + d) % 8], got.at[s]))
    for d in range(1, 8):
        waits[1].append(go(1, d, dkv.at[(s + d) % 8], kv_all.at[s]))
    got[s] = dstart[s]
    kv_all[s] = dkv[s]
    for item in waits[0]:
        item.wait_recv()
    heads = dstart.shape[1] // AP
    for k in range(heads):
        rows = slice(k * AP, k * AP + AP)
        running = jnp.zeros((AP, NST), F32)
        for c in range(7, -1, -1):
            made[c, rows, :] = running.astype(BF)
            if c > 0:
                running = running * fade_of(ends, c, s * heads + k) + got[c, rows, :].astype(F32)
    for d in range(1, 8):
        waits[2].append(go(2, d, made.at[(s + d) % 8], back.at[s]))
    back[s] = made[s]
    for item in waits[1]:
        item.wait_recv()
    total = kv_all[0].astype(F32)
    for c in range(1, 8):
        total = total + kv_all[c].astype(F32)
    dkv_out[...] = total
    for item in waits[2]:
        item.wait_recv()
    dends_out[...] = back[...]
    for item in started:
        item.wait_send()


def share_call(kernel, collective, outs, scratch, slots, *args):
    spec = pl.BlockSpec(memory_space=pltpu.VMEM)
    return pl.pallas_call(
        kernel,
        out_shape=[jax.ShapeDtypeStruct(shape, dtype) for shape, dtype in outs],
        in_specs=[spec] * len(args),
        out_specs=[spec] * len(outs),
        scratch_shapes=[pltpu.VMEM(shape, dtype) for shape, dtype in scratch]
        + [pltpu.SemaphoreType.DMA((slots, 8))] * 2,
        compiler_params=pltpu.CompilerParams(
            collective_id=collective, has_side_effects=True, vmem_limit_bytes=24 << 20
        ),
        cost_estimate=pl.CostEstimate(flops=10**7, bytes_accessed=10**7, transcendentals=0),
    )(*args)


def gather_kernel(own, out, send, recv, local):
    n = len(WIDTHS)
    y, x_lo, z, x_hi, core = places()
    yn, yp, yo = (y + 1) % 4, (y + 3) % 4, (y + 2) % 4
    zn, zp, zo = (z + 1) % 4, (z + 3) % 4, (z + 2) % 4
    y_next, y_prev = at_place(yn, x_lo, z, x_hi, core), at_place(yp, x_lo, z, x_hi, core)
    z_next, z_prev = at_place(y, x_lo, zn, x_hi, core), at_place(y, x_lo, zp, x_hi, core)
    across = at_place(y, 1 - x_lo, z, 1 - x_hi, core)
    twin = at_place(y, x_lo, z, x_hi, 1 - core)
    greet((y_next, y_prev, z_next, z_prev, across, twin))
    started = []

    def lanes(c):
        return pl.ds(sum(WIDTHS[:c]), WIDTHS[c])

    def go(c, slot, source, target, device):
        item = pltpu.make_async_remote_copy(
            src_ref=source, dst_ref=target, send_sem=send.at[c, slot], recv_sem=recv.at[c, slot],
            device_id=device, device_id_type=pl.DeviceIdType.MESH,
        )
        item.start()
        started.append(item)
        return item

    held = [[None] * 10 for _ in range(n)]
    loads = []

    def stage(c, step):
        kept = held[c]
        cols = lanes(c)
        split = c % 2 == 0
        rows = pl.ds(y, 1) if split else pl.ds(0, 4)

        def part(a, b, d):
            return out.at[a, b, core, d, :, cols]

        def pass_on(slot, source, device):
            kept[slot] = go(c, slot, source, source, device)

        if step == 0:
            kept[0] = go(c, 0, own.at[rows, :, cols], part(z, x_hi, rows), across)
            load = pltpu.make_async_copy(own.at[rows, :, cols], part(z, x_hi, rows), local.at[c])
            load.start()
            loads.append(load)
        elif step == 1:
            loads[c].wait()
            kept[0].wait_recv()
            pass_on(1, part(z, slice(None), rows), z_next)
            pass_on(2, part(z, slice(None), rows), z_prev)
        elif step == 2:
            kept[1].wait_recv()
            kept[2].wait_recv()
            pass_on(3, part(zp, 0, rows), z_next)
            pass_on(4, part(zn, 1, rows), z_prev)
        elif step == 3:
            kept[3].wait_recv()
            kept[4].wait_recv()
            if split:
                pass_on(5, part(slice(None), slice(None), rows), y_next)
                pass_on(6, part(slice(None), slice(None), rows), y_prev)
            else:
                pass_on(9, part(slice(None), slice(None), rows), twin)
        elif step == 4 and split:
            kept[5].wait_recv()
            kept[6].wait_recv()
            pass_on(7, part(slice(None), 0, pl.ds(yp, 1)), y_next)
            pass_on(8, part(slice(None), 1, pl.ds(yn, 1)), y_prev)
        elif step == 5 and split:
            kept[7].wait_recv()
            kept[8].wait_recv()
            pass_on(9, part(slice(None), slice(None), slice(None)), twin)
        elif step == 6:
            kept[9].wait_recv()

    for step in range(7):
        for c in range(n):
            stage(c, step)
    for item in started:
        item.wait_send()


def gather_all(own):
    cols = own.shape[1]
    n = len(WIDTHS)
    out = pl.pallas_call(
        gather_kernel,
        out_shape=jax.ShapeDtypeStruct((4, 2, 2, 4, 16, cols), BF),
        in_specs=[pl.BlockSpec(memory_space=pl.ANY)],
        out_specs=pl.BlockSpec(memory_space=pl.ANY),
        scratch_shapes=[
            pltpu.SemaphoreType.DMA((n, 10)), pltpu.SemaphoreType.DMA((n, 10)), pltpu.SemaphoreType.DMA((n,))
        ],
        compiler_params=pltpu.CompilerParams(collective_id=2, has_side_effects=True),
        cost_estimate=pl.CostEstimate(flops=10**8, bytes_accessed=10**8, transcendentals=0),
    )(own.reshape(4, 16, cols))
    return out.reshape(1024, cols)


def rope_parts(length, start):
    half = AP // 2
    inverse = THETA ** (-2.0 * jnp.arange(half).astype(F32) / AP)
    angles = (start + jnp.arange(length)).astype(F32)[:, None] * inverse[None, :]
    cosine = jnp.cos(angles)
    sine = jnp.sin(angles)
    return jnp.concatenate([cosine, cosine], axis=1), jnp.concatenate([-sine, sine], axis=1)


def swap_halves(value):
    rows, cols = value.shape
    parts = value.reshape(rows, cols // AP, 2, AP // 2)
    return parts[:, :, ::-1, :].reshape(rows, cols)


def pad_lanes(value):
    return jnp.pad(value.astype(F32), (0, 128 - value.shape[0]))[None, :]


def per_device(
    seqs, hidden_in, norm_gain, mixer_proj, attn_proj, conv_kernel, conv_bias, step_bias, decay_log,
    skip_gain, gated_gain, mixer_out, attn_out, ffn_gain, gate_up, down_proj, out_grad,
):
    T = hidden_in.shape[1]
    width = norm_gain.shape[0]
    shards = 1024 // width
    me = lax.axis_index("seq")
    mix_rows, att_rows, down_rows = mixer_out.shape[0], attn_out.shape[0], down_proj.shape[0]

    small = jnp.concatenate(
        [norm_gain, ffn_gain, gated_gain, conv_bias, conv_kernel.T.reshape(-1)]
    )
    slots = width * 104
    small = jnp.pad(small, (0, slots - small.shape[0])).reshape(width, 104)
    front_shard = jnp.concatenate(
        [mixer_proj[:, : D_SSM + XBC], attn_proj, mixer_proj[:, D_SSM + XBC :], small], axis=1
    )
    front = gather_all(front_shard)
    tail_shard = jnp.concatenate(
        [
            gate_up[:, :FF],
            gate_up[:, FF:],
            jnp.concatenate([jnp.concatenate([mixer_out, attn_out], axis=0), down_proj], axis=1),
        ],
        axis=0,
    )
    tail = lax.all_gather(tail_shard, "fsdp", axis=0, tiled=False)
    smalls = front.reshape(shards, width, FRONT)[:, :, 4120:].reshape(shards, slots)
    cuts = []
    at = 0
    for size in (width, width, gated_gain.shape[0], conv_bias.shape[0]):
        cuts.append(smalls[:, at : at + size].reshape(1, -1).astype(F32))
        at += size
    gain_one, gain_ffn, gain_gated, bias_all = cuts
    kernel_size = conv_kernel.shape[0]
    taps = smalls[:, at : at + 4 * kernel_size].reshape(shards, 4, kernel_size)
    taps = taps.transpose(1, 0, 2).reshape(4, XBC).astype(F32)
    taps = jnp.pad(taps, ((0, 4), (0, 0)))

    resid = hidden_in[0].astype(F32)
    scale_one = rms_scale(resid)
    normed_one = resid * scale_one
    normed_in = (normed_one * gain_one).astype(BF)
    projection = dot(normed_in, front)
    gate_pre = projection[:, :D_SSM]
    xbc = projection[:, D_SSM : D_SSM + XBC].astype(BF)
    queries = projection[:, 3328:3840].astype(BF)
    keyvals = projection[:, 3840:4096].astype(BF)
    steps = projection[:, 4096:].astype(BF)
    cosine, sine = rope_parts(T, me * T)
    cos_q, sin_q = jnp.tile(cosine, (1, QH)), jnp.tile(sine, (1, QH))
    cos_k, sin_k = jnp.tile(cosine, (1, KVH)), jnp.tile(sine, (1, KVH))
    query_rot = queries.astype(F32)
    query_rot = (query_rot * cos_q + swap_halves(query_rot) * sin_q).astype(BF)
    keys = keyvals[:, : KVH * AP].astype(F32)
    key_rot = (keys * cos_k + swap_halves(keys) * sin_k).astype(BF)
    kv_own = jnp.concatenate([key_rot, keyvals[:, KVH * AP :]], axis=1)
    halo = lax.ppermute(xbc[-8:], "seq", [(i, i + 1) for i in range(seqs - 1)])
    sbias, dlog, skip = pad_lanes(step_bias), pad_lanes(decay_log), pad_lanes(skip_gain)
    act, dt, cum, fresh = call(
        mamba_first,
        [((T, XBC), F32), ((T, 128), F32), ((T, 128), F32), ((D_SSM, NST), BF)],
        xbc, halo, steps, taps, bias_all, sbias, dlog,
        scratch=[pltpu.VMEM((T + 8, XBC), F32)],
    )
    heads = MH // seqs
    states = ((seqs, heads * AP, NST), BF)
    pairs = ((seqs, T, 2 * KVH * AP), BF)
    tails = ((seqs, 8, 128), F32)
    starts, kv_all, ends = share_call(
        share_forward, 3, [states, pairs, tails], [states, states, states, pairs, tails], 4,
        fresh.reshape(states[0]), cum[T - 8 :], kv_own,
    )
    starts = starts.reshape(D_SSM, NST)
    kv_all = kv_all.reshape(seqs * T, 2 * KVH * AP)
    attn_tok, lse = call(
        functools.partial(attend_forward, "seq"),
        [((T, QH * AP), BF), ((QH, T), F32)],
        query_rot, kv_all,
        scratch=[pltpu.VMEM((QH * AP, T), F32), pltpu.VMEM((QH, T), F32), pltpu.VMEM((QH, T), F32)],
    )
    (mixed_y,) = call(mamba_second, [((T, D_SSM), BF)], act, dt, cum, starts, skip)

    proj_gate = tail[:, :width].reshape(-1, FF)
    proj_up = tail[:, width : 2 * width].reshape(-1, FF)
    low_rows = 2 * width
    out_mixer = tail[:, low_rows : low_rows + mix_rows, :1024].reshape(-1, 1024)
    out_attn = tail[:, low_rows + mix_rows :, :1024].reshape(-1, 1024)
    proj_down = tail[:, low_rows:, 1024:].reshape(-1, 1024)
    mixed = mixed_y.astype(F32)
    gated = mixed * jax.nn.silu(gate_pre)
    scale_two = rms_scale(gated)
    normed_two = gated * scale_two
    normed_mix = (normed_two * gain_gated).astype(BF)
    middle = resid + dot(normed_mix, out_mixer) + dot(attn_tok, out_attn)
    scale_three = rms_scale(middle)
    normed_three = middle * scale_three
    normed_ffn = (normed_three * gain_ffn).astype(BF)
    gate_half = dot(normed_ffn, proj_gate)
    up_half = dot(normed_ffn, proj_up)
    activ = (jax.nn.silu(gate_half) * up_half).astype(BF)
    block_out = (middle + dot(activ, proj_down)).astype(BF)

    ograd = out_grad[0]
    grad_activ = dot(ograd, proj_down, NT)
    grad_down = dot(activ, ograd, TN).astype(BF)
    grad_g = (grad_activ * up_half * silu_slope(gate_half)).astype(BF)
    grad_u = (grad_activ * jax.nn.silu(gate_half)).astype(BF)
    grad_gateup = dot(normed_ffn, jnp.concatenate([grad_g, grad_u], axis=1), TN).astype(BF)
    grad_nffn = dot(grad_g, proj_gate, NT) + dot(grad_u, proj_up, NT)
    grad_ffn = jnp.sum(grad_nffn * normed_three, axis=0)
    grad_middle = ograd.astype(F32) + rms_back(grad_nffn * gain_ffn, normed_three, scale_three)
    middle_bf = grad_middle.astype(BF)
    grad_mixed = dot(normed_mix, middle_bf, TN).astype(BF)
    grad_attended = dot(attn_tok, middle_bf, TN).astype(BF)
    grad_nmix = dot(middle_bf, out_mixer, NT)
    grad_otok = dot(middle_bf, out_attn, NT).astype(BF)
    grad_gated = jnp.sum(grad_nmix * normed_two, axis=0)
    grad_gz = rms_back(grad_nmix * gain_gated, normed_two, scale_two)
    grad_ymix = (grad_gz * jax.nn.silu(gate_pre)).astype(BF)
    grad_gate = (grad_gz * mixed * silu_slope(gate_pre)).astype(BF)
    grad_outs = jnp.concatenate(
        [grad_mixed.reshape(shards, mix_rows, 1024), grad_attended.reshape(shards, att_rows, 1024)], axis=1
    ).reshape(-1, 1024)

    (dstart,) = call(mamba_back_first, [((D_SSM, NST), BF)], grad_ymix, act, cum)
    dq, dkv = call(
        functools.partial(attend_backward, "seq"),
        [((T, QH * AP), F32), ((kv_all.shape[0], 2 * KVH * AP), BF)],
        query_rot, kv_all, attn_tok, lse, grad_otok,
    )
    dends, dkv = share_call(
        share_backward, 4, [states, ((T, 2 * KVH * AP), F32)], [states, states, states, pairs], 3,
        dstart.reshape(states[0]), ends, dkv.reshape(pairs[0]),
    )
    dends = dends.reshape(D_SSM, NST)
    qgrad = (dq * cos_q - swap_halves(dq) * sin_q).astype(BF)
    dk = dkv[:, : KVH * AP]
    kgrad = (dk * cos_k - swap_halves(dk) * sin_k).astype(BF)
    dconv, dtaps, dbias, dsteps, dhead = call(
        mamba_back_second,
        [((T, XBC), F32), ((8, XBC), F32), ((8, XBC), F32), ((T, 128), BF), ((8, 128), F32)],
        grad_ymix, xbc, halo, act, dt, cum, starts, dends, steps, taps, bias_all, sbias, dlog, skip,
        scratch=[pltpu.VMEM((T + 8, XBC), F32), pltpu.VMEM((T, XBC), F32)],
        limit=32,
    )
    ahead = lax.ppermute(dconv[:8].astype(BF), "seq", [(i + 1, i) for i in range(seqs - 1)])
    later = jnp.concatenate([dconv, ahead.astype(F32)], axis=0)
    du = taps[3:4] * dconv
    for lag in range(3):
        du = du + taps[lag : lag + 1] * later[3 - lag : 3 - lag + T]
    grad_proj = jnp.concatenate(
        [grad_gate, du.astype(BF), qgrad, kgrad, dkv[:, KVH * AP :].astype(BF), dsteps], axis=1
    )

    grad_front = dot(normed_in, grad_proj, TN).astype(BF)
    grad_nin = dot(grad_proj, front, NT)
    grad_norm = jnp.sum(grad_nin * normed_one, axis=0)
    input_grad = grad_middle + rms_back(grad_nin * gain_one, normed_one, scale_one)
    vectors = [grad_norm, grad_ffn, grad_gated, dbias[0]] + [dtaps[lag] for lag in range(4)]
    vectors = [value.reshape(shards, -1) for value in vectors]
    vectors.append(jnp.broadcast_to(dhead[:3, :MH].reshape(1, 3 * MH), (shards, 3 * MH)))
    vectors = jnp.concatenate(vectors, axis=1)
    vectors = jnp.pad(vectors, ((0, 0), (0, slots - vectors.shape[1]))).astype(BF)
    last = jnp.concatenate([grad_front[:, 4096:4120], vectors.reshape(-1, 104)], axis=1)
    front_sum, gateup_sum, outs_sum, down_sum = reduce_all(
        [lax.dynamic_update_slice(grad_front, last, (0, 4096)), grad_gateup, grad_outs, grad_down], REDUCED
    )
    vectors = front_sum[:, 4120:].reshape(-1)
    owned = []
    at = 0
    for size in [width, width, gated_gain.shape[0], kernel_size] + [kernel_size] * 4 + [MH] * 3:
        owned.append(vectors[at : at + size])
        at += size
    own_taps = jnp.stack(owned[4:8], axis=1)
    return (
        block_out[None],
        input_grad[None],
        owned[0],
        jnp.concatenate([front_sum[:, : D_SSM + XBC], front_sum[:, 4096:4120]], axis=1),
        front_sum[:, 3328:4096],
        own_taps,
        owned[3],
        owned[8],
        owned[9],
        owned[10],
        owned[2],
        outs_sum[:mix_rows],
        outs_sum[mix_rows:],
        owned[1],
        gateup_sum,
        down_sum,
    )


def solution(mesh):
    tokens = P("fsdp", "seq", None)
    vector = P("fsdp")
    matrix = P("fsdp", None)
    in_specs = (
        tokens, vector, matrix, matrix, matrix, vector, P(), P(), P(), vector, matrix, matrix, vector,
        matrix, matrix, tokens,
    )
    out_specs = (
        tokens, tokens, vector, matrix, matrix, matrix, vector, P(), P(), P(), vector, matrix, matrix,
        vector, matrix, matrix,
    )
    return jax.shard_map(
        functools.partial(per_device, mesh.shape["seq"]),
        mesh=mesh, in_specs=in_specs, out_specs=out_specs, check_vma=False,
    )
```

```python
import functools
import math

import jax
import jax.numpy as jnp
from jax import lax
from jax.experimental import pallas as pl
from jax.experimental.pallas import tpu as pltpu
from jax.sharding import PartitionSpec as P

MH = 24
NST = 128
QH = 8
KVH = 2
AP = 64
FF = 2048
D_SSM = 1536
XBC = 1792
CIN = 3352
FRONT = 4224
EPSILON = 1e-05
THETA = 10000.0
HIGHEST = lax.Precision.HIGHEST
F32 = jnp.float32
BF = jnp.bfloat16
NT = (((1,), (1,)), ((), ()))
TN = (((0,), (0,)), ((), ()))


def dot(a, b, dims=(((1,), (0,)), ((), ())), precision=None):
    return lax.dot_general(a, b, dims, preferred_element_type=F32, precision=precision)


def silu_slope(value):
    sigma = jax.nn.sigmoid(value)
    return sigma * (1.0 + value * (1.0 - sigma))


def rms_scale(value):
    return lax.rsqrt(jnp.mean(value * value, axis=1, keepdims=True) + EPSILON)


def rms_back(grad_normed, normed, scale):
    return scale * (grad_normed - normed * jnp.mean(grad_normed * normed, axis=1, keepdims=True))


def head_selector(rows, cols):
    channel = lax.broadcasted_iota(jnp.int32, (rows, cols), 0)
    head = lax.broadcasted_iota(jnp.int32, (rows, cols), 1)
    return jnp.where((channel >= head * AP) & (channel < head * AP + AP), 1.0, 0.0).astype(F32)


def spread_heads(value):
    head = lax.broadcasted_iota(jnp.int32, (128, D_SSM), 0)
    channel = lax.broadcasted_iota(jnp.int32, (128, D_SSM), 1)
    select = jnp.where((channel >= head * AP) & (channel < head * AP + AP), 1.0, 0.0).astype(F32)
    return dot(value, select, precision=HIGHEST)


def gather_heads(value):
    return dot(value, head_selector(D_SSM, 128), precision=HIGHEST)


def conv_pre(ext, taps, bias, length):
    result = bias[...] + taps[3:4, :] * ext[8 : 8 + length, :]
    for lag in range(3):
        result = result + taps[lag : lag + 1, :] * ext[pl.ds(5 + lag, length), :]
    return result


def swap_halves(value):
    lane = lax.broadcasted_iota(jnp.int32, value.shape, 1)
    return jnp.where(lane % AP < AP // 2, pltpu.roll(value, 96, 1), pltpu.roll(value, 32, 1))


def mamba_first(
    proj, halo, cosine, sine, taps, bias, sbias, dlog,
    act_ref, dt_ref, cum_ref, fresh_ref, xbc_ref, steps_ref, q_ref, kv_ref, ext,
):
    length = proj.shape[0]
    for pair in range(QH // 2 + 1):
        at = D_SSM + XBC + pair * 128
        value = proj[:, at : at + 128].astype(BF).astype(F32)
        value = (value * cosine[...] + swap_halves(value) * sine[...]).astype(BF)
        if pair < QH // 2:
            q_ref[:, pair * 128 : pair * 128 + 128] = value
        else:
            kv_ref[:, 0:128] = value
    kv_ref[:, 128:256] = proj[:, 3968:4096].astype(BF)
    xbc = proj[:, D_SSM : D_SSM + XBC].astype(BF)
    steps = proj[:, 4096:].astype(BF)
    xbc_ref[...] = xbc
    steps_ref[...] = steps
    ext[0:8, :] = halo[...].astype(F32)
    ext[8 : 8 + length, :] = xbc.astype(F32)
    conv = conv_pre(ext, taps, bias, length)
    act = conv * jax.nn.sigmoid(conv)
    act_ref[...] = act
    lane = lax.broadcasted_iota(jnp.int32, (length, 128), 1)
    raw = steps.astype(F32) + sbias[...]
    dt = jnp.maximum(raw, 0.0) + jnp.log1p(jnp.exp(-jnp.abs(raw)))
    dt = jnp.where(lane < MH, dt, 0.0)
    dt_ref[...] = dt
    row = lax.broadcasted_iota(jnp.int32, (length, length), 0)
    col = lax.broadcasted_iota(jnp.int32, (length, length), 1)
    lower = jnp.where(row >= col, 1.0, 0.0).astype(F32)
    cum = dot(lower, dt * (-jnp.exp(dlog[...])), precision=HIGHEST)
    cum_ref[...] = cum
    weight = spread_heads(jnp.exp(cum[length - 1 : length, :] - cum) * dt)
    scaled = (act[:, :D_SSM] * weight).astype(BF)
    fresh_ref[...] = dot(scaled, act[:, D_SSM : D_SSM + NST].astype(BF), TN).astype(BF)


def mamba_second(act, dt, cum, starts, skip, y_ref):
    length = act.shape[0]
    cumv = cum[...]
    cum_t = cumv.T
    bmat = act[:, D_SSM : D_SSM + NST].astype(BF)
    cmat = act[:, D_SSM + NST :].astype(BF)
    inner = dot(cmat, bmat, NT)
    row = lax.broadcasted_iota(jnp.int32, (length, length), 0)
    col = lax.broadcasted_iota(jnp.int32, (length, length), 1)
    inner = jnp.where(row >= col, inner, 0.0)
    x = act[:, :D_SSM]
    scaled = (x * spread_heads(dt[...])).astype(BF)
    outer = dot(cmat, starts[...], NT) * spread_heads(jnp.exp(cumv))
    base = outer + spread_heads(skip[...]) * x
    for pair in range(MH // 2):
        parts = []
        for h in (2 * pair, 2 * pair + 1):
            fade = jnp.exp(jnp.minimum(cumv[:, h : h + 1] - cum_t[h : h + 1, :], 0.0))
            parts.append(dot((inner * fade).astype(BF), scaled[:, h * AP : h * AP + AP]))
        lanes = slice(pair * 128, pair * 128 + 128)
        y_ref[:, lanes] = (base[:, lanes] + jnp.concatenate(parts, axis=1)).astype(BF)


def mamba_back_first(gy, act, cum, dstart_ref):
    rise = spread_heads(jnp.exp(cum[...]))
    cmat = act[:, D_SSM + NST :].astype(BF)
    dstart_ref[...] = dot((gy[...].astype(F32) * rise).astype(BF), cmat, TN).astype(BF)


def mamba_back_second(
    gy, xbc, halo, act, dt, cum, starts, dends, steps, taps, bias, sbias, dlog, skip,
    dconv_ref, dtaps_ref, dbias_ref, dsteps_ref, dhead_ref, ext, dact,
):
    length = act.shape[0]
    cumv = cum[...]
    dtv = dt[...]
    cum_t = cumv.T
    lane = lax.broadcasted_iota(jnp.int32, (length, 128), 1)
    bmat = act[:, D_SSM : D_SSM + NST].astype(BF)
    cmat = act[:, D_SSM + NST :].astype(BF)
    row = lax.broadcasted_iota(jnp.int32, (length, length), 0)
    col = lax.broadcasted_iota(jnp.int32, (length, length), 1)
    inner_t = jnp.where(col >= row, dot(bmat, cmat, NT), 0.0)
    x = act[:, :D_SSM]
    gyb = gy[...]
    gyf = gyb.astype(F32)
    dt_full = spread_heads(dtv)
    tail = spread_heads(jnp.exp(cumv[length - 1 : length, :] - cumv))
    rise = spread_heads(jnp.exp(cumv))
    xs = x * dt_full
    xsb = xs.astype(BF)
    ginner = jnp.zeros((length, length), F32)
    qcols = jnp.zeros((length, 128), F32)
    rrows = []
    for pair in range(MH // 2):
        parts = []
        for h in (2 * pair, 2 * pair + 1):
            lanes = slice(h * AP, h * AP + AP)
            fade = jnp.exp(jnp.minimum(cum_t[h : h + 1, :] - cumv[:, h : h + 1], 0.0))
            graded = dot(xsb[:, lanes], gyb[:, lanes], NT) * fade
            ginner = ginner + graded
            weighed = graded * inner_t
            rrows.append(jnp.sum(weighed, axis=0, keepdims=True))
            qcols = jnp.where(lane == h, jnp.sum(weighed, axis=1, keepdims=True), qcols)
            parts.append(dot((inner_t * fade).astype(BF), gyb[:, lanes]))
        dact[:, pair * 128 : pair * 128 + 128] = jnp.concatenate(parts, axis=1)
    ginner = jnp.where(col >= row, ginner, 0.0).astype(BF)
    rrows = jnp.concatenate(rrows + [jnp.zeros((128 - MH, length), F32)], axis=0).T
    endb = dends[...]
    startb = starts[...]
    from_end = dot(bmat, endb, NT) * tail
    dxs = dact[:, :D_SSM] + from_end
    reach = gather_heads(xs * from_end)
    outer = dot(cmat, startb, NT) * rise
    dcum = rrows - qcols + gather_heads(gyf * outer) - reach
    total = jnp.exp(cumv[length - 1 : length, :])
    carried = gather_heads_rows(startb, endb) * total + jnp.sum(reach, axis=0, keepdims=True)
    last = lax.broadcasted_iota(jnp.int32, (length, 128), 0) == length - 1
    dcum = dcum + jnp.where(last, carried, 0.0)
    upper = jnp.where(col >= row, 1.0, 0.0).astype(F32)
    rest = dot(upper, dcum, precision=HIGHEST)
    decay = -jnp.exp(dlog[...])
    ddt = gather_heads(x * dxs) + decay * rest
    ddecay = jnp.sum(dtv * rest, axis=0, keepdims=True) * decay
    raw = steps[...].astype(F32) + sbias[...]
    dsteps = jnp.where(lane < MH, ddt * jax.nn.sigmoid(raw), 0.0)
    dsteps_ref[...] = dsteps.astype(BF)
    dskip = gather_heads(jnp.sum(x * gyf, axis=0, keepdims=True))
    dhead_ref[0:1, :] = jnp.sum(dsteps, axis=0, keepdims=True)
    dhead_ref[1:2, :] = ddecay
    dhead_ref[2:3, :] = dskip
    dhead_ref[3:8, :] = jnp.zeros((5, 128), F32)
    dact[:, :D_SSM] = dt_full * dxs + spread_heads(skip[...]) * gyf
    dact[:, D_SSM : D_SSM + NST] = dot((xs * tail).astype(BF), endb) + dot(ginner, cmat)
    dact[:, D_SSM + NST :] = dot((gyf * rise).astype(BF), startb) + dot(ginner, bmat, TN)
    ext[0:8, :] = halo[...].astype(F32)
    ext[8 : 8 + length, :] = xbc[...].astype(F32)
    conv = conv_pre(ext, taps, bias, length)
    dconv = dact[...] * silu_slope(conv)
    dconv_ref[...] = dconv
    dbias_ref[...] = jnp.broadcast_to(jnp.sum(dconv, axis=0, keepdims=True), (8, XBC))
    for lag in range(4):
        dtaps_ref[lag : lag + 1, :] = jnp.sum(
            dconv * ext[pl.ds(5 + lag, length), :], axis=0, keepdims=True
        )
    dtaps_ref[4:8, :] = jnp.zeros((4, XBC), F32)


def gather_heads_rows(a, b):
    product = a.astype(F32) * b.astype(F32)
    per_row = dot(jnp.ones((8, NST), F32), product, NT, precision=HIGHEST)
    return gather_heads(per_row)[0:1, :]


def attend_forward(axis, q, kv, o_ref, lse_ref, acc, top, total):
    me = lax.axis_index(axis)
    block = q.shape[0]
    scale = 1.0 / math.sqrt(AP)
    acc[...] = jnp.zeros_like(acc)
    top[...] = jnp.full(top.shape, -jnp.inf, F32)
    total[...] = jnp.zeros_like(total)
    key_at = lax.broadcasted_iota(jnp.int32, (block, block), 0)
    query_at = lax.broadcasted_iota(jnp.int32, (block, block), 1)

    def step(j, carry):
        rows = pl.ds(pl.multiple_of(j * block, block), block)
        allowed = (key_at + j * block) <= (query_at + me * block)
        for h in range(QH):
            g = h // (QH // KVH)
            keys = kv[rows, g * AP : g * AP + AP]
            values = kv[rows, KVH * AP + g * AP : KVH * AP + g * AP + AP]
            s = dot(keys, q[:, h * AP : h * AP + AP], NT) * scale
            s = jnp.where(allowed, s, -1e30)
            old = top[h : h + 1, :]
            new = jnp.maximum(old, jnp.max(s, axis=0, keepdims=True))
            p = jnp.exp(s - new)
            fix = jnp.exp(old - new)
            top[h : h + 1, :] = new
            total[h : h + 1, :] = total[h : h + 1, :] * fix + jnp.sum(p, axis=0, keepdims=True)
            band = slice(h * AP, h * AP + AP)
            acc[band, :] = acc[band, :] * fix + dot(values, p.astype(BF), TN)
        return carry

    lax.fori_loop(0, me + 1, step, 0)
    lse_ref[...] = top[...] + jnp.log(total[...])
    for pair in range(QH // 2):
        parts = []
        for h in (2 * pair, 2 * pair + 1):
            parts.append(acc[h * AP : h * AP + AP, :] / total[h : h + 1, :])
        o_ref[:, pair * 128 : pair * 128 + 128] = jnp.concatenate(parts, axis=0).T.astype(BF)


def attend_backward(axis, q, kv, o, lse, go, cosine, sine, out_ref, dkv_ref, dq_ref):
    me = lax.axis_index(axis)
    block = q.shape[0]
    scale = 1.0 / math.sqrt(AP)
    dq_ref[...] = jnp.zeros_like(dq_ref)
    dkv_ref[...] = jnp.zeros_like(dkv_ref)
    key_at = lax.broadcasted_iota(jnp.int32, (block, block), 0)
    query_at = lax.broadcasted_iota(jnp.int32, (block, block), 1)
    centred = go[...].astype(F32) * o[...].astype(F32)
    pick_h = lax.broadcasted_iota(jnp.int32, (8, QH * AP), 0)
    pick_c = lax.broadcasted_iota(jnp.int32, (8, QH * AP), 1)
    pick = jnp.where((pick_c >= pick_h * AP) & (pick_c < pick_h * AP + AP), 1.0, 0.0).astype(F32)
    centre = dot(pick, centred, NT, precision=HIGHEST)

    def step(j, carry):
        rows = pl.ds(pl.multiple_of(j * block, block), block)
        allowed = (key_at + j * block) <= (query_at + me * block)
        sums = []
        for g in range(KVH):
            keys = kv[rows, g * AP : g * AP + AP]
            values = kv[rows, KVH * AP + g * AP : KVH * AP + g * AP + AP]
            dk = jnp.zeros((block, AP), F32)
            dv = jnp.zeros((block, AP), F32)
            for h in range(g * (QH // KVH), (g + 1) * (QH // KVH)):
                band = slice(h * AP, h * AP + AP)
                qh = q[:, band]
                gh = go[:, band]
                s = dot(keys, qh, NT) * scale
                p = jnp.exp(jnp.where(allowed, s - lse[h : h + 1, :], -1e30))
                dv = dv + dot(p.astype(BF), gh)
                dp = dot(values, gh, NT)
                ds = (p * (dp - centre[h : h + 1, :])).astype(BF)
                dk = dk + dot(ds, qh)
                dq_ref[:, band] += dot(ds, keys, TN) * scale
            sums.append((dk * scale, dv))
        dkv_ref[rows, 0:128] = jnp.concatenate([sums[0][0], sums[1][0]], axis=1).astype(BF)
        dkv_ref[rows, 128:256] = jnp.concatenate([sums[0][1], sums[1][1]], axis=1).astype(BF)
        return carry

    lax.fori_loop(0, me + 1, step, 0)
    for pair in range(QH // 2):
        value = dq_ref[:, pair * 128 : pair * 128 + 128]
        value = value * cosine[...] - swap_halves(value) * sine[...]
        out_ref[:, pair * 128 : pair * 128 + 128] = value.astype(BF)


def finish_grads(dconv, ahead, taps, gate, dq, dkv, dsteps, out_ref, ext):
    length = dconv.shape[0]
    ext[0:length, :] = dconv[...]
    ext[length : length + 8, :] = ahead[...].astype(F32)
    du = taps[3:4, :] * ext[0:length, :]
    for lag in range(3):
        du = du + taps[lag : lag + 1, :] * ext[pl.ds(3 - lag, length), :]
    out_ref[:, :D_SSM] = gate[...]
    out_ref[:, D_SSM : D_SSM + XBC] = du.astype(BF)
    out_ref[:, 3328:3840] = dq[...]
    out_ref[:, 3840:4096] = dkv[...]
    out_ref[:, 4096:] = dsteps[...]


def call(kernel, outs, *args, scratch=(), limit=20):
    spec = pl.BlockSpec(memory_space=pltpu.VMEM)
    return pl.pallas_call(
        kernel,
        out_shape=[jax.ShapeDtypeStruct(shape, dtype) for shape, dtype in outs],
        in_specs=[spec] * len(args),
        out_specs=[spec] * len(outs),
        scratch_shapes=list(scratch),
        compiler_params=pltpu.CompilerParams(vmem_limit_bytes=limit << 20),
    )(*args)


def places():
    s, f = lax.axis_index("seq"), lax.axis_index("fsdp")
    return s // 2, s % 2, f // 4, (f // 2) % 2, f % 2


def at_place(y, x_lo, z, x_hi, core):
    return {"seq": y * 2 + x_lo, "fsdp": z * 4 + x_hi * 2 + core}


def greet(others):
    barrier = pltpu.get_barrier_semaphore()
    for other in others:
        pl.semaphore_signal(barrier, inc=1, device_id=other, device_id_type=pl.DeviceIdType.MESH)
    pl.semaphore_wait(barrier, len(others))


WIDTHS = (1024, 1024, 1024, 1152)


def reduce_kernel(chunks, *refs):
    n = len(chunks)
    count = max(chunk[0] for chunk in chunks) + 1
    inputs, outs, refs = refs[:count], refs[count : count + 7], refs[count + 7 :]
    groups = [refs[i * 10 : i * 10 + 10] for i in range(n)]
    refs = refs[n * 10 :]
    pieces, (send, recv, local) = refs[:count], refs[count:]
    y, x_lo, z, x_hi, core = places()
    yn, yp, yo = (y + 1) % 4, (y + 3) % 4, (y + 2) % 4
    zn, zp, zo = (z + 1) % 4, (z + 3) % 4, (z + 2) % 4
    y_next, y_prev = at_place(yn, x_lo, z, x_hi, core), at_place(yp, x_lo, z, x_hi, core)
    y_far = at_place(yo, x_lo, z, x_hi, core)
    z_next, z_prev = at_place(y, x_lo, zn, x_hi, core), at_place(y, x_lo, zp, x_hi, core)
    across = at_place(y, 1 - x_lo, z, 1 - x_hi, core)
    beside = at_place(y, 1 - x_lo, z, x_hi, core)
    twin = at_place(y, x_lo, z, x_hi, 1 - core)
    greet((y_next, y_prev, y_far, z_next, z_prev, across, beside, twin))

    def copy(c, slot, source, target, device):
        return pltpu.make_async_remote_copy(
            src_ref=source, dst_ref=target, send_sem=send.at[c, slot], recv_sem=recv.at[c, slot],
            device_id=device, device_id_type=pl.DeviceIdType.MESH,
        )

    started = []

    def go(c, slot, source, target, device):
        item = copy(c, slot, source, target, device)
        item.start()
        started.append(item)
        return item

    def lanes(c):
        return pl.ds(chunks[c][1], chunks[c][2])

    first = [[None] * 16 for _ in range(n)]
    loads = []
    for c in range(n):
        acc, twin_buf = groups[c][0], groups[c][1]
        g = inputs[chunks[c][0]]
        first[c][0] = go(c, 0, g.at[:, :, 1 - core, :, :, lanes(c)], twin_buf, twin)
        load = pltpu.make_async_copy(g.at[:, :, core, :, :, lanes(c)], acc, local.at[c])
        load.start()
        loads.append(load)

    def add(target, source):
        target[...] = target[...] + source[...]

    def stage(c, step):
        acc, twin_buf, p1, m1, p2, m2, q1, r1, q2, r2 = groups[c][:10]
        kept = first[c]
        gathered = pieces[chunks[c][0]]
        y_first = c % 2 == 0
        if step == 0:
            loads[c].wait()
            kept[0].wait_recv()

            def body(i, carry):
                a, b, d = i // 8, (i // 4) % 2, i % 4
                add(acc.at[a, b, d], twin_buf.at[a, b, d])
                return carry

            lax.fori_loop(0, 32, body, 0)
            if y_first:
                kept[1] = go(c, 1, acc.at[:, 0, yo], p1, y_next)
                kept[2] = go(c, 2, acc.at[:, 1, yo], m1, y_prev)
            else:
                kept[1] = go(c, 1, acc.at[zo, 0], p1, z_next)
                kept[2] = go(c, 2, acc.at[zo, 1], m1, z_prev)
        elif step == 1:
            kept[1].wait_recv()
            kept[2].wait_recv()

            def body(i, carry):
                if y_first:
                    add(acc.at[i, 0, yn], p1.at[i])
                    add(acc.at[i, 1, yp], m1.at[i])
                else:
                    add(acc.at[zn, 0, i], p1.at[i])
                    add(acc.at[zp, 1, i], m1.at[i])
                return carry

            lax.fori_loop(0, 4, body, 0)
            if y_first:
                kept[3] = go(c, 3, acc.at[:, :, yn], p2, y_next)
                kept[4] = go(c, 4, acc.at[:, :, yp], m2, y_prev)
            else:
                kept[3] = go(c, 3, acc.at[zn], p2, z_next)
                kept[4] = go(c, 4, acc.at[zp], m2, z_prev)
        elif step == 2:
            kept[3].wait_recv()
            kept[4].wait_recv()

            def body(i, carry):
                if y_first:
                    a, b = i // 2, i % 2
                    add(acc.at[a, b, y], p2.at[a, b])
                    add(acc.at[a, b, y], m2.at[a, b])
                else:
                    a, b = i // 4, i % 4
                    add(acc.at[z, a, b], p2.at[a, b])
                    add(acc.at[z, a, b], m2.at[a, b])
                return carry

            lax.fori_loop(0, 8, body, 0)
            if y_first:
                kept[5] = go(c, 5, acc.at[zo, 0, y], q1, z_next)
                kept[6] = go(c, 6, acc.at[zo, 1, y], r1, z_prev)
            else:
                kept[5] = go(c, 5, acc.at[z, 0, yo], q1, y_next)
                kept[6] = go(c, 6, acc.at[z, 1, yo], r1, y_prev)
        elif step == 3:
            kept[5].wait_recv()
            kept[6].wait_recv()
            if y_first:
                add(acc.at[zn, 0, y], q1)
                add(acc.at[zp, 1, y], r1)
                kept[7] = go(c, 7, acc.at[zn, :, y], q2, z_next)
                kept[8] = go(c, 8, acc.at[zp, :, y], r2, z_prev)
            else:
                add(acc.at[z, 0, yn], q1)
                add(acc.at[z, 1, yp], r1)
                kept[7] = go(c, 7, acc.at[z, :, yn], q2, y_next)
                kept[8] = go(c, 8, acc.at[z, :, yp], r2, y_prev)
        elif step == 4:
            kept[7].wait_recv()
            kept[8].wait_recv()
            for b in range(2):
                add(acc.at[z, b, y], q2.at[b])
                add(acc.at[z, b, y], r2.at[b])
            kept[9] = go(c, 9, acc.at[z, 1 - x_hi, y], gathered.at[4, :, lanes(c)], across)
        elif step == 5:
            kept[9].wait_recv()
            acc[z, x_hi, y] = acc[z, x_hi, y] + gathered[4, :, lanes(c)]
            kept[10] = go(c, 10, acc.at[z, x_hi, y], gathered.at[5, :, lanes(c)], beside)
        elif step == 6:
            kept[10].wait_recv()
            gathered[y, :, lanes(c)] = acc[z, x_hi, y] + gathered[5, :, lanes(c)]
            mine = gathered.at[y, :, lanes(c)]
            kept[11] = go(c, 11, mine, mine, y_next)
            kept[12] = go(c, 12, mine, mine, y_prev)
            kept[13] = go(c, 13, mine, mine, y_far)
        else:
            for slot in (11, 12, 13):
                kept[slot].wait_recv()

    for turn in range(n // 2 + 7):
        for c in reversed(range(n)):
            if 0 <= turn - c // 2 < 8:
                stage(c, turn - c // 2)
    mixer, attn, vector, gateup, mixed, attended, down = outs
    for i in range(4):
        mixer[i, :, : D_SSM + XBC] = pieces[0][i, :, : D_SSM + XBC].astype(F32)
        mixer[i, :, D_SSM + XBC :] = pieces[0][i, :, 4096:4120].astype(F32)
        attn[i] = pieces[0][i, :, 3328:4096].astype(F32)
        vector[i] = pieces[0][i, :, 4096:].astype(F32)
        gateup[i] = pieces[1][i].astype(F32)
        if i < 3:
            mixed[i] = pieces[2][i].astype(F32)
        else:
            attended[0] = pieces[2][i].astype(F32)
        down[i] = pieces[3][i].astype(F32)
    for item in started:
        item.wait_send()


def reduce_all(values, chunks):
    shapes = [(value.shape[0] // 64, value.shape[1]) for value in values]
    scratch = []
    for c, (which, _, w) in enumerate(chunks):
        r = shapes[which][0]
        scratch += [pltpu.VMEM((4, 2, 4, r, w), BF)] * 2 + [pltpu.VMEM((4, r, w), BF)] * 2
        scratch += [pltpu.VMEM((4, 2, r, w) if c % 2 == 0 else (2, 4, r, w), BF)] * 2
        scratch += [pltpu.VMEM((r, w), BF)] * 2 + [pltpu.VMEM((2, r, w), BF)] * 2
    n = len(chunks)
    scratch += [pltpu.VMEM((6,) + shape, BF) for shape in shapes]
    scratch += [pltpu.SemaphoreType.DMA((n, 14)), pltpu.SemaphoreType.DMA((n, 14)), pltpu.SemaphoreType.DMA((n,))]
    outs = [(4, 16, CIN), (4, 16, 768), (4, 16, 128), (4, 16, 2 * FF), (3, 32, 1024), (1, 32, 1024), (4, 32, 1024)]
    outs = pl.pallas_call(
        functools.partial(reduce_kernel, chunks),
        out_shape=[jax.ShapeDtypeStruct(shape, F32) for shape in outs],
        in_specs=[pl.BlockSpec(memory_space=pl.ANY)] * len(values),
        out_specs=[pl.BlockSpec(memory_space=pltpu.VMEM)] * len(outs),
        scratch_shapes=scratch,
        compiler_params=pltpu.CompilerParams(
            collective_id=1, has_side_effects=True, vmem_limit_bytes=60 << 20
        ),
        cost_estimate=pl.CostEstimate(flops=10**8, bytes_accessed=10**8, transcendentals=0),
    )(*[value.reshape((4, 2, 2, 4) + shape) for value, shape in zip(values, shapes)])
    return [out.reshape(-1, out.shape[2]) for out in outs]


REDUCED = (
    (2, 0, 1024), (3, 0, 1024), (1, 0, 1408), (1, 1408, 1408), (1, 2816, 1280), (0, 0, 1408), (0, 1408, 1408),
    (0, 2816, 1408),
)


def seq_group(s, send, recv):
    group = [{"seq": (s + d) % 8} for d in range(1, 8)]
    started = []

    def make(slot, d, source, target):
        return pltpu.make_async_remote_copy(
            src_ref=source, dst_ref=target, send_sem=send.at[slot, d % 8], recv_sem=recv.at[slot, d % 8],
            device_id={"seq": (s + d) % 8}, device_id_type=pl.DeviceIdType.MESH,
        )

    def go(slot, d, source, target):
        item = make(slot, d, source, target)
        item.start()
        started.append(item)
        return item

    return group, started, make, go


def fade_of(ends, c, head):
    lane = lax.broadcasted_iota(jnp.int32, (1, 128), 1)
    row = ends[c][7:8, :]
    return jnp.exp(jnp.sum(jnp.where(lane == head, row, 0.0), axis=1, keepdims=True))


def share_forward(fresh, last, kv, starts_out, kv_out, ends_out, got, made, back, kv_all, ends, send, recv):
    s = lax.axis_index("seq")
    group, started, make, go = seq_group(s, send, recv)
    kv_all[...] = jnp.zeros_like(kv_all)
    greet(group)
    waits = [[], [], [], []]
    for d in range(1, 8):
        waits[0].append(go(0, d, fresh.at[(s + d) % 8], got.at[s]))
        waits[1].append(go(1, d, last, ends.at[s]))
    for d in range(1, 8):
        item = make(2, d, kv, kv_all.at[s])
        waits[2].append(item)
        pl.when(s + d < 8)(item.start)
    got[s] = fresh[s]
    ends[s] = last[...]
    kv_all[s] = kv[...]
    for item in waits[0] + waits[1]:
        item.wait_recv()
    heads = fresh.shape[1] // AP
    for k in range(heads):
        rows = slice(k * AP, k * AP + AP)
        running = jnp.zeros((AP, NST), F32)
        for c in range(8):
            made[c, rows, :] = running.astype(BF)
            if c < 7:
                running = running * fade_of(ends, c, s * heads + k) + got[c, rows, :].astype(F32)
    for d in range(1, 8):
        waits[3].append(go(3, d, made.at[(s + d) % 8], back.at[s]))
    back[s] = made[s]
    for item in waits[3]:
        item.wait_recv()
    for d in range(1, 8):
        pl.when(s - d >= 0)(waits[2][d - 1].wait_recv)
        pl.when(s + d < 8)(waits[2][d - 1].wait_send)
    starts_out[...] = back[...]
    kv_out[...] = kv_all[...]
    ends_out[...] = ends[...]
    for item in started:
        item.wait_send()


def share_backward(dstart, ends, dkv, cosine, sine, dends_out, dkv_out, got, made, back, kv_all, send, recv):
    s = lax.axis_index("seq")
    group, started, make, go = seq_group(s, send, recv)
    kv_all[...] = jnp.zeros_like(kv_all)
    greet(group)
    waits = [[], [], []]
    for d in range(1, 8):
        waits[0].append(go(0, d, dstart.at[(s + d) % 8], got.at[s]))
    for d in range(1, 8):
        item = make(1, 8 - d, dkv.at[(s - d + 8) % 8], kv_all.at[s])
        waits[1].append(item)
        pl.when(s - d >= 0)(item.start)
    got[s] = dstart[s]
    kv_all[s] = dkv[s]
    for item in waits[0]:
        item.wait_recv()
    heads = dstart.shape[1] // AP
    for k in range(heads):
        rows = slice(k * AP, k * AP + AP)
        running = jnp.zeros((AP, NST), F32)
        for c in range(7, -1, -1):
            made[c, rows, :] = running.astype(BF)
            if c > 0:
                running = running * fade_of(ends, c, s * heads + k) + got[c, rows, :].astype(F32)
    for d in range(1, 8):
        waits[2].append(go(2, d, made.at[(s + d) % 8], back.at[s]))
    back[s] = made[s]
    for d in range(1, 8):
        pl.when(s + d < 8)(waits[1][d - 1].wait_recv)
        pl.when(s - d >= 0)(waits[1][d - 1].wait_send)
    total = kv_all[0].astype(F32)
    for c in range(1, 8):
        total = total + kv_all[c].astype(F32)
    turned = total[:, 0:128] * cosine[...] - swap_halves(total[:, 0:128]) * sine[...]
    dkv_out[:, 0:128] = turned.astype(BF)
    dkv_out[:, 128:256] = total[:, 128:256].astype(BF)
    for item in waits[2]:
        item.wait_recv()
    dends_out[...] = back[...]
    for item in started:
        item.wait_send()


def share_call(kernel, collective, outs, scratch, slots, *args):
    spec = pl.BlockSpec(memory_space=pltpu.VMEM)
    return pl.pallas_call(
        kernel,
        out_shape=[jax.ShapeDtypeStruct(shape, dtype) for shape, dtype in outs],
        in_specs=[spec] * len(args),
        out_specs=[spec] * len(outs),
        scratch_shapes=[pltpu.VMEM(shape, dtype) for shape, dtype in scratch]
        + [pltpu.SemaphoreType.DMA((slots, 8))] * 2,
        compiler_params=pltpu.CompilerParams(
            collective_id=collective, has_side_effects=True, vmem_limit_bytes=24 << 20
        ),
        cost_estimate=pl.CostEstimate(flops=10**7, bytes_accessed=10**7, transcendentals=0),
    )(*args)


def gather_kernel(own, out, send, recv, local):
    n = len(WIDTHS)
    y, x_lo, z, x_hi, core = places()
    yn, yp, yo = (y + 1) % 4, (y + 3) % 4, (y + 2) % 4
    zn, zp, zo = (z + 1) % 4, (z + 3) % 4, (z + 2) % 4
    y_next, y_prev = at_place(yn, x_lo, z, x_hi, core), at_place(yp, x_lo, z, x_hi, core)
    z_next, z_prev = at_place(y, x_lo, zn, x_hi, core), at_place(y, x_lo, zp, x_hi, core)
    across = at_place(y, 1 - x_lo, z, 1 - x_hi, core)
    twin = at_place(y, x_lo, z, x_hi, 1 - core)
    greet((y_next, y_prev, z_next, z_prev, across, twin))
    started = []

    def lanes(c):
        return pl.ds(sum(WIDTHS[:c]), WIDTHS[c])

    def go(c, slot, source, target, device):
        item = pltpu.make_async_remote_copy(
            src_ref=source, dst_ref=target, send_sem=send.at[c, slot], recv_sem=recv.at[c, slot],
            device_id=device, device_id_type=pl.DeviceIdType.MESH,
        )
        item.start()
        started.append(item)
        return item

    held = [[None] * 10 for _ in range(n)]
    loads = []

    def stage(c, step):
        kept = held[c]
        cols = lanes(c)
        split = c % 2 == 0
        rows = pl.ds(y, 1) if split else pl.ds(0, 4)

        def part(a, b, d):
            return out.at[a, b, core, d, :, cols]

        def pass_on(slot, source, device):
            kept[slot] = go(c, slot, source, source, device)

        if step == 0:
            kept[0] = go(c, 0, own.at[rows, :, cols], part(z, x_hi, rows), across)
            load = pltpu.make_async_copy(own.at[rows, :, cols], part(z, x_hi, rows), local.at[c])
            load.start()
            loads.append(load)
        elif step == 1:
            loads[c].wait()
            kept[0].wait_recv()
            pass_on(1, part(z, slice(None), rows), z_next)
            pass_on(2, part(z, slice(None), rows), z_prev)
        elif step == 2:
            kept[1].wait_recv()
            kept[2].wait_recv()
            pass_on(3, part(zp, 0, rows), z_next)
            pass_on(4, part(zn, 1, rows), z_prev)
        elif step == 3:
            kept[3].wait_recv()
            kept[4].wait_recv()
            if split:
                pass_on(5, part(slice(None), slice(None), rows), y_next)
                pass_on(6, part(slice(None), slice(None), rows), y_prev)
            else:
                pass_on(9, part(slice(None), slice(None), rows), twin)
        elif step == 4 and split:
            kept[5].wait_recv()
            kept[6].wait_recv()
            pass_on(7, part(slice(None), 0, pl.ds(yp, 1)), y_next)
            pass_on(8, part(slice(None), 1, pl.ds(yn, 1)), y_prev)
        elif step == 5 and split:
            kept[7].wait_recv()
            kept[8].wait_recv()
            pass_on(9, part(slice(None), slice(None), slice(None)), twin)
        elif step == 6:
            kept[9].wait_recv()

    for step in range(7):
        for c in range(n):
            stage(c, step)
    for item in started:
        item.wait_send()


def gather_all(own):
    cols = own.shape[1]
    n = len(WIDTHS)
    out = pl.pallas_call(
        gather_kernel,
        out_shape=jax.ShapeDtypeStruct((4, 2, 2, 4, 16, cols), BF),
        in_specs=[pl.BlockSpec(memory_space=pl.ANY)],
        out_specs=pl.BlockSpec(memory_space=pl.ANY),
        scratch_shapes=[
            pltpu.SemaphoreType.DMA((n, 10)), pltpu.SemaphoreType.DMA((n, 10)), pltpu.SemaphoreType.DMA((n,))
        ],
        compiler_params=pltpu.CompilerParams(collective_id=2, has_side_effects=True),
        cost_estimate=pl.CostEstimate(flops=10**8, bytes_accessed=10**8, transcendentals=0),
    )(own.reshape(4, 16, cols))
    return out.reshape(1024, cols)


def rope_parts(length, start):
    half = AP // 2
    inverse = THETA ** (-2.0 * jnp.arange(half).astype(F32) / AP)
    angles = (start + jnp.arange(length)).astype(F32)[:, None] * inverse[None, :]
    cosine = jnp.cos(angles)
    sine = jnp.sin(angles)
    return jnp.concatenate([cosine] * 4, axis=1), jnp.concatenate([-sine, sine] * 2, axis=1)


def pad_lanes(value):
    return jnp.pad(value.astype(F32), (0, 128 - value.shape[0]))[None, :]


def per_device(
    seqs, hidden_in, norm_gain, mixer_proj, attn_proj, conv_kernel, conv_bias, step_bias, decay_log,
    skip_gain, gated_gain, mixer_out, attn_out, ffn_gain, gate_up, down_proj, out_grad,
):
    T = hidden_in.shape[1]
    width = norm_gain.shape[0]
    shards = 1024 // width
    me = lax.axis_index("seq")
    mix_rows, att_rows, down_rows = mixer_out.shape[0], attn_out.shape[0], down_proj.shape[0]

    small = jnp.concatenate(
        [norm_gain, ffn_gain, gated_gain, conv_bias, conv_kernel.T.reshape(-1)]
    )
    slots = width * 104
    small = jnp.pad(small, (0, slots - small.shape[0])).reshape(width, 104)
    front_shard = jnp.concatenate(
        [mixer_proj[:, : D_SSM + XBC], attn_proj, mixer_proj[:, D_SSM + XBC :], small], axis=1
    )
    front = gather_all(front_shard)
    tail_shard = jnp.concatenate(
        [
            gate_up[:, :FF],
            gate_up[:, FF:],
            jnp.concatenate([jnp.concatenate([mixer_out, attn_out], axis=0), down_proj], axis=1),
        ],
        axis=0,
    )
    tail = lax.all_gather(tail_shard, "fsdp", axis=0, tiled=False)
    smalls = front.reshape(shards, width, FRONT)[:, :, 4120:].reshape(shards, slots)
    cuts = []
    at = 0
    for size in (width, width, gated_gain.shape[0], conv_bias.shape[0]):
        cuts.append(smalls[:, at : at + size].reshape(1, -1).astype(F32))
        at += size
    gain_one, gain_ffn, gain_gated, bias_all = cuts
    kernel_size = conv_kernel.shape[0]
    taps = smalls[:, at : at + 4 * kernel_size].reshape(shards, 4, kernel_size)
    taps = taps.transpose(1, 0, 2).reshape(4, XBC).astype(F32)
    taps = jnp.pad(taps, ((0, 4), (0, 0)))

    resid = hidden_in[0].astype(F32)
    scale_one = rms_scale(resid)
    normed_one = resid * scale_one
    normed_in = (normed_one * gain_one).astype(BF)
    projection = dot(normed_in, front)
    gate_pre = projection[:, :D_SSM]
    cosine, sine = rope_parts(T, me * T)
    edge = projection[T - 8 :, D_SSM : D_SSM + XBC].astype(BF)
    halo = lax.ppermute(edge, "seq", [(i, i + 1) for i in range(seqs - 1)])
    sbias, dlog, skip = pad_lanes(step_bias), pad_lanes(decay_log), pad_lanes(skip_gain)
    act, dt, cum, fresh, xbc, steps, query_rot, kv_own = call(
        mamba_first,
        [
            ((T, XBC), F32), ((T, 128), F32), ((T, 128), F32), ((D_SSM, NST), BF), ((T, XBC), BF),
            ((T, 128), BF), ((T, QH * AP), BF), ((T, 2 * KVH * AP), BF),
        ],
        projection, halo, cosine, sine, taps, bias_all, sbias, dlog,
        scratch=[pltpu.VMEM((T + 8, XBC), F32)],
    )
    heads = MH // seqs
    states = ((seqs, heads * AP, NST), BF)
    pairs = ((seqs, T, 2 * KVH * AP), BF)
    tails = ((seqs, 8, 128), F32)
    starts, kv_all, ends = share_call(
        share_forward, 3, [states, pairs, tails], [states, states, states, pairs, tails], 4,
        fresh.reshape(states[0]), cum[T - 8 :], kv_own,
    )
    starts = starts.reshape(D_SSM, NST)
    kv_all = kv_all.reshape(seqs * T, 2 * KVH * AP)
    attn_tok, lse = call(
        functools.partial(attend_forward, "seq"),
        [((T, QH * AP), BF), ((QH, T), F32)],
        query_rot, kv_all,
        scratch=[pltpu.VMEM((QH * AP, T), F32), pltpu.VMEM((QH, T), F32), pltpu.VMEM((QH, T), F32)],
    )
    (mixed_y,) = call(mamba_second, [((T, D_SSM), BF)], act, dt, cum, starts, skip)

    proj_gate = tail[:, :width].reshape(-1, FF)
    proj_up = tail[:, width : 2 * width].reshape(-1, FF)
    low_rows = 2 * width
    out_mixer = tail[:, low_rows : low_rows + mix_rows, :1024].reshape(-1, 1024)
    out_attn = tail[:, low_rows + mix_rows :, :1024].reshape(-1, 1024)
    proj_down = tail[:, low_rows:, 1024:].reshape(-1, 1024)
    mixed = mixed_y.astype(F32)
    gated = mixed * jax.nn.silu(gate_pre)
    scale_two = rms_scale(gated)
    normed_two = gated * scale_two
    normed_mix = (normed_two * gain_gated).astype(BF)
    middle = resid + dot(normed_mix, out_mixer) + dot(attn_tok, out_attn)
    scale_three = rms_scale(middle)
    normed_three = middle * scale_three
    normed_ffn = (normed_three * gain_ffn).astype(BF)
    gate_half = dot(normed_ffn, proj_gate)
    up_half = dot(normed_ffn, proj_up)
    activ = (jax.nn.silu(gate_half) * up_half).astype(BF)
    block_out = (middle + dot(activ, proj_down)).astype(BF)

    ograd = out_grad[0]
    grad_activ = dot(ograd, proj_down, NT)
    grad_down = dot(activ, ograd, TN).astype(BF)
    grad_g = (grad_activ * up_half * silu_slope(gate_half)).astype(BF)
    grad_u = (grad_activ * jax.nn.silu(gate_half)).astype(BF)
    grad_gateup = dot(normed_ffn, jnp.concatenate([grad_g, grad_u], axis=1), TN).astype(BF)
    grad_nffn = dot(grad_g, proj_gate, NT) + dot(grad_u, proj_up, NT)
    grad_ffn = jnp.sum(grad_nffn * normed_three, axis=0)
    grad_middle = ograd.astype(F32) + rms_back(grad_nffn * gain_ffn, normed_three, scale_three)
    middle_bf = grad_middle.astype(BF)
    grad_mixed = dot(normed_mix, middle_bf, TN).astype(BF)
    grad_attended = dot(attn_tok, middle_bf, TN).astype(BF)
    grad_nmix = dot(middle_bf, out_mixer, NT)
    grad_otok = dot(middle_bf, out_attn, NT).astype(BF)
    grad_gated = jnp.sum(grad_nmix * normed_two, axis=0)
    grad_gz = rms_back(grad_nmix * gain_gated, normed_two, scale_two)
    grad_ymix = (grad_gz * jax.nn.silu(gate_pre)).astype(BF)
    grad_gate = (grad_gz * mixed * silu_slope(gate_pre)).astype(BF)
    grad_outs = jnp.concatenate(
        [grad_mixed.reshape(shards, mix_rows, 1024), grad_attended.reshape(shards, att_rows, 1024)], axis=1
    ).reshape(-1, 1024)

    (dstart,) = call(mamba_back_first, [((D_SSM, NST), BF)], grad_ymix, act, cum)
    qgrad, dkv = call(
        functools.partial(attend_backward, "seq"),
        [((T, QH * AP), BF), ((kv_all.shape[0], 2 * KVH * AP), BF)],
        query_rot, kv_all, attn_tok, lse, grad_otok, cosine, sine,
        scratch=[pltpu.VMEM((T, QH * AP), F32)],
    )
    dends, dkv = share_call(
        share_backward, 4, [states, ((T, 2 * KVH * AP), BF)], [states, states, states, pairs], 3,
        dstart.reshape(states[0]), ends, dkv.reshape(pairs[0]), cosine, sine,
    )
    dends = dends.reshape(D_SSM, NST)
    dconv, dtaps, dbias, dsteps, dhead = call(
        mamba_back_second,
        [((T, XBC), F32), ((8, XBC), F32), ((8, XBC), F32), ((T, 128), BF), ((8, 128), F32)],
        grad_ymix, xbc, halo, act, dt, cum, starts, dends, steps, taps, bias_all, sbias, dlog, skip,
        scratch=[pltpu.VMEM((T + 8, XBC), F32), pltpu.VMEM((T, XBC), F32)],
        limit=32,
    )
    ahead = lax.ppermute(dconv[:8].astype(BF), "seq", [(i + 1, i) for i in range(seqs - 1)])
    (grad_proj,) = call(
        finish_grads, [((T, FRONT), BF)], dconv, ahead, taps, grad_gate, qgrad, dkv, dsteps,
        scratch=[pltpu.VMEM((T + 8, XBC), F32)],
    )

    grad_front = dot(normed_in, grad_proj, TN).astype(BF)
    grad_nin = dot(grad_proj, front, NT)
    grad_norm = jnp.sum(grad_nin * normed_one, axis=0)
    input_grad = grad_middle + rms_back(grad_nin * gain_one, normed_one, scale_one)
    vectors = [grad_norm, grad_ffn, grad_gated, dbias[0]] + [dtaps[lag] for lag in range(4)]
    vectors = [value.reshape(shards, -1) for value in vectors]
    vectors.append(jnp.broadcast_to(dhead[:3, :MH].reshape(1, 3 * MH), (shards, 3 * MH)))
    vectors = jnp.concatenate(vectors, axis=1)
    vectors = jnp.pad(vectors, ((0, 0), (0, slots - vectors.shape[1]))).astype(BF)
    last = jnp.concatenate([grad_front[:, 4096:4120], vectors.reshape(-1, 104)], axis=1)
    mixer_sum, attn_sum, vectors, gateup_sum, mixed_sum, attended_sum, down_sum = reduce_all(
        [lax.dynamic_update_slice(grad_front, last, (0, 4096)), grad_gateup, grad_outs, grad_down], REDUCED
    )
    vectors = vectors[:, 24:].reshape(-1)
    owned = []
    at = 0
    for size in [width, width, gated_gain.shape[0], kernel_size] + [kernel_size] * 4 + [MH] * 3:
        owned.append(vectors[at : at + size])
        at += size
    own_taps = jnp.stack(owned[4:8], axis=1)
    return (
        block_out[None],
        input_grad[None],
        owned[0],
        mixer_sum,
        attn_sum,
        own_taps,
        owned[3],
        owned[8],
        owned[9],
        owned[10],
        owned[2],
        mixed_sum,
        attended_sum,
        owned[1],
        gateup_sum,
        down_sum,
    )


def solution(mesh):
    tokens = P("fsdp", "seq", None)
    vector = P("fsdp")
    matrix = P("fsdp", None)
    in_specs = (
        tokens, vector, matrix, matrix, matrix, vector, P(), P(), P(), vector, matrix, matrix, vector,
        matrix, matrix, tokens,
    )
    out_specs = (
        tokens, tokens, vector, matrix, matrix, matrix, vector, P(), P(), P(), vector, matrix, matrix,
        vector, matrix, matrix,
    )
    return jax.shard_map(
        functools.partial(per_device, mesh.shape["seq"]),
        mesh=mesh, in_specs=in_specs, out_specs=out_specs, check_vma=False,
    )
```

```python
import functools
import math

import jax
import jax.numpy as jnp
from jax import lax
from jax.experimental import pallas as pl
from jax.experimental.pallas import tpu as pltpu
from jax.sharding import PartitionSpec as P

MH = 24
NST = 128
QH = 8
KVH = 2
AP = 64
FF = 2048
D_SSM = 1536
XBC = 1792
CIN = 3352
FRONT = 4224
EPSILON = 1e-05
THETA = 10000.0
HIGHEST = lax.Precision.HIGHEST
F32 = jnp.float32
BF = jnp.bfloat16
NT = (((1,), (1,)), ((), ()))
TN = (((0,), (0,)), ((), ()))


def dot(a, b, dims=(((1,), (0,)), ((), ())), precision=None):
    return lax.dot_general(a, b, dims, preferred_element_type=F32, precision=precision)


def silu_slope(value):
    sigma = jax.nn.sigmoid(value)
    return sigma * (1.0 + value * (1.0 - sigma))


def rms_scale(value):
    return lax.rsqrt(jnp.mean(value * value, axis=1, keepdims=True) + EPSILON)


def rms_back(grad_normed, normed, scale):
    return scale * (grad_normed - normed * jnp.mean(grad_normed * normed, axis=1, keepdims=True))


def head_selector(rows, cols):
    channel = lax.broadcasted_iota(jnp.int32, (rows, cols), 0)
    head = lax.broadcasted_iota(jnp.int32, (rows, cols), 1)
    return jnp.where((channel >= head * AP) & (channel < head * AP + AP), 1.0, 0.0).astype(F32)


def spread_heads(value):
    head = lax.broadcasted_iota(jnp.int32, (128, D_SSM), 0)
    channel = lax.broadcasted_iota(jnp.int32, (128, D_SSM), 1)
    select = jnp.where((channel >= head * AP) & (channel < head * AP + AP), 1.0, 0.0).astype(F32)
    return dot(value, select, precision=HIGHEST)


def gather_heads(value):
    return dot(value, head_selector(D_SSM, 128), precision=HIGHEST)


def conv_pre(ext, taps, bias, length):
    result = bias[...] + taps[3:4, :] * ext[8 : 8 + length, :]
    for lag in range(3):
        result = result + taps[lag : lag + 1, :] * ext[pl.ds(5 + lag, length), :]
    return result


def swap_halves(value):
    lane = lax.broadcasted_iota(jnp.int32, value.shape, 1)
    return jnp.where(lane % AP < AP // 2, pltpu.roll(value, 96, 1), pltpu.roll(value, 32, 1))


def mamba_first(
    proj, halo, cosine, sine, taps, bias, sbias, dlog,
    act_ref, dt_ref, cum_ref, fresh_ref, xbc_ref, steps_ref, q_ref, kv_ref, ext,
):
    length = proj.shape[0]
    for pair in range(QH // 2 + 1):
        at = D_SSM + XBC + pair * 128
        value = proj[:, at : at + 128].astype(BF).astype(F32)
        value = (value * cosine[...] + swap_halves(value) * sine[...]).astype(BF)
        if pair < QH // 2:
            q_ref[:, pair * 128 : pair * 128 + 128] = value
        else:
            kv_ref[:, 0:128] = value
    kv_ref[:, 128:256] = proj[:, 3968:4096].astype(BF)
    xbc = proj[:, D_SSM : D_SSM + XBC].astype(BF)
    steps = proj[:, 4096:].astype(BF)
    xbc_ref[...] = xbc
    steps_ref[...] = steps
    ext[0:8, :] = halo[...].astype(F32)
    ext[8 : 8 + length, :] = xbc.astype(F32)
    conv = conv_pre(ext, taps, bias, length)
    act = conv * jax.nn.sigmoid(conv)
    act_ref[...] = act
    lane = lax.broadcasted_iota(jnp.int32, (length, 128), 1)
    raw = steps.astype(F32) + sbias[...]
    dt = jnp.maximum(raw, 0.0) + jnp.log1p(jnp.exp(-jnp.abs(raw)))
    dt = jnp.where(lane < MH, dt, 0.0)
    dt_ref[...] = dt
    row = lax.broadcasted_iota(jnp.int32, (length, length), 0)
    col = lax.broadcasted_iota(jnp.int32, (length, length), 1)
    lower = jnp.where(row >= col, 1.0, 0.0).astype(F32)
    cum = dot(lower, dt * (-jnp.exp(dlog[...])), precision=HIGHEST)
    cum_ref[...] = cum
    weight = spread_heads(jnp.exp(cum[length - 1 : length, :] - cum) * dt)
    scaled = (act[:, :D_SSM] * weight).astype(BF)
    fresh_ref[...] = dot(scaled, act[:, D_SSM : D_SSM + NST].astype(BF), TN).astype(BF)


def mamba_second(act, dt, cum, starts, skip, y_ref):
    length = act.shape[0]
    cumv = cum[...]
    cum_t = cumv.T
    bmat = act[:, D_SSM : D_SSM + NST].astype(BF)
    cmat = act[:, D_SSM + NST :].astype(BF)
    inner = dot(cmat, bmat, NT)
    row = lax.broadcasted_iota(jnp.int32, (length, length), 0)
    col = lax.broadcasted_iota(jnp.int32, (length, length), 1)
    inner = jnp.where(row >= col, inner, 0.0)
    x = act[:, :D_SSM]
    scaled = (x * spread_heads(dt[...])).astype(BF)
    outer = dot(cmat, starts[...], NT) * spread_heads(jnp.exp(cumv))
    base = outer + spread_heads(skip[...]) * x
    for pair in range(MH // 2):
        parts = []
        for h in (2 * pair, 2 * pair + 1):
            fade = jnp.exp(jnp.minimum(cumv[:, h : h + 1] - cum_t[h : h + 1, :], 0.0))
            parts.append(dot((inner * fade).astype(BF), scaled[:, h * AP : h * AP + AP]))
        lanes = slice(pair * 128, pair * 128 + 128)
        y_ref[:, lanes] = (base[:, lanes] + jnp.concatenate(parts, axis=1)).astype(BF)


def mamba_back_first(gy, act, cum, dstart_ref):
    rise = spread_heads(jnp.exp(cum[...]))
    cmat = act[:, D_SSM + NST :].astype(BF)
    dstart_ref[...] = dot((gy[...].astype(F32) * rise).astype(BF), cmat, TN).astype(BF)


def mamba_back_second(
    gy, xbc, halo, act, dt, cum, starts, dends, steps, taps, bias, sbias, dlog, skip,
    dconv_ref, dtaps_ref, dbias_ref, dsteps_ref, dhead_ref, ext, dact,
):
    length = act.shape[0]
    cumv = cum[...]
    dtv = dt[...]
    cum_t = cumv.T
    lane = lax.broadcasted_iota(jnp.int32, (length, 128), 1)
    bmat = act[:, D_SSM : D_SSM + NST].astype(BF)
    cmat = act[:, D_SSM + NST :].astype(BF)
    row = lax.broadcasted_iota(jnp.int32, (length, length), 0)
    col = lax.broadcasted_iota(jnp.int32, (length, length), 1)
    inner_t = jnp.where(col >= row, dot(bmat, cmat, NT), 0.0)
    x = act[:, :D_SSM]
    gyb = gy[...]
    gyf = gyb.astype(F32)
    dt_full = spread_heads(dtv)
    tail = spread_heads(jnp.exp(cumv[length - 1 : length, :] - cumv))
    rise = spread_heads(jnp.exp(cumv))
    xs = x * dt_full
    xsb = xs.astype(BF)
    ginner = jnp.zeros((length, length), F32)
    qcols = jnp.zeros((length, 128), F32)
    rrows = []
    for pair in range(MH // 2):
        parts = []
        for h in (2 * pair, 2 * pair + 1):
            lanes = slice(h * AP, h * AP + AP)
            fade = jnp.exp(jnp.minimum(cum_t[h : h + 1, :] - cumv[:, h : h + 1], 0.0))
            graded = dot(xsb[:, lanes], gyb[:, lanes], NT) * fade
            ginner = ginner + graded
            weighed = graded * inner_t
            rrows.append(jnp.sum(weighed, axis=0, keepdims=True))
            qcols = jnp.where(lane == h, jnp.sum(weighed, axis=1, keepdims=True), qcols)
            parts.append(dot((inner_t * fade).astype(BF), gyb[:, lanes]))
        dact[:, pair * 128 : pair * 128 + 128] = jnp.concatenate(parts, axis=1)
    ginner = jnp.where(col >= row, ginner, 0.0).astype(BF)
    rrows = jnp.concatenate(rrows + [jnp.zeros((128 - MH, length), F32)], axis=0).T
    endb = dends[...]
    startb = starts[...]
    from_end = dot(bmat, endb, NT) * tail
    dxs = dact[:, :D_SSM] + from_end
    reach = gather_heads(xs * from_end)
    outer = dot(cmat, startb, NT) * rise
    dcum = rrows - qcols + gather_heads(gyf * outer) - reach
    total = jnp.exp(cumv[length - 1 : length, :])
    carried = gather_heads_rows(startb, endb) * total + jnp.sum(reach, axis=0, keepdims=True)
    last = lax.broadcasted_iota(jnp.int32, (length, 128), 0) == length - 1
    dcum = dcum + jnp.where(last, carried, 0.0)
    upper = jnp.where(col >= row, 1.0, 0.0).astype(F32)
    rest = dot(upper, dcum, precision=HIGHEST)
    decay = -jnp.exp(dlog[...])
    ddt = gather_heads(x * dxs) + decay * rest
    ddecay = jnp.sum(dtv * rest, axis=0, keepdims=True) * decay
    raw = steps[...].astype(F32) + sbias[...]
    dsteps = jnp.where(lane < MH, ddt * jax.nn.sigmoid(raw), 0.0)
    dsteps_ref[...] = dsteps.astype(BF)
    dskip = gather_heads(jnp.sum(x * gyf, axis=0, keepdims=True))
    dhead_ref[0:1, :] = jnp.sum(dsteps, axis=0, keepdims=True)
    dhead_ref[1:2, :] = ddecay
    dhead_ref[2:3, :] = dskip
    dhead_ref[3:8, :] = jnp.zeros((5, 128), F32)
    dact[:, :D_SSM] = dt_full * dxs + spread_heads(skip[...]) * gyf
    dact[:, D_SSM : D_SSM + NST] = dot((xs * tail).astype(BF), endb) + dot(ginner, cmat)
    dact[:, D_SSM + NST :] = dot((gyf * rise).astype(BF), startb) + dot(ginner, bmat, TN)
    ext[0:8, :] = halo[...].astype(F32)
    ext[8 : 8 + length, :] = xbc[...].astype(F32)
    conv = conv_pre(ext, taps, bias, length)
    dconv = dact[...] * silu_slope(conv)
    dconv_ref[...] = dconv
    dbias_ref[...] = jnp.broadcast_to(jnp.sum(dconv, axis=0, keepdims=True), (8, XBC))
    for lag in range(4):
        dtaps_ref[lag : lag + 1, :] = jnp.sum(
            dconv * ext[pl.ds(5 + lag, length), :], axis=0, keepdims=True
        )
    dtaps_ref[4:8, :] = jnp.zeros((4, XBC), F32)


def gather_heads_rows(a, b):
    product = a.astype(F32) * b.astype(F32)
    per_row = dot(jnp.ones((8, NST), F32), product, NT, precision=HIGHEST)
    return gather_heads(per_row)[0:1, :]


def attend_block(q, kv, c, diagonal, acc, top, total):
    block = q.shape[0]
    scale = 1.0 / math.sqrt(AP)
    if diagonal:
        key_at = lax.broadcasted_iota(jnp.int32, (block, block), 0)
        allowed = key_at <= lax.broadcasted_iota(jnp.int32, (block, block), 1)
    for h in range(QH):
        g = h // (QH // KVH)
        keys = kv[c, :, g * AP : g * AP + AP]
        values = kv[c, :, KVH * AP + g * AP : KVH * AP + g * AP + AP]
        s = dot(keys, q[:, h * AP : h * AP + AP], NT) * scale
        band = slice(h * AP, h * AP + AP)
        if diagonal:
            s = jnp.where(allowed, s, -1e30)
            new = jnp.max(s, axis=0, keepdims=True)
            p = jnp.exp(s - new)
            total[h : h + 1, :] = jnp.sum(p, axis=0, keepdims=True)
            acc[band, :] = dot(values, p.astype(BF), TN)
        else:
            old = top[h : h + 1, :]
            new = jnp.maximum(old, jnp.max(s, axis=0, keepdims=True))
            p = jnp.exp(s - new)
            fix = jnp.exp(old - new)
            total[h : h + 1, :] = total[h : h + 1, :] * fix + jnp.sum(p, axis=0, keepdims=True)
            acc[band, :] = acc[band, :] * fix + dot(values, p.astype(BF), TN)
        top[h : h + 1, :] = new


def attend_back_block(q, kv, c, diagonal, lse, go, centre, dq_ref):
    block = q.shape[0]
    scale = 1.0 / math.sqrt(AP)
    if diagonal:
        key_at = lax.broadcasted_iota(jnp.int32, (block, block), 0)
        allowed = key_at <= lax.broadcasted_iota(jnp.int32, (block, block), 1)
    sums = []
    for g in range(KVH):
        keys = kv[c, :, g * AP : g * AP + AP]
        values = kv[c, :, KVH * AP + g * AP : KVH * AP + g * AP + AP]
        dk = jnp.zeros((block, AP), F32)
        dv = jnp.zeros((block, AP), F32)
        for h in range(g * (QH // KVH), (g + 1) * (QH // KVH)):
            band = slice(h * AP, h * AP + AP)
            qh = q[:, band]
            gh = go[:, band]
            s = dot(keys, qh, NT) * scale - lse[h : h + 1, :]
            p = jnp.exp(jnp.where(allowed, s, -1e30) if diagonal else s)
            dv = dv + dot(p.astype(BF), gh)
            dp = dot(values, gh, NT)
            ds = (p * (dp - centre[h : h + 1, :])).astype(BF)
            dk = dk + dot(ds, qh)
            part = dot(ds, keys, TN) * scale
            dq_ref[:, band] = part if diagonal else dq_ref[:, band] + part
        sums.append((dk * scale, dv))
    return (
        jnp.concatenate([sums[0][0], sums[1][0]], axis=1),
        jnp.concatenate([sums[0][1], sums[1][1]], axis=1),
    )


def finish_grads(dconv, ahead, taps, gate, dq, dkv, dsteps, out_ref, ext):
    length = dconv.shape[0]
    ext[0:length, :] = dconv[...]
    ext[length : length + 8, :] = ahead[...].astype(F32)
    du = taps[3:4, :] * ext[0:length, :]
    for lag in range(3):
        du = du + taps[lag : lag + 1, :] * ext[pl.ds(3 - lag, length), :]
    out_ref[:, :D_SSM] = gate[...]
    out_ref[:, D_SSM : D_SSM + XBC] = du.astype(BF)
    out_ref[:, 3328:3840] = dq[...]
    out_ref[:, 3840:4096] = dkv[...]
    out_ref[:, 4096:] = dsteps[...]


def call(kernel, outs, *args, scratch=(), limit=20):
    spec = pl.BlockSpec(memory_space=pltpu.VMEM)
    return pl.pallas_call(
        kernel,
        out_shape=[jax.ShapeDtypeStruct(shape, dtype) for shape, dtype in outs],
        in_specs=[spec] * len(args),
        out_specs=[spec] * len(outs),
        scratch_shapes=list(scratch),
        compiler_params=pltpu.CompilerParams(vmem_limit_bytes=limit << 20),
    )(*args)


def places():
    s, f = lax.axis_index("seq"), lax.axis_index("fsdp")
    return s // 2, s % 2, f // 4, (f // 2) % 2, f % 2


def at_place(y, x_lo, z, x_hi, core):
    return {"seq": y * 2 + x_lo, "fsdp": z * 4 + x_hi * 2 + core}


def greet(others):
    barrier = pltpu.get_barrier_semaphore()
    for other in others:
        pl.semaphore_signal(barrier, inc=1, device_id=other, device_id_type=pl.DeviceIdType.MESH)
    pl.semaphore_wait(barrier, len(others))


WIDTHS = (1024, 1024, 1024, 1152)


def reduce_kernel(chunks, *refs):
    n = len(chunks)
    count = max(chunk[0] for chunk in chunks) + 1
    inputs, outs, refs = refs[:count], refs[count : count + 7], refs[count + 7 :]
    groups = [refs[i * 10 : i * 10 + 10] for i in range(n)]
    refs = refs[n * 10 :]
    pieces, (send, recv, local) = refs[:count], refs[count:]
    y, x_lo, z, x_hi, core = places()
    yn, yp, yo = (y + 1) % 4, (y + 3) % 4, (y + 2) % 4
    zn, zp, zo = (z + 1) % 4, (z + 3) % 4, (z + 2) % 4
    y_next, y_prev = at_place(yn, x_lo, z, x_hi, core), at_place(yp, x_lo, z, x_hi, core)
    y_far = at_place(yo, x_lo, z, x_hi, core)
    z_next, z_prev = at_place(y, x_lo, zn, x_hi, core), at_place(y, x_lo, zp, x_hi, core)
    across = at_place(y, 1 - x_lo, z, 1 - x_hi, core)
    beside = at_place(y, 1 - x_lo, z, x_hi, core)
    twin = at_place(y, x_lo, z, x_hi, 1 - core)
    greet((y_next, y_prev, y_far, z_next, z_prev, across, beside, twin))

    def copy(c, slot, source, target, device):
        return pltpu.make_async_remote_copy(
            src_ref=source, dst_ref=target, send_sem=send.at[c, slot], recv_sem=recv.at[c, slot],
            device_id=device, device_id_type=pl.DeviceIdType.MESH,
        )

    started = []

    def go(c, slot, source, target, device):
        item = copy(c, slot, source, target, device)
        item.start()
        started.append(item)
        return item

    def lanes(c):
        return pl.ds(chunks[c][1], chunks[c][2])

    first = [[None] * 16 for _ in range(n)]
    loads = []
    for c in range(n):
        acc, twin_buf = groups[c][0], groups[c][1]
        g = inputs[chunks[c][0]]
        first[c][0] = go(c, 0, g.at[:, :, 1 - core, :, :, lanes(c)], twin_buf, twin)
        load = pltpu.make_async_copy(g.at[:, :, core, :, :, lanes(c)], acc, local.at[c])
        load.start()
        loads.append(load)

    def add(target, source):
        target[...] = target[...] + source[...]

    def stage(c, step):
        acc, twin_buf, p1, m1, p2, m2, q1, r1, q2, r2 = groups[c][:10]
        kept = first[c]
        gathered = pieces[chunks[c][0]]
        y_first = c % 2 == 0
        if step == 0:
            loads[c].wait()
            kept[0].wait_recv()

            def body(i, carry):
                a, b, d = i // 8, (i // 4) % 2, i % 4
                add(acc.at[a, b, d], twin_buf.at[a, b, d])
                return carry

            lax.fori_loop(0, 32, body, 0)
            if y_first:
                kept[1] = go(c, 1, acc.at[:, 0, yo], p1, y_next)
                kept[2] = go(c, 2, acc.at[:, 1, yo], m1, y_prev)
            else:
                kept[1] = go(c, 1, acc.at[zo, 0], p1, z_next)
                kept[2] = go(c, 2, acc.at[zo, 1], m1, z_prev)
        elif step == 1:
            kept[1].wait_recv()
            kept[2].wait_recv()

            def body(i, carry):
                if y_first:
                    add(acc.at[i, 0, yn], p1.at[i])
                    add(acc.at[i, 1, yp], m1.at[i])
                else:
                    add(acc.at[zn, 0, i], p1.at[i])
                    add(acc.at[zp, 1, i], m1.at[i])
                return carry

            lax.fori_loop(0, 4, body, 0)
            if y_first:
                kept[3] = go(c, 3, acc.at[:, :, yn], p2, y_next)
                kept[4] = go(c, 4, acc.at[:, :, yp], m2, y_prev)
            else:
                kept[3] = go(c, 3, acc.at[zn], p2, z_next)
                kept[4] = go(c, 4, acc.at[zp], m2, z_prev)
        elif step == 2:
            kept[3].wait_recv()
            kept[4].wait_recv()

            def body(i, carry):
                if y_first:
                    a, b = i // 2, i % 2
                    add(acc.at[a, b, y], p2.at[a, b])
                    add(acc.at[a, b, y], m2.at[a, b])
                else:
                    a, b = i // 4, i % 4
                    add(acc.at[z, a, b], p2.at[a, b])
                    add(acc.at[z, a, b], m2.at[a, b])
                return carry

            lax.fori_loop(0, 8, body, 0)
            if y_first:
                kept[5] = go(c, 5, acc.at[zo, 0, y], q1, z_next)
                kept[6] = go(c, 6, acc.at[zo, 1, y], r1, z_prev)
            else:
                kept[5] = go(c, 5, acc.at[z, 0, yo], q1, y_next)
                kept[6] = go(c, 6, acc.at[z, 1, yo], r1, y_prev)
        elif step == 3:
            kept[5].wait_recv()
            kept[6].wait_recv()
            if y_first:
                add(acc.at[zn, 0, y], q1)
                add(acc.at[zp, 1, y], r1)
                kept[7] = go(c, 7, acc.at[zn, :, y], q2, z_next)
                kept[8] = go(c, 8, acc.at[zp, :, y], r2, z_prev)
            else:
                add(acc.at[z, 0, yn], q1)
                add(acc.at[z, 1, yp], r1)
                kept[7] = go(c, 7, acc.at[z, :, yn], q2, y_next)
                kept[8] = go(c, 8, acc.at[z, :, yp], r2, y_prev)
        elif step == 4:
            kept[7].wait_recv()
            kept[8].wait_recv()
            for b in range(2):
                add(acc.at[z, b, y], q2.at[b])
                add(acc.at[z, b, y], r2.at[b])
            kept[9] = go(c, 9, acc.at[z, 1 - x_hi, y], gathered.at[4, :, lanes(c)], across)
        elif step == 5:
            kept[9].wait_recv()
            acc[z, x_hi, y] = acc[z, x_hi, y] + gathered[4, :, lanes(c)]
            kept[10] = go(c, 10, acc.at[z, x_hi, y], gathered.at[5, :, lanes(c)], beside)
        elif step == 6:
            kept[10].wait_recv()
            gathered[y, :, lanes(c)] = acc[z, x_hi, y] + gathered[5, :, lanes(c)]
            mine = gathered.at[y, :, lanes(c)]
            kept[11] = go(c, 11, mine, mine, y_next)
            kept[12] = go(c, 12, mine, mine, y_prev)
            kept[13] = go(c, 13, mine, mine, y_far)
        else:
            for slot in (11, 12, 13):
                kept[slot].wait_recv()

    for turn in range(n // 2 + 7):
        for c in reversed(range(n)):
            if 0 <= turn - c // 2 < 8:
                stage(c, turn - c // 2)
    mixer, attn, vector, gateup, mixed, attended, down = outs
    for i in range(4):
        mixer[i, :, : D_SSM + XBC] = pieces[0][i, :, : D_SSM + XBC].astype(F32)
        mixer[i, :, D_SSM + XBC :] = pieces[0][i, :, 4096:4120].astype(F32)
        attn[i] = pieces[0][i, :, 3328:4096].astype(F32)
        vector[i] = pieces[0][i, :, 4096:].astype(F32)
        gateup[i] = pieces[1][i].astype(F32)
        if i < 3:
            mixed[i] = pieces[2][i].astype(F32)
        else:
            attended[0] = pieces[2][i].astype(F32)
        down[i] = pieces[3][i].astype(F32)
    for item in started:
        item.wait_send()


def reduce_all(values, chunks):
    shapes = [(value.shape[0] // 64, value.shape[1]) for value in values]
    scratch = []
    for c, (which, _, w) in enumerate(chunks):
        r = shapes[which][0]
        scratch += [pltpu.VMEM((4, 2, 4, r, w), BF)] * 2 + [pltpu.VMEM((4, r, w), BF)] * 2
        scratch += [pltpu.VMEM((4, 2, r, w) if c % 2 == 0 else (2, 4, r, w), BF)] * 2
        scratch += [pltpu.VMEM((r, w), BF)] * 2 + [pltpu.VMEM((2, r, w), BF)] * 2
    n = len(chunks)
    scratch += [pltpu.VMEM((6,) + shape, BF) for shape in shapes]
    scratch += [pltpu.SemaphoreType.DMA((n, 14)), pltpu.SemaphoreType.DMA((n, 14)), pltpu.SemaphoreType.DMA((n,))]
    outs = [(4, 16, CIN), (4, 16, 768), (4, 16, 128), (4, 16, 2 * FF), (3, 32, 1024), (1, 32, 1024), (4, 32, 1024)]
    outs = pl.pallas_call(
        functools.partial(reduce_kernel, chunks),
        out_shape=[jax.ShapeDtypeStruct(shape, F32) for shape in outs],
        in_specs=[pl.BlockSpec(memory_space=pl.ANY)] * len(values),
        out_specs=[pl.BlockSpec(memory_space=pltpu.VMEM)] * len(outs),
        scratch_shapes=scratch,
        compiler_params=pltpu.CompilerParams(
            collective_id=1, has_side_effects=True, vmem_limit_bytes=60 << 20
        ),
        cost_estimate=pl.CostEstimate(flops=10**8, bytes_accessed=10**8, transcendentals=0),
    )(*[value.reshape((4, 2, 2, 4) + shape) for value, shape in zip(values, shapes)])
    return [out.reshape(-1, out.shape[2]) for out in outs]


REDUCED = (
    (2, 0, 1024), (3, 0, 1024), (1, 0, 1408), (1, 1408, 1408), (1, 2816, 1280), (0, 0, 1408), (0, 1408, 1408),
    (0, 2816, 1408),
)


def seq_group(s, send, recv):
    group = [{"seq": (s + d) % 8} for d in range(1, 8)]
    started = []

    def make(slot, d, source, target):
        return pltpu.make_async_remote_copy(
            src_ref=source, dst_ref=target, send_sem=send.at[slot, d % 8], recv_sem=recv.at[slot, d % 8],
            device_id={"seq": (s + d) % 8}, device_id_type=pl.DeviceIdType.MESH,
        )

    def go(slot, d, source, target):
        item = make(slot, d, source, target)
        item.start()
        started.append(item)
        return item

    return group, started, make, go


def fade_of(ends, c, head):
    lane = lax.broadcasted_iota(jnp.int32, (1, 128), 1)
    row = ends[c][7:8, :]
    return jnp.exp(jnp.sum(jnp.where(lane == head, row, 0.0), axis=1, keepdims=True))


def scan_states(ends, s, heads, got, made, order):
    for k in range(heads):
        rows = slice(k * AP, k * AP + AP)
        running = jnp.zeros((AP, NST), F32)
        for c in order:
            made[c, rows, :] = running.astype(BF)
            if c != order[-1]:
                running = running * fade_of(ends, c, s * heads + k) + got[c, rows, :].astype(F32)


def share_forward(
    fresh, last, kv, q, starts_out, kv_out, ends_out, o_ref, lse_ref,
    got, made, back, kv_all, ends, acc, top, total, send, recv,
):
    s = lax.axis_index("seq")
    group, started, make, go = seq_group(s, send, recv)
    kv_all[...] = jnp.zeros_like(kv_all)
    greet(group)
    waits = [[], []]
    for d in range(1, 8):
        waits[0].append(go(0, d, fresh.at[(s + d) % 8], got.at[s]))
        waits[0].append(go(1, d, last, ends.at[s]))
    for d in range(1, 8):
        pl.when(s + d < 8)(make(2, d, kv, kv_all.at[s]).start)
    got[s] = fresh[s]
    ends[s] = last[...]
    kv_all[s] = kv[...]
    attend_block(q, kv_all, s, True, acc, top, total)
    for item in waits[0]:
        item.wait_recv()
    scan_states(ends, s, fresh.shape[1] // AP, got, made, list(range(8)))
    for d in range(1, 8):
        waits[1].append(go(3, d, made.at[(s + d) % 8], back.at[s]))
    back[s] = made[s]

    def step(d, carry):
        make(2, d, kv, kv_all.at[s]).wait_recv()
        attend_block(q, kv_all, s - d, False, acc, top, total)
        return carry

    lax.fori_loop(1, s + 1, step, 0)
    lse_ref[...] = top[...] + jnp.log(total[...])
    for pair in range(QH // 2):
        parts = []
        for h in (2 * pair, 2 * pair + 1):
            parts.append(acc[h * AP : h * AP + AP, :] / total[h : h + 1, :])
        o_ref[:, pair * 128 : pair * 128 + 128] = jnp.concatenate(parts, axis=0).T.astype(BF)
    for item in waits[1]:
        item.wait_recv()
    starts_out[...] = back[...]
    kv_out[...] = kv_all[...]
    ends_out[...] = ends[...]
    for d in range(1, 8):
        pl.when(s + d < 8)(make(2, d, kv, kv_all.at[s]).wait_send)
    for item in started:
        item.wait_send()


def share_backward(
    dstart, ends, q, kv, o, lse, go_ref, cosine, sine, dends_out, dq_out, dkv_out,
    got, made, back, kv_got, kv_made, dq, send, recv,
):
    s = lax.axis_index("seq")
    group, started, make, go = seq_group(s, send, recv)
    kv_got[...] = jnp.zeros_like(kv_got)
    greet(group)
    waits = [[], []]
    for d in range(1, 8):
        waits[0].append(go(0, d, dstart.at[(s + d) % 8], got.at[s]))
    got[s] = dstart[s]
    pick_h = lax.broadcasted_iota(jnp.int32, (8, QH * AP), 0)
    pick_c = lax.broadcasted_iota(jnp.int32, (8, QH * AP), 1)
    pick = jnp.where((pick_c >= pick_h * AP) & (pick_c < pick_h * AP + AP), 1.0, 0.0).astype(F32)
    centre = dot(pick, go_ref[...].astype(F32) * o[...].astype(F32), NT, precision=HIGHEST)
    own_k, own_v = attend_back_block(q, kv, s, True, lse, go_ref, centre, dq)
    for item in waits[0]:
        item.wait_recv()
    scan_states(ends, s, dstart.shape[1] // AP, got, made, list(range(7, -1, -1)))
    for d in range(1, 8):
        waits[1].append(go(2, d, made.at[(s + d) % 8], back.at[s]))
    back[s] = made[s]

    def sent(d):
        return make(1, 8 - d, kv_made.at[s - d], kv_got.at[s])

    def step(d, carry):
        dk, dv = attend_back_block(q, kv, s - d, False, lse, go_ref, centre, dq)
        kv_made[s - d, :, 0:128] = dk.astype(BF)
        kv_made[s - d, :, 128:256] = dv.astype(BF)
        sent(d).start()
        return carry

    lax.fori_loop(1, s + 1, step, 0)
    for pair in range(QH // 2):
        value = dq[:, pair * 128 : pair * 128 + 128]
        value = value * cosine[...] - swap_halves(value) * sine[...]
        dq_out[:, pair * 128 : pair * 128 + 128] = value.astype(BF)
    for d in range(1, 8):
        pl.when(s + d < 8)(make(1, 8 - d, kv_made.at[0], kv_got.at[s]).wait_recv)
    for c in range(8):
        own_k = own_k + kv_got[c, :, 0:128].astype(F32)
        own_v = own_v + kv_got[c, :, 128:256].astype(F32)
    dkv_out[:, 0:128] = (own_k * cosine[...] - swap_halves(own_k) * sine[...]).astype(BF)
    dkv_out[:, 128:256] = own_v.astype(BF)
    for item in waits[1]:
        item.wait_recv()
    dends_out[...] = back[...]
    for d in range(1, 8):
        pl.when(s - d >= 0)(make(1, 8 - d, kv_made.at[0], kv_got.at[s]).wait_send)
    for item in started:
        item.wait_send()


def share_call(kernel, collective, outs, scratch, slots, *args):
    spec = pl.BlockSpec(memory_space=pltpu.VMEM)
    return pl.pallas_call(
        kernel,
        out_shape=[jax.ShapeDtypeStruct(shape, dtype) for shape, dtype in outs],
        in_specs=[spec] * len(args),
        out_specs=[spec] * len(outs),
        scratch_shapes=[pltpu.VMEM(shape, dtype) for shape, dtype in scratch]
        + [pltpu.SemaphoreType.DMA((slots, 8))] * 2,
        compiler_params=pltpu.CompilerParams(
            collective_id=collective, has_side_effects=True, vmem_limit_bytes=32 << 20
        ),
        cost_estimate=pl.CostEstimate(flops=10**7, bytes_accessed=10**7, transcendentals=0),
    )(*args)


def gather_kernel(own, out, send, recv, local):
    n = len(WIDTHS)
    y, x_lo, z, x_hi, core = places()
    yn, yp, yo = (y + 1) % 4, (y + 3) % 4, (y + 2) % 4
    zn, zp, zo = (z + 1) % 4, (z + 3) % 4, (z + 2) % 4
    y_next, y_prev = at_place(yn, x_lo, z, x_hi, core), at_place(yp, x_lo, z, x_hi, core)
    z_next, z_prev = at_place(y, x_lo, zn, x_hi, core), at_place(y, x_lo, zp, x_hi, core)
    across = at_place(y, 1 - x_lo, z, 1 - x_hi, core)
    twin = at_place(y, x_lo, z, x_hi, 1 - core)
    greet((y_next, y_prev, z_next, z_prev, across, twin))
    started = []

    def lanes(c):
        return pl.ds(sum(WIDTHS[:c]), WIDTHS[c])

    def go(c, slot, source, target, device):
        item = pltpu.make_async_remote_copy(
            src_ref=source, dst_ref=target, send_sem=send.at[c, slot], recv_sem=recv.at[c, slot],
            device_id=device, device_id_type=pl.DeviceIdType.MESH,
        )
        item.start()
        started.append(item)
        return item

    held = [[None] * 10 for _ in range(n)]
    loads = []

    def stage(c, step):
        kept = held[c]
        cols = lanes(c)
        split = c % 2 == 0
        rows = pl.ds(y, 1) if split else pl.ds(0, 4)

        def part(a, b, d):
            return out.at[a, b, core, d, :, cols]

        def pass_on(slot, source, device):
            kept[slot] = go(c, slot, source, source, device)

        if step == 0:
            kept[0] = go(c, 0, own.at[rows, :, cols], part(z, x_hi, rows), across)
            load = pltpu.make_async_copy(own.at[rows, :, cols], part(z, x_hi, rows), local.at[c])
            load.start()
            loads.append(load)
        elif step == 1:
            loads[c].wait()
            kept[0].wait_recv()
            pass_on(1, part(z, slice(None), rows), z_next)
            pass_on(2, part(z, slice(None), rows), z_prev)
        elif step == 2:
            kept[1].wait_recv()
            kept[2].wait_recv()
            pass_on(3, part(zp, 0, rows), z_next)
            pass_on(4, part(zn, 1, rows), z_prev)
        elif step == 3:
            kept[3].wait_recv()
            kept[4].wait_recv()
            if split:
                pass_on(5, part(slice(None), slice(None), rows), y_next)
                pass_on(6, part(slice(None), slice(None), rows), y_prev)
            else:
                pass_on(9, part(slice(None), slice(None), rows), twin)
        elif step == 4 and split:
            kept[5].wait_recv()
            kept[6].wait_recv()
            pass_on(7, part(slice(None), 0, pl.ds(yp, 1)), y_next)
            pass_on(8, part(slice(None), 1, pl.ds(yn, 1)), y_prev)
        elif step == 5 and split:
            kept[7].wait_recv()
            kept[8].wait_recv()
            pass_on(9, part(slice(None), slice(None), slice(None)), twin)
        elif step == 6:
            kept[9].wait_recv()

    for step in range(7):
        for c in range(n):
            stage(c, step)
    for item in started:
        item.wait_send()


def gather_all(own):
    cols = own.shape[1]
    n = len(WIDTHS)
    out = pl.pallas_call(
        gather_kernel,
        out_shape=jax.ShapeDtypeStruct((4, 2, 2, 4, 16, cols), BF),
        in_specs=[pl.BlockSpec(memory_space=pl.ANY)],
        out_specs=pl.BlockSpec(memory_space=pl.ANY),
        scratch_shapes=[
            pltpu.SemaphoreType.DMA((n, 10)), pltpu.SemaphoreType.DMA((n, 10)), pltpu.SemaphoreType.DMA((n,))
        ],
        compiler_params=pltpu.CompilerParams(collective_id=2, has_side_effects=True),
        cost_estimate=pl.CostEstimate(flops=10**8, bytes_accessed=10**8, transcendentals=0),
    )(own.reshape(4, 16, cols))
    return out.reshape(1024, cols)


def rope_parts(length, start):
    half = AP // 2
    inverse = THETA ** (-2.0 * jnp.arange(half).astype(F32) / AP)
    angles = (start + jnp.arange(length)).astype(F32)[:, None] * inverse[None, :]
    cosine = jnp.cos(angles)
    sine = jnp.sin(angles)
    return jnp.concatenate([cosine] * 4, axis=1), jnp.concatenate([-sine, sine] * 2, axis=1)


def pad_lanes(value):
    return jnp.pad(value.astype(F32), (0, 128 - value.shape[0]))[None, :]


def per_device(
    seqs, hidden_in, norm_gain, mixer_proj, attn_proj, conv_kernel, conv_bias, step_bias, decay_log,
    skip_gain, gated_gain, mixer_out, attn_out, ffn_gain, gate_up, down_proj, out_grad,
):
    T = hidden_in.shape[1]
    width = norm_gain.shape[0]
    shards = 1024 // width
    me = lax.axis_index("seq")
    mix_rows, att_rows, down_rows = mixer_out.shape[0], attn_out.shape[0], down_proj.shape[0]

    small = jnp.concatenate(
        [norm_gain, ffn_gain, gated_gain, conv_bias, conv_kernel.T.reshape(-1)]
    )
    slots = width * 104
    small = jnp.pad(small, (0, slots - small.shape[0])).reshape(width, 104)
    front_shard = jnp.concatenate(
        [mixer_proj[:, : D_SSM + XBC], attn_proj, mixer_proj[:, D_SSM + XBC :], small], axis=1
    )
    front = gather_all(front_shard)
    tail_shard = jnp.concatenate(
        [
            gate_up[:, :FF],
            gate_up[:, FF:],
            jnp.concatenate([jnp.concatenate([mixer_out, attn_out], axis=0), down_proj], axis=1),
        ],
        axis=0,
    )
    tail = lax.all_gather(tail_shard, "fsdp", axis=0, tiled=False)
    smalls = front.reshape(shards, width, FRONT)[:, :, 4120:].reshape(shards, slots)
    cuts = []
    at = 0
    for size in (width, width, gated_gain.shape[0], conv_bias.shape[0]):
        cuts.append(smalls[:, at : at + size].reshape(1, -1).astype(F32))
        at += size
    gain_one, gain_ffn, gain_gated, bias_all = cuts
    kernel_size = conv_kernel.shape[0]
    taps = smalls[:, at : at + 4 * kernel_size].reshape(shards, 4, kernel_size)
    taps = taps.transpose(1, 0, 2).reshape(4, XBC).astype(F32)
    taps = jnp.pad(taps, ((0, 4), (0, 0)))

    resid = hidden_in[0].astype(F32)
    scale_one = rms_scale(resid)
    normed_one = resid * scale_one
    normed_in = (normed_one * gain_one).astype(BF)
    projection = dot(normed_in, front)
    gate_pre = projection[:, :D_SSM]
    cosine, sine = rope_parts(T, me * T)
    edge = projection[T - 8 :, D_SSM : D_SSM + XBC].astype(BF)
    halo = lax.ppermute(edge, "seq", [(i, i + 1) for i in range(seqs - 1)])
    sbias, dlog, skip = pad_lanes(step_bias), pad_lanes(decay_log), pad_lanes(skip_gain)
    act, dt, cum, fresh, xbc, steps, query_rot, kv_own = call(
        mamba_first,
        [
            ((T, XBC), F32), ((T, 128), F32), ((T, 128), F32), ((D_SSM, NST), BF), ((T, XBC), BF),
            ((T, 128), BF), ((T, QH * AP), BF), ((T, 2 * KVH * AP), BF),
        ],
        projection, halo, cosine, sine, taps, bias_all, sbias, dlog,
        scratch=[pltpu.VMEM((T + 8, XBC), F32)],
    )
    heads = MH // seqs
    states = ((seqs, heads * AP, NST), BF)
    pairs = ((seqs, T, 2 * KVH * AP), BF)
    tails = ((seqs, 8, 128), F32)
    heads_out = ((T, QH * AP), BF)
    starts, kv_all, ends, attn_tok, lse = share_call(
        share_forward, 3, [states, pairs, tails, heads_out, ((QH, T), F32)],
        [states, states, states, pairs, tails, ((QH * AP, T), F32), ((QH, T), F32), ((QH, T), F32)], 4,
        fresh.reshape(states[0]), cum[T - 8 :], kv_own, query_rot,
    )
    starts = starts.reshape(D_SSM, NST)
    (mixed_y,) = call(mamba_second, [((T, D_SSM), BF)], act, dt, cum, starts, skip)

    proj_gate = tail[:, :width].reshape(-1, FF)
    proj_up = tail[:, width : 2 * width].reshape(-1, FF)
    low_rows = 2 * width
    out_mixer = tail[:, low_rows : low_rows + mix_rows, :1024].reshape(-1, 1024)
    out_attn = tail[:, low_rows + mix_rows :, :1024].reshape(-1, 1024)
    proj_down = tail[:, low_rows:, 1024:].reshape(-1, 1024)
    mixed = mixed_y.astype(F32)
    gated = mixed * jax.nn.silu(gate_pre)
    scale_two = rms_scale(gated)
    normed_two = gated * scale_two
    normed_mix = (normed_two * gain_gated).astype(BF)
    middle = resid + dot(normed_mix, out_mixer) + dot(attn_tok, out_attn)
    scale_three = rms_scale(middle)
    normed_three = middle * scale_three
    normed_ffn = (normed_three * gain_ffn).astype(BF)
    gate_half = dot(normed_ffn, proj_gate)
    up_half = dot(normed_ffn, proj_up)
    activ = (jax.nn.silu(gate_half) * up_half).astype(BF)
    block_out = (middle + dot(activ, proj_down)).astype(BF)

    ograd = out_grad[0]
    grad_activ = dot(ograd, proj_down, NT)
    grad_down = dot(activ, ograd, TN).astype(BF)
    grad_g = (grad_activ * up_half * silu_slope(gate_half)).astype(BF)
    grad_u = (grad_activ * jax.nn.silu(gate_half)).astype(BF)
    grad_gateup = dot(normed_ffn, jnp.concatenate([grad_g, grad_u], axis=1), TN).astype(BF)
    grad_nffn = dot(grad_g, proj_gate, NT) + dot(grad_u, proj_up, NT)
    grad_ffn = jnp.sum(grad_nffn * normed_three, axis=0)
    grad_middle = ograd.astype(F32) + rms_back(grad_nffn * gain_ffn, normed_three, scale_three)
    middle_bf = grad_middle.astype(BF)
    grad_mixed = dot(normed_mix, middle_bf, TN).astype(BF)
    grad_attended = dot(attn_tok, middle_bf, TN).astype(BF)
    grad_nmix = dot(middle_bf, out_mixer, NT)
    grad_otok = dot(middle_bf, out_attn, NT).astype(BF)
    grad_gated = jnp.sum(grad_nmix * normed_two, axis=0)
    grad_gz = rms_back(grad_nmix * gain_gated, normed_two, scale_two)
    grad_ymix = (grad_gz * jax.nn.silu(gate_pre)).astype(BF)
    grad_gate = (grad_gz * mixed * silu_slope(gate_pre)).astype(BF)
    grad_outs = jnp.concatenate(
        [grad_mixed.reshape(shards, mix_rows, 1024), grad_attended.reshape(shards, att_rows, 1024)], axis=1
    ).reshape(-1, 1024)

    (dstart,) = call(mamba_back_first, [((D_SSM, NST), BF)], grad_ymix, act, cum)
    dends, qgrad, dkv = share_call(
        share_backward, 4, [states, heads_out, ((T, 2 * KVH * AP), BF)],
        [states, states, states, pairs, pairs, ((T, QH * AP), F32)], 3,
        dstart.reshape(states[0]), ends, query_rot, kv_all, attn_tok, lse, grad_otok, cosine, sine,
    )
    dends = dends.reshape(D_SSM, NST)
    dconv, dtaps, dbias, dsteps, dhead = call(
        mamba_back_second,
        [((T, XBC), F32), ((8, XBC), F32), ((8, XBC), F32), ((T, 128), BF), ((8, 128), F32)],
        grad_ymix, xbc, halo, act, dt, cum, starts, dends, steps, taps, bias_all, sbias, dlog, skip,
        scratch=[pltpu.VMEM((T + 8, XBC), F32), pltpu.VMEM((T, XBC), F32)],
        limit=32,
    )
    ahead = lax.ppermute(dconv[:8].astype(BF), "seq", [(i + 1, i) for i in range(seqs - 1)])
    (grad_proj,) = call(
        finish_grads, [((T, FRONT), BF)], dconv, ahead, taps, grad_gate, qgrad, dkv, dsteps,
        scratch=[pltpu.VMEM((T + 8, XBC), F32)],
    )

    grad_front = dot(normed_in, grad_proj, TN).astype(BF)
    grad_nin = dot(grad_proj, front, NT)
    grad_norm = jnp.sum(grad_nin * normed_one, axis=0)
    input_grad = grad_middle + rms_back(grad_nin * gain_one, normed_one, scale_one)
    vectors = [grad_norm, grad_ffn, grad_gated, dbias[0]] + [dtaps[lag] for lag in range(4)]
    vectors = [value.reshape(shards, -1) for value in vectors]
    vectors.append(jnp.broadcast_to(dhead[:3, :MH].reshape(1, 3 * MH), (shards, 3 * MH)))
    vectors = jnp.concatenate(vectors, axis=1)
    vectors = jnp.pad(vectors, ((0, 0), (0, slots - vectors.shape[1]))).astype(BF)
    last = jnp.concatenate([grad_front[:, 4096:4120], vectors.reshape(-1, 104)], axis=1)
    mixer_sum, attn_sum, vectors, gateup_sum, mixed_sum, attended_sum, down_sum = reduce_all(
        [lax.dynamic_update_slice(grad_front, last, (0, 4096)), grad_gateup, grad_outs, grad_down], REDUCED
    )
    vectors = vectors[:, 24:].reshape(-1)
    owned = []
    at = 0
    for size in [width, width, gated_gain.shape[0], kernel_size] + [kernel_size] * 4 + [MH] * 3:
        owned.append(vectors[at : at + size])
        at += size
    own_taps = jnp.stack(owned[4:8], axis=1)
    return (
        block_out[None],
        input_grad[None],
        owned[0],
        mixer_sum,
        attn_sum,
        own_taps,
        owned[3],
        owned[8],
        owned[9],
        owned[10],
        owned[2],
        mixed_sum,
        attended_sum,
        owned[1],
        gateup_sum,
        down_sum,
    )


def solution(mesh):
    tokens = P("fsdp", "seq", None)
    vector = P("fsdp")
    matrix = P("fsdp", None)
    in_specs = (
        tokens, vector, matrix, matrix, matrix, vector, P(), P(), P(), vector, matrix, matrix, vector,
        matrix, matrix, tokens,
    )
    out_specs = (
        tokens, tokens, vector, matrix, matrix, matrix, vector, P(), P(), P(), vector, matrix, matrix,
        vector, matrix, matrix,
    )
    return jax.shard_map(
        functools.partial(per_device, mesh.shape["seq"]),
        mesh=mesh, in_specs=in_specs, out_specs=out_specs, check_vma=False,
    )
```

```python
import functools
import math

import jax
import jax.numpy as jnp
from jax import lax
from jax.experimental import pallas as pl
from jax.experimental.pallas import tpu as pltpu
from jax.sharding import PartitionSpec as P

MH = 24
NST = 128
QH = 8
KVH = 2
AP = 64
FF = 2048
D_SSM = 1536
XBC = 1792
CIN = 3352
FRONT = 4224
EPSILON = 1e-05
THETA = 10000.0
HIGHEST = lax.Precision.HIGHEST
F32 = jnp.float32
BF = jnp.bfloat16
NT = (((1,), (1,)), ((), ()))
TN = (((0,), (0,)), ((), ()))


def dot(a, b, dims=(((1,), (0,)), ((), ())), precision=None):
    return lax.dot_general(a, b, dims, preferred_element_type=F32, precision=precision)


def silu_slope(value):
    sigma = jax.nn.sigmoid(value)
    return sigma * (1.0 + value * (1.0 - sigma))


def rms_scale(value):
    return lax.rsqrt(jnp.mean(value * value, axis=1, keepdims=True) + EPSILON)


def rms_back(grad_normed, normed, scale):
    return scale * (grad_normed - normed * jnp.mean(grad_normed * normed, axis=1, keepdims=True))


def head_selector(rows, cols):
    channel = lax.broadcasted_iota(jnp.int32, (rows, cols), 0)
    head = lax.broadcasted_iota(jnp.int32, (rows, cols), 1)
    return jnp.where((channel >= head * AP) & (channel < head * AP + AP), 1.0, 0.0).astype(F32)


def spread_heads(value):
    head = lax.broadcasted_iota(jnp.int32, (128, D_SSM), 0)
    channel = lax.broadcasted_iota(jnp.int32, (128, D_SSM), 1)
    select = jnp.where((channel >= head * AP) & (channel < head * AP + AP), 1.0, 0.0).astype(F32)
    return dot(value, select, precision=HIGHEST)


def gather_heads(value):
    return dot(value, head_selector(D_SSM, 128), precision=HIGHEST)


def conv_pre(ext, taps, bias, length):
    result = bias[...] + taps[3:4, :] * ext[8 : 8 + length, :]
    for lag in range(3):
        result = result + taps[lag : lag + 1, :] * ext[pl.ds(5 + lag, length), :]
    return result


def swap_halves(value):
    lane = lax.broadcasted_iota(jnp.int32, value.shape, 1)
    return jnp.where(lane % AP < AP // 2, pltpu.roll(value, 96, 1), pltpu.roll(value, 32, 1))


def mamba_first(
    proj, halo, cosine, sine, taps, bias, sbias, dlog,
    act_ref, dt_ref, cum_ref, fresh_ref, xbc_ref, steps_ref, q_ref, kv_ref, ext,
):
    length = proj.shape[0]
    for pair in range(QH // 2 + 1):
        at = D_SSM + XBC + pair * 128
        value = proj[:, at : at + 128].astype(BF).astype(F32)
        value = (value * cosine[...] + swap_halves(value) * sine[...]).astype(BF)
        if pair < QH // 2:
            q_ref[:, pair * 128 : pair * 128 + 128] = value * (1.0 / math.sqrt(AP))
        else:
            kv_ref[:, 0:128] = value
    kv_ref[:, 128:256] = proj[:, 3968:4096].astype(BF)
    xbc = proj[:, D_SSM : D_SSM + XBC].astype(BF)
    steps = proj[:, 4096:].astype(BF)
    xbc_ref[...] = xbc
    steps_ref[...] = steps
    ext[0:8, :] = halo[...].astype(F32)
    ext[8 : 8 + length, :] = xbc.astype(F32)
    conv = conv_pre(ext, taps, bias, length)
    act = conv * jax.nn.sigmoid(conv)
    act_ref[...] = act
    lane = lax.broadcasted_iota(jnp.int32, (length, 128), 1)
    raw = steps.astype(F32) + sbias[...]
    dt = jnp.maximum(raw, 0.0) + jnp.log1p(jnp.exp(-jnp.abs(raw)))
    dt = jnp.where(lane < MH, dt, 0.0)
    dt_ref[...] = dt
    row = lax.broadcasted_iota(jnp.int32, (length, length), 0)
    col = lax.broadcasted_iota(jnp.int32, (length, length), 1)
    lower = jnp.where(row >= col, 1.0, 0.0).astype(F32)
    cum = dot(lower, dt * (-jnp.exp(dlog[...])), precision=HIGHEST)
    cum_ref[...] = cum
    weight = spread_heads(jnp.exp(cum[length - 1 : length, :] - cum) * dt)
    scaled = (act[:, :D_SSM] * weight).astype(BF)
    fresh_ref[...] = dot(scaled, act[:, D_SSM : D_SSM + NST].astype(BF), TN).astype(BF)


def mamba_second(act, dt, cum, starts, skip, y_ref):
    length = act.shape[0]
    cumv = cum[...]
    cum_t = cumv.T
    bmat = act[:, D_SSM : D_SSM + NST].astype(BF)
    cmat = act[:, D_SSM + NST :].astype(BF)
    inner = dot(cmat, bmat, NT)
    row = lax.broadcasted_iota(jnp.int32, (length, length), 0)
    col = lax.broadcasted_iota(jnp.int32, (length, length), 1)
    inner = jnp.where(row >= col, inner, 0.0)
    x = act[:, :D_SSM]
    scaled = (x * spread_heads(dt[...])).astype(BF)
    outer = dot(cmat, starts[...], NT) * spread_heads(jnp.exp(cumv))
    base = outer + spread_heads(skip[...]) * x
    for pair in range(MH // 2):
        parts = []
        for h in (2 * pair, 2 * pair + 1):
            fade = jnp.exp(jnp.minimum(cumv[:, h : h + 1] - cum_t[h : h + 1, :], 0.0))
            parts.append(dot((inner * fade).astype(BF), scaled[:, h * AP : h * AP + AP]))
        lanes = slice(pair * 128, pair * 128 + 128)
        y_ref[:, lanes] = (base[:, lanes] + jnp.concatenate(parts, axis=1)).astype(BF)


def mamba_back_first(gy, act, cum, dstart_ref):
    rise = spread_heads(jnp.exp(cum[...]))
    cmat = act[:, D_SSM + NST :].astype(BF)
    dstart_ref[...] = dot((gy[...].astype(F32) * rise).astype(BF), cmat, TN).astype(BF)


def mamba_back_second(
    gy, xbc, halo, act, dt, cum, starts, dends, steps, taps, bias, sbias, dlog, skip,
    dconv_ref, dtaps_ref, dbias_ref, dsteps_ref, dhead_ref, ext, dact,
):
    length = act.shape[0]
    cumv = cum[...]
    dtv = dt[...]
    cum_t = cumv.T
    lane = lax.broadcasted_iota(jnp.int32, (length, 128), 1)
    bmat = act[:, D_SSM : D_SSM + NST].astype(BF)
    cmat = act[:, D_SSM + NST :].astype(BF)
    row = lax.broadcasted_iota(jnp.int32, (length, length), 0)
    col = lax.broadcasted_iota(jnp.int32, (length, length), 1)
    inner_t = jnp.where(col >= row, dot(bmat, cmat, NT), 0.0)
    x = act[:, :D_SSM]
    gyb = gy[...]
    gyf = gyb.astype(F32)
    dt_full = spread_heads(dtv)
    tail = spread_heads(jnp.exp(cumv[length - 1 : length, :] - cumv))
    rise = spread_heads(jnp.exp(cumv))
    xs = x * dt_full
    xsb = xs.astype(BF)
    ginner = jnp.zeros((length, length), F32)
    qcols = jnp.zeros((length, 128), F32)
    rrows = []
    for pair in range(MH // 2):
        parts = []
        for h in (2 * pair, 2 * pair + 1):
            lanes = slice(h * AP, h * AP + AP)
            fade = jnp.exp(jnp.minimum(cum_t[h : h + 1, :] - cumv[:, h : h + 1], 0.0))
            graded = dot(xsb[:, lanes], gyb[:, lanes], NT) * fade
            ginner = ginner + graded
            weighed = graded * inner_t
            rrows.append(jnp.sum(weighed, axis=0, keepdims=True))
            qcols = jnp.where(lane == h, jnp.sum(weighed, axis=1, keepdims=True), qcols)
            parts.append(dot((inner_t * fade).astype(BF), gyb[:, lanes]))
        dact[:, pair * 128 : pair * 128 + 128] = jnp.concatenate(parts, axis=1)
    ginner = jnp.where(col >= row, ginner, 0.0).astype(BF)
    rrows = jnp.concatenate(rrows + [jnp.zeros((128 - MH, length), F32)], axis=0).T
    endb = dends[...]
    startb = starts[...]
    from_end = dot(bmat, endb, NT) * tail
    dxs = dact[:, :D_SSM] + from_end
    reach = gather_heads(xs * from_end)
    outer = dot(cmat, startb, NT) * rise
    dcum = rrows - qcols + gather_heads(gyf * outer) - reach
    total = jnp.exp(cumv[length - 1 : length, :])
    carried = gather_heads_rows(startb, endb) * total + jnp.sum(reach, axis=0, keepdims=True)
    last = lax.broadcasted_iota(jnp.int32, (length, 128), 0) == length - 1
    dcum = dcum + jnp.where(last, carried, 0.0)
    upper = jnp.where(col >= row, 1.0, 0.0).astype(F32)
    rest = dot(upper, dcum, precision=HIGHEST)
    decay = -jnp.exp(dlog[...])
    ddt = gather_heads(x * dxs) + decay * rest
    ddecay = jnp.sum(dtv * rest, axis=0, keepdims=True) * decay
    raw = steps[...].astype(F32) + sbias[...]
    dsteps = jnp.where(lane < MH, ddt * jax.nn.sigmoid(raw), 0.0)
    dsteps_ref[...] = dsteps.astype(BF)
    dskip = gather_heads(jnp.sum(x * gyf, axis=0, keepdims=True))
    dhead_ref[0:1, :] = jnp.sum(dsteps, axis=0, keepdims=True)
    dhead_ref[1:2, :] = ddecay
    dhead_ref[2:3, :] = dskip
    dhead_ref[3:8, :] = jnp.zeros((5, 128), F32)
    dact[:, :D_SSM] = dt_full * dxs + spread_heads(skip[...]) * gyf
    dact[:, D_SSM : D_SSM + NST] = dot((xs * tail).astype(BF), endb) + dot(ginner, cmat)
    dact[:, D_SSM + NST :] = dot((gyf * rise).astype(BF), startb) + dot(ginner, bmat, TN)
    ext[0:8, :] = halo[...].astype(F32)
    ext[8 : 8 + length, :] = xbc[...].astype(F32)
    conv = conv_pre(ext, taps, bias, length)
    dconv = dact[...] * silu_slope(conv)
    dconv_ref[...] = dconv
    dbias_ref[...] = jnp.broadcast_to(jnp.sum(dconv, axis=0, keepdims=True), (8, XBC))
    for lag in range(4):
        dtaps_ref[lag : lag + 1, :] = jnp.sum(
            dconv * ext[pl.ds(5 + lag, length), :], axis=0, keepdims=True
        )
    dtaps_ref[4:8, :] = jnp.zeros((4, XBC), F32)


def gather_heads_rows(a, b):
    product = a.astype(F32) * b.astype(F32)
    per_row = dot(jnp.ones((8, NST), F32), product, NT, precision=HIGHEST)
    return gather_heads(per_row)[0:1, :]


def attend_block(q, kv, c, diagonal, acc, top, total):
    block = q.shape[0]
    if diagonal:
        key_at = lax.broadcasted_iota(jnp.int32, (block, block), 0)
        allowed = key_at <= lax.broadcasted_iota(jnp.int32, (block, block), 1)
    turned = kv[c, :, KVH * AP :].astype(F32).T.astype(BF)
    for h in range(QH):
        g = h // (QH // KVH)
        keys = kv[c, :, g * AP : g * AP + AP]
        values = turned[g * AP : g * AP + AP, :]
        s = dot(keys, q[:, h * AP : h * AP + AP], NT)
        band = slice(h * AP, h * AP + AP)
        if diagonal:
            s = jnp.where(allowed, s, -1e30)
            new = jnp.max(s, axis=0, keepdims=True)
            p = jnp.exp(s - new)
            total[h : h + 1, :] = jnp.sum(p, axis=0, keepdims=True)
            acc[band, :] = dot(values, p.astype(BF))
        else:
            old = top[h : h + 1, :]
            new = jnp.maximum(old, jnp.max(s, axis=0, keepdims=True))
            p = jnp.exp(s - new)
            fix = jnp.exp(old - new)
            total[h : h + 1, :] = total[h : h + 1, :] * fix + jnp.sum(p, axis=0, keepdims=True)
            acc[band, :] = acc[band, :] * fix + dot(values, p.astype(BF))
        top[h : h + 1, :] = new


def attend_back_block(q, kv, c, diagonal, lse, go, centre, dq_ref):
    block = q.shape[0]
    if diagonal:
        key_at = lax.broadcasted_iota(jnp.int32, (block, block), 0)
        allowed = key_at <= lax.broadcasted_iota(jnp.int32, (block, block), 1)
    turned = kv[c, :, : KVH * AP].astype(F32).T.astype(BF)
    sums = []
    for g in range(KVH):
        keys = kv[c, :, g * AP : g * AP + AP]
        values = kv[c, :, KVH * AP + g * AP : KVH * AP + g * AP + AP]
        dk = jnp.zeros((block, AP), F32)
        dv = jnp.zeros((block, AP), F32)
        for h in range(g * (QH // KVH), (g + 1) * (QH // KVH)):
            band = slice(h * AP, h * AP + AP)
            qh = q[:, band]
            gh = go[:, band]
            s = dot(keys, qh, NT) - lse[h : h + 1, :]
            p = jnp.exp(jnp.where(allowed, s, -1e30) if diagonal else s)
            dv = dv + dot(p.astype(BF), gh)
            dp = dot(values, gh, NT)
            ds = (p * (dp - centre[h : h + 1, :])).astype(BF)
            dk = dk + dot(ds, qh)
            part = dot(turned[g * AP : g * AP + AP, :], ds)
            dq_ref[band, :] = part if diagonal else dq_ref[band, :] + part
        sums.append((dk, dv))
    return (
        jnp.concatenate([sums[0][0], sums[1][0]], axis=1),
        jnp.concatenate([sums[0][1], sums[1][1]], axis=1),
    )


def finish_grads(dconv, ahead, taps, gate, dq, dkv, dsteps, out_ref, ext):
    length = dconv.shape[0]
    ext[0:length, :] = dconv[...]
    ext[length : length + 8, :] = ahead[...].astype(F32)
    du = taps[3:4, :] * ext[0:length, :]
    for lag in range(3):
        du = du + taps[lag : lag + 1, :] * ext[pl.ds(3 - lag, length), :]
    out_ref[:, :D_SSM] = gate[...]
    out_ref[:, D_SSM : D_SSM + XBC] = du.astype(BF)
    out_ref[:, 3328:3840] = dq[...]
    out_ref[:, 3840:4096] = dkv[...]
    out_ref[:, 4096:] = dsteps[...]


def call(kernel, outs, *args, scratch=(), limit=20):
    spec = pl.BlockSpec(memory_space=pltpu.VMEM)
    return pl.pallas_call(
        kernel,
        out_shape=[jax.ShapeDtypeStruct(shape, dtype) for shape, dtype in outs],
        in_specs=[spec] * len(args),
        out_specs=[spec] * len(outs),
        scratch_shapes=list(scratch),
        compiler_params=pltpu.CompilerParams(vmem_limit_bytes=limit << 20),
    )(*args)


def places():
    s, f = lax.axis_index("seq"), lax.axis_index("fsdp")
    return s // 2, s % 2, f // 4, (f // 2) % 2, f % 2


def at_place(y, x_lo, z, x_hi, core):
    return {"seq": y * 2 + x_lo, "fsdp": z * 4 + x_hi * 2 + core}


def greet(others):
    barrier = pltpu.get_barrier_semaphore()
    for other in others:
        pl.semaphore_signal(barrier, inc=1, device_id=other, device_id_type=pl.DeviceIdType.MESH)
    pl.semaphore_wait(barrier, len(others))


WIDTHS = (1024, 1024, 1024, 1152)


def reduce_kernel(chunks, *refs):
    n = len(chunks)
    count = max(chunk[0] for chunk in chunks) + 1
    inputs, outs, refs = refs[:count], refs[count : count + 7], refs[count + 7 :]
    groups = [refs[i * 10 : i * 10 + 10] for i in range(n)]
    refs = refs[n * 10 :]
    pieces, (send, recv, local) = refs[:count], refs[count:]
    y, x_lo, z, x_hi, core = places()
    yn, yp, yo = (y + 1) % 4, (y + 3) % 4, (y + 2) % 4
    zn, zp, zo = (z + 1) % 4, (z + 3) % 4, (z + 2) % 4
    y_next, y_prev = at_place(yn, x_lo, z, x_hi, core), at_place(yp, x_lo, z, x_hi, core)
    y_far = at_place(yo, x_lo, z, x_hi, core)
    z_next, z_prev = at_place(y, x_lo, zn, x_hi, core), at_place(y, x_lo, zp, x_hi, core)
    across = at_place(y, 1 - x_lo, z, 1 - x_hi, core)
    beside = at_place(y, 1 - x_lo, z, x_hi, core)
    twin = at_place(y, x_lo, z, x_hi, 1 - core)
    greet((y_next, y_prev, y_far, z_next, z_prev, across, beside, twin))

    def copy(c, slot, source, target, device):
        return pltpu.make_async_remote_copy(
            src_ref=source, dst_ref=target, send_sem=send.at[c, slot], recv_sem=recv.at[c, slot],
            device_id=device, device_id_type=pl.DeviceIdType.MESH,
        )

    started = []

    def go(c, slot, source, target, device):
        item = copy(c, slot, source, target, device)
        item.start()
        started.append(item)
        return item

    def lanes(c):
        return pl.ds(chunks[c][1], chunks[c][2])

    first = [[None] * 16 for _ in range(n)]
    loads = []
    for c in range(n):
        acc, twin_buf = groups[c][0], groups[c][1]
        g = inputs[chunks[c][0]]
        first[c][0] = go(c, 0, g.at[:, :, 1 - core, :, :, lanes(c)], twin_buf, twin)
        load = pltpu.make_async_copy(g.at[:, :, core, :, :, lanes(c)], acc, local.at[c])
        load.start()
        loads.append(load)

    def add(target, source):
        target[...] = target[...] + source[...]

    def stage(c, step):
        acc, twin_buf, p1, m1, p2, m2, q1, r1, q2, r2 = groups[c][:10]
        kept = first[c]
        gathered = pieces[chunks[c][0]]
        y_first = c % 2 == 0
        if step == 0:
            loads[c].wait()
            kept[0].wait_recv()

            def body(i, carry):
                a, b, d = i // 8, (i // 4) % 2, i % 4
                add(acc.at[a, b, d], twin_buf.at[a, b, d])
                return carry

            lax.fori_loop(0, 32, body, 0)
            if y_first:
                kept[1] = go(c, 1, acc.at[:, 0, yo], p1, y_next)
                kept[2] = go(c, 2, acc.at[:, 1, yo], m1, y_prev)
            else:
                kept[1] = go(c, 1, acc.at[zo, 0], p1, z_next)
                kept[2] = go(c, 2, acc.at[zo, 1], m1, z_prev)
        elif step == 1:
            kept[1].wait_recv()
            kept[2].wait_recv()

            def body(i, carry):
                if y_first:
                    add(acc.at[i, 0, yn], p1.at[i])
                    add(acc.at[i, 1, yp], m1.at[i])
                else:
                    add(acc.at[zn, 0, i], p1.at[i])
                    add(acc.at[zp, 1, i], m1.at[i])
                return carry

            lax.fori_loop(0, 4, body, 0)
            if y_first:
                kept[3] = go(c, 3, acc.at[:, :, yn], p2, y_next)
                kept[4] = go(c, 4, acc.at[:, :, yp], m2, y_prev)
            else:
                kept[3] = go(c, 3, acc.at[zn], p2, z_next)
                kept[4] = go(c, 4, acc.at[zp], m2, z_prev)
        elif step == 2:
            kept[3].wait_recv()
            kept[4].wait_recv()

            def body(i, carry):
                if y_first:
                    a, b = i // 2, i % 2
                    add(acc.at[a, b, y], p2.at[a, b])
                    add(acc.at[a, b, y], m2.at[a, b])
                else:
                    a, b = i // 4, i % 4
                    add(acc.at[z, a, b], p2.at[a, b])
                    add(acc.at[z, a, b], m2.at[a, b])
                return carry

            lax.fori_loop(0, 8, body, 0)
            if y_first:
                kept[5] = go(c, 5, acc.at[zo, 0, y], q1, z_next)
                kept[6] = go(c, 6, acc.at[zo, 1, y], r1, z_prev)
            else:
                kept[5] = go(c, 5, acc.at[z, 0, yo], q1, y_next)
                kept[6] = go(c, 6, acc.at[z, 1, yo], r1, y_prev)
        elif step == 3:
            kept[5].wait_recv()
            kept[6].wait_recv()
            if y_first:
                add(acc.at[zn, 0, y], q1)
                add(acc.at[zp, 1, y], r1)
                kept[7] = go(c, 7, acc.at[zn, :, y], q2, z_next)
                kept[8] = go(c, 8, acc.at[zp, :, y], r2, z_prev)
            else:
                add(acc.at[z, 0, yn], q1)
                add(acc.at[z, 1, yp], r1)
                kept[7] = go(c, 7, acc.at[z, :, yn], q2, y_next)
                kept[8] = go(c, 8, acc.at[z, :, yp], r2, y_prev)
        elif step == 4:
            kept[7].wait_recv()
            kept[8].wait_recv()
            for b in range(2):
                add(acc.at[z, b, y], q2.at[b])
                add(acc.at[z, b, y], r2.at[b])
            kept[9] = go(c, 9, acc.at[z, 1 - x_hi, y], gathered.at[4, :, lanes(c)], across)
        elif step == 5:
            kept[9].wait_recv()
            acc[z, x_hi, y] = acc[z, x_hi, y] + gathered[4, :, lanes(c)]
            kept[10] = go(c, 10, acc.at[z, x_hi, y], gathered.at[5, :, lanes(c)], beside)
        elif step == 6:
            kept[10].wait_recv()
            gathered[y, :, lanes(c)] = acc[z, x_hi, y] + gathered[5, :, lanes(c)]
            mine = gathered.at[y, :, lanes(c)]
            kept[11] = go(c, 11, mine, mine, y_next)
            kept[12] = go(c, 12, mine, mine, y_prev)
            kept[13] = go(c, 13, mine, mine, y_far)
        else:
            for slot in (11, 12, 13):
                kept[slot].wait_recv()

    for turn in range(n // 2 + 7):
        for c in reversed(range(n)):
            if 0 <= turn - c // 2 < 8:
                stage(c, turn - c // 2)
    mixer, attn, vector, gateup, mixed, attended, down = outs
    for i in range(4):
        mixer[i, :, : D_SSM + XBC] = pieces[0][i, :, : D_SSM + XBC].astype(F32)
        mixer[i, :, D_SSM + XBC :] = pieces[0][i, :, 4096:4120].astype(F32)
        attn[i] = pieces[0][i, :, 3328:4096].astype(F32)
        vector[i] = pieces[0][i, :, 4096:].astype(F32)
        gateup[i] = pieces[1][i].astype(F32)
        if i < 3:
            mixed[i] = pieces[2][i].astype(F32)
        else:
            attended[0] = pieces[2][i].astype(F32)
        down[i] = pieces[3][i].astype(F32)
    for item in started:
        item.wait_send()


def reduce_all(values, chunks):
    shapes = [(value.shape[0] // 64, value.shape[1]) for value in values]
    scratch = []
    for c, (which, _, w) in enumerate(chunks):
        r = shapes[which][0]
        scratch += [pltpu.VMEM((4, 2, 4, r, w), BF)] * 2 + [pltpu.VMEM((4, r, w), BF)] * 2
        scratch += [pltpu.VMEM((4, 2, r, w) if c % 2 == 0 else (2, 4, r, w), BF)] * 2
        scratch += [pltpu.VMEM((r, w), BF)] * 2 + [pltpu.VMEM((2, r, w), BF)] * 2
    n = len(chunks)
    scratch += [pltpu.VMEM((6,) + shape, BF) for shape in shapes]
    scratch += [pltpu.SemaphoreType.DMA((n, 14)), pltpu.SemaphoreType.DMA((n, 14)), pltpu.SemaphoreType.DMA((n,))]
    outs = [(4, 16, CIN), (4, 16, 768), (4, 16, 128), (4, 16, 2 * FF), (3, 32, 1024), (1, 32, 1024), (4, 32, 1024)]
    outs = pl.pallas_call(
        functools.partial(reduce_kernel, chunks),
        out_shape=[jax.ShapeDtypeStruct(shape, F32) for shape in outs],
        in_specs=[pl.BlockSpec(memory_space=pl.ANY)] * len(values),
        out_specs=[pl.BlockSpec(memory_space=pltpu.VMEM)] * len(outs),
        scratch_shapes=scratch,
        compiler_params=pltpu.CompilerParams(
            collective_id=1, has_side_effects=True, vmem_limit_bytes=60 << 20
        ),
        cost_estimate=pl.CostEstimate(flops=10**8, bytes_accessed=10**8, transcendentals=0),
    )(*[value.reshape((4, 2, 2, 4) + shape) for value, shape in zip(values, shapes)])
    return [out.reshape(-1, out.shape[2]) for out in outs]


REDUCED = (
    (2, 0, 1024), (3, 0, 1024), (1, 0, 1408), (1, 1408, 1408), (1, 2816, 1280), (0, 0, 1408), (0, 1408, 1408),
    (0, 2816, 1408),
)


def seq_group(s, send, recv):
    group = [{"seq": (s + d) % 8} for d in range(1, 8)]
    started = []

    def make(slot, d, source, target):
        return pltpu.make_async_remote_copy(
            src_ref=source, dst_ref=target, send_sem=send.at[slot, d % 8], recv_sem=recv.at[slot, d % 8],
            device_id={"seq": (s + d) % 8}, device_id_type=pl.DeviceIdType.MESH,
        )

    def go(slot, d, source, target):
        item = make(slot, d, source, target)
        item.start()
        started.append(item)
        return item

    return group, started, make, go


def fade_of(ends, c, head):
    lane = lax.broadcasted_iota(jnp.int32, (1, 128), 1)
    row = ends[c][7:8, :]
    return jnp.exp(jnp.sum(jnp.where(lane == head, row, 0.0), axis=1, keepdims=True))


def scan_states(ends, s, heads, got, made, order):
    for k in range(heads):
        rows = slice(k * AP, k * AP + AP)
        running = jnp.zeros((AP, NST), F32)
        for c in order:
            made[c, rows, :] = running.astype(BF)
            if c != order[-1]:
                running = running * fade_of(ends, c, s * heads + k) + got[c, rows, :].astype(F32)


def share_forward(
    fresh, last, kv, q, starts_out, kv_out, ends_out, o_ref, lse_ref,
    got, made, back, kv_all, ends, acc, top, total, send, recv,
):
    s = lax.axis_index("seq")
    group, started, make, go = seq_group(s, send, recv)
    kv_all[...] = jnp.zeros_like(kv_all)
    greet(group)
    waits = [[], []]
    for d in range(1, 8):
        waits[0].append(go(0, d, fresh.at[(s + d) % 8], got.at[s]))
        waits[0].append(go(1, d, last, ends.at[s]))
    for d in range(1, 8):
        pl.when(s + d < 8)(make(2, d, kv, kv_all.at[s]).start)
    got[s] = fresh[s]
    ends[s] = last[...]
    kv_all[s] = kv[...]
    attend_block(q, kv_all, s, True, acc, top, total)
    for item in waits[0]:
        item.wait_recv()
    scan_states(ends, s, fresh.shape[1] // AP, got, made, list(range(8)))
    for d in range(1, 8):
        waits[1].append(go(3, d, made.at[(s + d) % 8], back.at[s]))
    back[s] = made[s]

    def step(d, carry):
        make(2, d, kv, kv_all.at[s]).wait_recv()
        attend_block(q, kv_all, s - d, False, acc, top, total)
        return carry

    lax.fori_loop(1, s + 1, step, 0)
    lse_ref[...] = top[...] + jnp.log(total[...])
    for pair in range(QH // 2):
        parts = []
        for h in (2 * pair, 2 * pair + 1):
            parts.append(acc[h * AP : h * AP + AP, :] / total[h : h + 1, :])
        o_ref[:, pair * 128 : pair * 128 + 128] = jnp.concatenate(parts, axis=0).T.astype(BF)
    for item in waits[1]:
        item.wait_recv()
    starts_out[...] = back[...]
    kv_out[...] = kv_all[...]
    ends_out[...] = ends[...]
    for d in range(1, 8):
        pl.when(s + d < 8)(make(2, d, kv, kv_all.at[s]).wait_send)
    for item in started:
        item.wait_send()


def share_backward(
    dstart, ends, q, kv, o, lse, go_ref, cosine, sine, dends_out, dq_out, dkv_out,
    got, made, back, kv_got, kv_made, dq, send, recv,
):
    s = lax.axis_index("seq")
    group, started, make, go = seq_group(s, send, recv)
    kv_got[...] = jnp.zeros_like(kv_got)
    greet(group)
    waits = [[], []]
    for d in range(1, 8):
        waits[0].append(go(0, d, dstart.at[(s + d) % 8], got.at[s]))
    got[s] = dstart[s]
    pick_h = lax.broadcasted_iota(jnp.int32, (8, QH * AP), 0)
    pick_c = lax.broadcasted_iota(jnp.int32, (8, QH * AP), 1)
    pick = jnp.where((pick_c >= pick_h * AP) & (pick_c < pick_h * AP + AP), 1.0, 0.0).astype(F32)
    centre = dot(pick, go_ref[...].astype(F32) * o[...].astype(F32), NT, precision=HIGHEST)
    own_k, own_v = attend_back_block(q, kv, s, True, lse, go_ref, centre, dq)
    for item in waits[0]:
        item.wait_recv()
    scan_states(ends, s, dstart.shape[1] // AP, got, made, list(range(7, -1, -1)))
    for d in range(1, 8):
        waits[1].append(go(2, d, made.at[(s + d) % 8], back.at[s]))
    back[s] = made[s]

    def sent(d):
        return make(1, 8 - d, kv_made.at[s - d], kv_got.at[s])

    def step(d, carry):
        dk, dv = attend_back_block(q, kv, s - d, False, lse, go_ref, centre, dq)
        kv_made[s - d, :, 0:128] = dk.astype(BF)
        kv_made[s - d, :, 128:256] = dv.astype(BF)
        sent(d).start()
        return carry

    lax.fori_loop(1, s + 1, step, 0)
    for pair in range(QH // 2):
        value = dq[pair * 128 : pair * 128 + 128, :].T * (1.0 / math.sqrt(AP))
        value = value * cosine[...] - swap_halves(value) * sine[...]
        dq_out[:, pair * 128 : pair * 128 + 128] = value.astype(BF)
    for d in range(1, 8):
        pl.when(s + d < 8)(make(1, 8 - d, kv_made.at[0], kv_got.at[s]).wait_recv)
    for c in range(8):
        own_k = own_k + kv_got[c, :, 0:128].astype(F32)
        own_v = own_v + kv_got[c, :, 128:256].astype(F32)
    dkv_out[:, 0:128] = (own_k * cosine[...] - swap_halves(own_k) * sine[...]).astype(BF)
    dkv_out[:, 128:256] = own_v.astype(BF)
    for item in waits[1]:
        item.wait_recv()
    dends_out[...] = back[...]
    for d in range(1, 8):
        pl.when(s - d >= 0)(make(1, 8 - d, kv_made.at[0], kv_got.at[s]).wait_send)
    for item in started:
        item.wait_send()


def share_call(kernel, collective, outs, scratch, slots, *args):
    spec = pl.BlockSpec(memory_space=pltpu.VMEM)
    return pl.pallas_call(
        kernel,
        out_shape=[jax.ShapeDtypeStruct(shape, dtype) for shape, dtype in outs],
        in_specs=[spec] * len(args),
        out_specs=[spec] * len(outs),
        scratch_shapes=[pltpu.VMEM(shape, dtype) for shape, dtype in scratch]
        + [pltpu.SemaphoreType.DMA((slots, 8))] * 2,
        compiler_params=pltpu.CompilerParams(
            collective_id=collective, has_side_effects=True, vmem_limit_bytes=32 << 20
        ),
        cost_estimate=pl.CostEstimate(flops=10**7, bytes_accessed=10**7, transcendentals=0),
    )(*args)


def gather_kernel(own, out, send, recv, local):
    n = len(WIDTHS)
    y, x_lo, z, x_hi, core = places()
    yn, yp, yo = (y + 1) % 4, (y + 3) % 4, (y + 2) % 4
    zn, zp, zo = (z + 1) % 4, (z + 3) % 4, (z + 2) % 4
    y_next, y_prev = at_place(yn, x_lo, z, x_hi, core), at_place(yp, x_lo, z, x_hi, core)
    z_next, z_prev = at_place(y, x_lo, zn, x_hi, core), at_place(y, x_lo, zp, x_hi, core)
    across = at_place(y, 1 - x_lo, z, 1 - x_hi, core)
    twin = at_place(y, x_lo, z, x_hi, 1 - core)
    greet((y_next, y_prev, z_next, z_prev, across, twin))
    started = []

    def lanes(c):
        return pl.ds(sum(WIDTHS[:c]), WIDTHS[c])

    def go(c, slot, source, target, device):
        item = pltpu.make_async_remote_copy(
            src_ref=source, dst_ref=target, send_sem=send.at[c, slot], recv_sem=recv.at[c, slot],
            device_id=device, device_id_type=pl.DeviceIdType.MESH,
        )
        item.start()
        started.append(item)
        return item

    held = [[None] * 10 for _ in range(n)]
    loads = []

    def stage(c, step):
        kept = held[c]
        cols = lanes(c)
        split = c % 2 == 0
        rows = pl.ds(y, 1) if split else pl.ds(0, 4)

        def part(a, b, d):
            return out.at[a, b, core, d, :, cols]

        def pass_on(slot, source, device):
            kept[slot] = go(c, slot, source, source, device)

        if step == 0:
            kept[0] = go(c, 0, own.at[rows, :, cols], part(z, x_hi, rows), across)
            load = pltpu.make_async_copy(own.at[rows, :, cols], part(z, x_hi, rows), local.at[c])
            load.start()
            loads.append(load)
        elif step == 1:
            loads[c].wait()
            kept[0].wait_recv()
            pass_on(1, part(z, slice(None), rows), z_next)
            pass_on(2, part(z, slice(None), rows), z_prev)
        elif step == 2:
            kept[1].wait_recv()
            kept[2].wait_recv()
            pass_on(3, part(zp, 0, rows), z_next)
            pass_on(4, part(zn, 1, rows), z_prev)
        elif step == 3:
            kept[3].wait_recv()
            kept[4].wait_recv()
            if split:
                pass_on(5, part(slice(None), slice(None), rows), y_next)
                pass_on(6, part(slice(None), slice(None), rows), y_prev)
            else:
                pass_on(9, part(slice(None), slice(None), rows), twin)
        elif step == 4 and split:
            kept[5].wait_recv()
            kept[6].wait_recv()
            pass_on(7, part(slice(None), 0, pl.ds(yp, 1)), y_next)
            pass_on(8, part(slice(None), 1, pl.ds(yn, 1)), y_prev)
        elif step == 5 and split:
            kept[7].wait_recv()
            kept[8].wait_recv()
            pass_on(9, part(slice(None), slice(None), slice(None)), twin)
        elif step == 6:
            kept[9].wait_recv()

    for step in range(7):
        for c in range(n):
            stage(c, step)
    for item in started:
        item.wait_send()


def gather_all(own):
    cols = own.shape[1]
    n = len(WIDTHS)
    out = pl.pallas_call(
        gather_kernel,
        out_shape=jax.ShapeDtypeStruct((4, 2, 2, 4, 16, cols), BF),
        in_specs=[pl.BlockSpec(memory_space=pl.ANY)],
        out_specs=pl.BlockSpec(memory_space=pl.ANY),
        scratch_shapes=[
            pltpu.SemaphoreType.DMA((n, 10)), pltpu.SemaphoreType.DMA((n, 10)), pltpu.SemaphoreType.DMA((n,))
        ],
        compiler_params=pltpu.CompilerParams(collective_id=2, has_side_effects=True),
        cost_estimate=pl.CostEstimate(flops=10**8, bytes_accessed=10**8, transcendentals=0),
    )(own.reshape(4, 16, cols))
    return out.reshape(1024, cols)


def rope_parts(length, start):
    half = AP // 2
    inverse = THETA ** (-2.0 * jnp.arange(half).astype(F32) / AP)
    angles = (start + jnp.arange(length)).astype(F32)[:, None] * inverse[None, :]
    cosine = jnp.cos(angles)
    sine = jnp.sin(angles)
    return jnp.concatenate([cosine] * 4, axis=1), jnp.concatenate([-sine, sine] * 2, axis=1)


def pad_lanes(value):
    return jnp.pad(value.astype(F32), (0, 128 - value.shape[0]))[None, :]


def per_device(
    seqs, hidden_in, norm_gain, mixer_proj, attn_proj, conv_kernel, conv_bias, step_bias, decay_log,
    skip_gain, gated_gain, mixer_out, attn_out, ffn_gain, gate_up, down_proj, out_grad,
):
    T = hidden_in.shape[1]
    width = norm_gain.shape[0]
    shards = 1024 // width
    me = lax.axis_index("seq")
    mix_rows, att_rows, down_rows = mixer_out.shape[0], attn_out.shape[0], down_proj.shape[0]

    small = jnp.concatenate(
        [norm_gain, ffn_gain, gated_gain, conv_bias, conv_kernel.T.reshape(-1)]
    )
    slots = width * 104
    small = jnp.pad(small, (0, slots - small.shape[0])).reshape(width, 104)
    front_shard = jnp.concatenate(
        [mixer_proj[:, : D_SSM + XBC], attn_proj, mixer_proj[:, D_SSM + XBC :], small], axis=1
    )
    front = gather_all(front_shard)
    tail_shard = jnp.concatenate(
        [
            gate_up[:, :FF],
            gate_up[:, FF:],
            jnp.concatenate([jnp.concatenate([mixer_out, attn_out], axis=0), down_proj], axis=1),
        ],
        axis=0,
    )
    tail = lax.all_gather(tail_shard, "fsdp", axis=0, tiled=False)
    smalls = front.reshape(shards, width, FRONT)[:, :, 4120:].reshape(shards, slots)
    cuts = []
    at = 0
    for size in (width, width, gated_gain.shape[0], conv_bias.shape[0]):
        cuts.append(smalls[:, at : at + size].reshape(1, -1).astype(F32))
        at += size
    gain_one, gain_ffn, gain_gated, bias_all = cuts
    kernel_size = conv_kernel.shape[0]
    taps = smalls[:, at : at + 4 * kernel_size].reshape(shards, 4, kernel_size)
    taps = taps.transpose(1, 0, 2).reshape(4, XBC).astype(F32)
    taps = jnp.pad(taps, ((0, 4), (0, 0)))

    resid = hidden_in[0].astype(F32)
    scale_one = rms_scale(resid)
    normed_one = resid * scale_one
    normed_in = (normed_one * gain_one).astype(BF)
    projection = dot(normed_in, front)
    gate_pre = projection[:, :D_SSM]
    cosine, sine = rope_parts(T, me * T)
    edge = projection[T - 8 :, D_SSM : D_SSM + XBC].astype(BF)
    halo = lax.ppermute(edge, "seq", [(i, i + 1) for i in range(seqs - 1)])
    sbias, dlog, skip = pad_lanes(step_bias), pad_lanes(decay_log), pad_lanes(skip_gain)
    act, dt, cum, fresh, xbc, steps, query_rot, kv_own = call(
        mamba_first,
        [
            ((T, XBC), F32), ((T, 128), F32), ((T, 128), F32), ((D_SSM, NST), BF), ((T, XBC), BF),
            ((T, 128), BF), ((T, QH * AP), BF), ((T, 2 * KVH * AP), BF),
        ],
        projection, halo, cosine, sine, taps, bias_all, sbias, dlog,
        scratch=[pltpu.VMEM((T + 8, XBC), F32)],
    )
    heads = MH // seqs
    states = ((seqs, heads * AP, NST), BF)
    pairs = ((seqs, T, 2 * KVH * AP), BF)
    tails = ((seqs, 8, 128), F32)
    heads_out = ((T, QH * AP), BF)
    starts, kv_all, ends, attn_tok, lse = share_call(
        share_forward, 3, [states, pairs, tails, heads_out, ((QH, T), F32)],
        [states, states, states, pairs, tails, ((QH * AP, T), F32), ((QH, T), F32), ((QH, T), F32)], 4,
        fresh.reshape(states[0]), cum[T - 8 :], kv_own, query_rot,
    )
    starts = starts.reshape(D_SSM, NST)
    (mixed_y,) = call(mamba_second, [((T, D_SSM), BF)], act, dt, cum, starts, skip)

    proj_gate = tail[:, :width].reshape(-1, FF)
    proj_up = tail[:, width : 2 * width].reshape(-1, FF)
    low_rows = 2 * width
    out_mixer = tail[:, low_rows : low_rows + mix_rows, :1024].reshape(-1, 1024)
    out_attn = tail[:, low_rows + mix_rows :, :1024].reshape(-1, 1024)
    proj_down = tail[:, low_rows:, 1024:].reshape(-1, 1024)
    mixed = mixed_y.astype(F32)
    gated = mixed * jax.nn.silu(gate_pre)
    scale_two = rms_scale(gated)
    normed_two = gated * scale_two
    normed_mix = (normed_two * gain_gated).astype(BF)
    middle = resid + dot(normed_mix, out_mixer) + dot(attn_tok, out_attn)
    scale_three = rms_scale(middle)
    normed_three = middle * scale_three
    normed_ffn = (normed_three * gain_ffn).astype(BF)
    gate_half = dot(normed_ffn, proj_gate)
    up_half = dot(normed_ffn, proj_up)
    activ = (jax.nn.silu(gate_half) * up_half).astype(BF)
    block_out = (middle + dot(activ, proj_down)).astype(BF)

    ograd = out_grad[0]
    grad_activ = dot(ograd, proj_down, NT)
    grad_down = dot(activ, ograd, TN).astype(BF)
    grad_g = (grad_activ * up_half * silu_slope(gate_half)).astype(BF)
    grad_u = (grad_activ * jax.nn.silu(gate_half)).astype(BF)
    grad_gateup = dot(normed_ffn, jnp.concatenate([grad_g, grad_u], axis=1), TN).astype(BF)
    grad_nffn = dot(grad_g, proj_gate, NT) + dot(grad_u, proj_up, NT)
    grad_ffn = jnp.sum(grad_nffn * normed_three, axis=0)
    grad_middle = ograd.astype(F32) + rms_back(grad_nffn * gain_ffn, normed_three, scale_three)
    middle_bf = grad_middle.astype(BF)
    grad_mixed = dot(normed_mix, middle_bf, TN).astype(BF)
    grad_attended = dot(attn_tok, middle_bf, TN).astype(BF)
    grad_nmix = dot(middle_bf, out_mixer, NT)
    grad_otok = dot(middle_bf, out_attn, NT).astype(BF)
    grad_gated = jnp.sum(grad_nmix * normed_two, axis=0)
    grad_gz = rms_back(grad_nmix * gain_gated, normed_two, scale_two)
    grad_ymix = (grad_gz * jax.nn.silu(gate_pre)).astype(BF)
    grad_gate = (grad_gz * mixed * silu_slope(gate_pre)).astype(BF)
    grad_outs = jnp.concatenate(
        [grad_mixed.reshape(shards, mix_rows, 1024), grad_attended.reshape(shards, att_rows, 1024)], axis=1
    ).reshape(-1, 1024)

    (dstart,) = call(mamba_back_first, [((D_SSM, NST), BF)], grad_ymix, act, cum)
    dends, qgrad, dkv = share_call(
        share_backward, 4, [states, heads_out, ((T, 2 * KVH * AP), BF)],
        [states, states, states, pairs, pairs, ((QH * AP, T), F32)], 3,
        dstart.reshape(states[0]), ends, query_rot, kv_all, attn_tok, lse, grad_otok, cosine, sine,
    )
    dends = dends.reshape(D_SSM, NST)
    dconv, dtaps, dbias, dsteps, dhead = call(
        mamba_back_second,
        [((T, XBC), F32), ((8, XBC), F32), ((8, XBC), F32), ((T, 128), BF), ((8, 128), F32)],
        grad_ymix, xbc, halo, act, dt, cum, starts, dends, steps, taps, bias_all, sbias, dlog, skip,
        scratch=[pltpu.VMEM((T + 8, XBC), F32), pltpu.VMEM((T, XBC), F32)],
        limit=32,
    )
    ahead = lax.ppermute(dconv[:8].astype(BF), "seq", [(i + 1, i) for i in range(seqs - 1)])
    (grad_proj,) = call(
        finish_grads, [((T, FRONT), BF)], dconv, ahead, taps, grad_gate, qgrad, dkv, dsteps,
        scratch=[pltpu.VMEM((T + 8, XBC), F32)],
    )

    grad_front = dot(normed_in, grad_proj, TN).astype(BF)
    grad_nin = dot(grad_proj, front, NT)
    grad_norm = jnp.sum(grad_nin * normed_one, axis=0)
    input_grad = grad_middle + rms_back(grad_nin * gain_one, normed_one, scale_one)
    vectors = [grad_norm, grad_ffn, grad_gated, dbias[0]] + [dtaps[lag] for lag in range(4)]
    vectors = [value.reshape(shards, -1) for value in vectors]
    vectors.append(jnp.broadcast_to(dhead[:3, :MH].reshape(1, 3 * MH), (shards, 3 * MH)))
    vectors = jnp.concatenate(vectors, axis=1)
    vectors = jnp.pad(vectors, ((0, 0), (0, slots - vectors.shape[1]))).astype(BF)
    last = jnp.concatenate([grad_front[:, 4096:4120], vectors.reshape(-1, 104)], axis=1)
    mixer_sum, attn_sum, vectors, gateup_sum, mixed_sum, attended_sum, down_sum = reduce_all(
        [lax.dynamic_update_slice(grad_front, last, (0, 4096)), grad_gateup, grad_outs, grad_down], REDUCED
    )
    vectors = vectors[:, 24:].reshape(-1)
    owned = []
    at = 0
    for size in [width, width, gated_gain.shape[0], kernel_size] + [kernel_size] * 4 + [MH] * 3:
        owned.append(vectors[at : at + size])
        at += size
    own_taps = jnp.stack(owned[4:8], axis=1)
    return (
        block_out[None],
        input_grad[None],
        owned[0],
        mixer_sum,
        attn_sum,
        own_taps,
        owned[3],
        owned[8],
        owned[9],
        owned[10],
        owned[2],
        mixed_sum,
        attended_sum,
        owned[1],
        gateup_sum,
        down_sum,
    )


def solution(mesh):
    tokens = P("fsdp", "seq", None)
    vector = P("fsdp")
    matrix = P("fsdp", None)
    in_specs = (
        tokens, vector, matrix, matrix, matrix, vector, P(), P(), P(), vector, matrix, matrix, vector,
        matrix, matrix, tokens,
    )
    out_specs = (
        tokens, tokens, vector, matrix, matrix, matrix, vector, P(), P(), P(), vector, matrix, matrix,
        vector, matrix, matrix,
    )
    return jax.shard_map(
        functools.partial(per_device, mesh.shape["seq"]),
        mesh=mesh, in_specs=in_specs, out_specs=out_specs, check_vma=False,
    )
```

```python
import functools
import math

import jax
import jax.numpy as jnp
from jax import lax
from jax.experimental import pallas as pl
from jax.experimental.pallas import tpu as pltpu
from jax.sharding import PartitionSpec as P

MH = 24
NST = 128
QH = 8
KVH = 2
AP = 64
FF = 2048
D_SSM = 1536
XBC = 1792
CIN = 3352
FRONT = 4224
EPSILON = 1e-05
THETA = 10000.0
HIGHEST = lax.Precision.HIGHEST
F32 = jnp.float32
BF = jnp.bfloat16
NT = (((1,), (1,)), ((), ()))
TN = (((0,), (0,)), ((), ()))


def dot(a, b, dims=(((1,), (0,)), ((), ())), precision=None):
    return lax.dot_general(a, b, dims, preferred_element_type=F32, precision=precision)


def silu_slope(value):
    sigma = jax.nn.sigmoid(value)
    return sigma * (1.0 + value * (1.0 - sigma))


def rms_scale(value):
    return lax.rsqrt(jnp.mean(value * value, axis=1, keepdims=True) + EPSILON)


def rms_back(grad_normed, normed, scale):
    return scale * (grad_normed - normed * jnp.mean(grad_normed * normed, axis=1, keepdims=True))


def head_selector(rows, cols):
    channel = lax.broadcasted_iota(jnp.int32, (rows, cols), 0)
    head = lax.broadcasted_iota(jnp.int32, (rows, cols), 1)
    return jnp.where((channel >= head * AP) & (channel < head * AP + AP), 1.0, 0.0).astype(F32)


def spread_heads(value):
    head = lax.broadcasted_iota(jnp.int32, (128, D_SSM), 0)
    channel = lax.broadcasted_iota(jnp.int32, (128, D_SSM), 1)
    select = jnp.where((channel >= head * AP) & (channel < head * AP + AP), 1.0, 0.0).astype(F32)
    return dot(value, select, precision=HIGHEST)


def gather_heads(value):
    return dot(value, head_selector(D_SSM, 128), precision=HIGHEST)


def conv_pre(ext, taps, bias, length):
    result = bias[...] + taps[3:4, :] * ext[8 : 8 + length, :]
    for lag in range(3):
        result = result + taps[lag : lag + 1, :] * ext[pl.ds(5 + lag, length), :]
    return result


def swap_halves(value):
    lane = lax.broadcasted_iota(jnp.int32, value.shape, 1)
    return jnp.where(lane % AP < AP // 2, pltpu.roll(value, 96, 1), pltpu.roll(value, 32, 1))


def mamba_first(
    proj, halo, cosine, sine, taps, bias, sbias, dlog,
    act_ref, dt_ref, cum_ref, fresh_ref, xbc_ref, steps_ref, q_ref, kv_ref, ext,
):
    length = proj.shape[0]
    for pair in range(QH // 2 + 1):
        at = D_SSM + XBC + pair * 128
        value = proj[:, at : at + 128].astype(BF).astype(F32)
        value = (value * cosine[...] + swap_halves(value) * sine[...]).astype(BF)
        if pair < QH // 2:
            q_ref[:, pair * 128 : pair * 128 + 128] = value * (1.0 / math.sqrt(AP))
        else:
            kv_ref[:, 0:128] = value
    kv_ref[:, 128:256] = proj[:, 3968:4096].astype(BF)
    xbc = proj[:, D_SSM : D_SSM + XBC].astype(BF)
    steps = proj[:, 4096:].astype(BF)
    xbc_ref[...] = xbc
    steps_ref[...] = steps
    ext[0:8, :] = halo[...].astype(F32)
    ext[8 : 8 + length, :] = xbc.astype(F32)
    conv = conv_pre(ext, taps, bias, length)
    act = conv * jax.nn.sigmoid(conv)
    act_ref[...] = act
    lane = lax.broadcasted_iota(jnp.int32, (length, 128), 1)
    raw = steps.astype(F32) + sbias[...]
    dt = jnp.maximum(raw, 0.0) + jnp.log1p(jnp.exp(-jnp.abs(raw)))
    dt = jnp.where(lane < MH, dt, 0.0)
    dt_ref[...] = dt
    row = lax.broadcasted_iota(jnp.int32, (length, length), 0)
    col = lax.broadcasted_iota(jnp.int32, (length, length), 1)
    lower = jnp.where(row >= col, 1.0, 0.0).astype(F32)
    cum = dot(lower, dt * (-jnp.exp(dlog[...])), precision=HIGHEST)
    cum_ref[...] = cum
    weight = spread_heads(jnp.exp(cum[length - 1 : length, :] - cum) * dt)
    scaled = (act[:, :D_SSM] * weight).astype(BF)
    fresh_ref[...] = dot(scaled, act[:, D_SSM : D_SSM + NST].astype(BF), TN).astype(BF)


def mamba_second(act, dt, cum, starts, skip, y_ref):
    length = act.shape[0]
    cumv = cum[...]
    cum_t = cumv.T
    bmat = act[:, D_SSM : D_SSM + NST].astype(BF)
    cmat = act[:, D_SSM + NST :].astype(BF)
    inner = dot(cmat, bmat, NT)
    row = lax.broadcasted_iota(jnp.int32, (length, length), 0)
    col = lax.broadcasted_iota(jnp.int32, (length, length), 1)
    inner = jnp.where(row >= col, inner, 0.0)
    x = act[:, :D_SSM]
    scaled = (x * spread_heads(dt[...])).astype(BF)
    outer = dot(cmat, starts[...], NT) * spread_heads(jnp.exp(cumv))
    base = outer + spread_heads(skip[...]) * x
    for pair in range(MH // 2):
        parts = []
        for h in (2 * pair, 2 * pair + 1):
            fade = jnp.exp(jnp.minimum(cumv[:, h : h + 1] - cum_t[h : h + 1, :], 0.0))
            parts.append(dot((inner * fade).astype(BF), scaled[:, h * AP : h * AP + AP]))
        lanes = slice(pair * 128, pair * 128 + 128)
        y_ref[:, lanes] = (base[:, lanes] + jnp.concatenate(parts, axis=1)).astype(BF)


def mamba_back_first(gy, act, cum, dstart_ref):
    rise = spread_heads(jnp.exp(cum[...]))
    cmat = act[:, D_SSM + NST :].astype(BF)
    dstart_ref[...] = dot((gy[...].astype(F32) * rise).astype(BF), cmat, TN).astype(BF)


def mamba_back_second(
    gy, xbc, halo, act, dt, cum, starts, dends, steps, taps, bias, sbias, dlog, skip,
    dconv_ref, dtaps_ref, dbias_ref, dsteps_ref, dhead_ref, ext, dact,
):
    length = act.shape[0]
    cumv = cum[...]
    dtv = dt[...]
    cum_t = cumv.T
    lane = lax.broadcasted_iota(jnp.int32, (length, 128), 1)
    bmat = act[:, D_SSM : D_SSM + NST].astype(BF)
    cmat = act[:, D_SSM + NST :].astype(BF)
    row = lax.broadcasted_iota(jnp.int32, (length, length), 0)
    col = lax.broadcasted_iota(jnp.int32, (length, length), 1)
    inner_t = jnp.where(col >= row, dot(bmat, cmat, NT), 0.0)
    x = act[:, :D_SSM]
    gyb = gy[...]
    gyf = gyb.astype(F32)
    dt_full = spread_heads(dtv)
    tail = spread_heads(jnp.exp(cumv[length - 1 : length, :] - cumv))
    rise = spread_heads(jnp.exp(cumv))
    xs = x * dt_full
    xsb = xs.astype(BF)
    ginner = jnp.zeros((length, length), F32)
    qcols = jnp.zeros((length, 128), F32)
    rrows = []
    for pair in range(MH // 2):
        parts = []
        for h in (2 * pair, 2 * pair + 1):
            lanes = slice(h * AP, h * AP + AP)
            fade = jnp.exp(jnp.minimum(cum_t[h : h + 1, :] - cumv[:, h : h + 1], 0.0))
            graded = dot(xsb[:, lanes], gyb[:, lanes], NT) * fade
            ginner = ginner + graded
            weighed = graded * inner_t
            rrows.append(jnp.sum(weighed, axis=0, keepdims=True))
            qcols = jnp.where(lane == h, jnp.sum(weighed, axis=1, keepdims=True), qcols)
            parts.append(dot((inner_t * fade).astype(BF), gyb[:, lanes]))
        dact[:, pair * 128 : pair * 128 + 128] = jnp.concatenate(parts, axis=1)
    ginner = jnp.where(col >= row, ginner, 0.0).astype(BF)
    rrows = jnp.concatenate(rrows + [jnp.zeros((128 - MH, length), F32)], axis=0).T
    endb = dends[...]
    startb = starts[...]
    from_end = dot(bmat, endb, NT) * tail
    dxs = dact[:, :D_SSM] + from_end
    reach = gather_heads(xs * from_end)
    outer = dot(cmat, startb, NT) * rise
    dcum = rrows - qcols + gather_heads(gyf * outer) - reach
    total = jnp.exp(cumv[length - 1 : length, :])
    carried = gather_heads_rows(startb, endb) * total + jnp.sum(reach, axis=0, keepdims=True)
    last = lax.broadcasted_iota(jnp.int32, (length, 128), 0) == length - 1
    dcum = dcum + jnp.where(last, carried, 0.0)
    upper = jnp.where(col >= row, 1.0, 0.0).astype(F32)
    rest = dot(upper, dcum, precision=HIGHEST)
    decay = -jnp.exp(dlog[...])
    ddt = gather_heads(x * dxs) + decay * rest
    ddecay = jnp.sum(dtv * rest, axis=0, keepdims=True) * decay
    raw = steps[...].astype(F32) + sbias[...]
    dsteps = jnp.where(lane < MH, ddt * jax.nn.sigmoid(raw), 0.0)
    dsteps_ref[...] = dsteps.astype(BF)
    dskip = gather_heads(jnp.sum(x * gyf, axis=0, keepdims=True))
    dhead_ref[0:1, :] = jnp.sum(dsteps, axis=0, keepdims=True)
    dhead_ref[1:2, :] = ddecay
    dhead_ref[2:3, :] = dskip
    dhead_ref[3:8, :] = jnp.zeros((5, 128), F32)
    dact[:, :D_SSM] = dt_full * dxs + spread_heads(skip[...]) * gyf
    dact[:, D_SSM : D_SSM + NST] = dot((xs * tail).astype(BF), endb) + dot(ginner, cmat)
    dact[:, D_SSM + NST :] = dot((gyf * rise).astype(BF), startb) + dot(ginner, bmat, TN)
    ext[0:8, :] = halo[...].astype(F32)
    ext[8 : 8 + length, :] = xbc[...].astype(F32)
    conv = conv_pre(ext, taps, bias, length)
    dconv = dact[...] * silu_slope(conv)
    dconv_ref[...] = dconv
    dbias_ref[...] = jnp.broadcast_to(jnp.sum(dconv, axis=0, keepdims=True), (8, XBC))
    for lag in range(4):
        dtaps_ref[lag : lag + 1, :] = jnp.sum(
            dconv * ext[pl.ds(5 + lag, length), :], axis=0, keepdims=True
        )
    dtaps_ref[4:8, :] = jnp.zeros((4, XBC), F32)


def gather_heads_rows(a, b):
    product = a.astype(F32) * b.astype(F32)
    per_row = dot(jnp.ones((8, NST), F32), product, NT, precision=HIGHEST)
    return gather_heads(per_row)[0:1, :]


def attend_block(q, kv, c, diagonal, acc, top, total):
    block = q.shape[0]
    if diagonal:
        key_at = lax.broadcasted_iota(jnp.int32, (block, block), 0)
        allowed = key_at <= lax.broadcasted_iota(jnp.int32, (block, block), 1)
    turned = kv[c, :, KVH * AP :].astype(F32).T.astype(BF)
    for h in range(QH):
        g = h // (QH // KVH)
        keys = kv[c, :, g * AP : g * AP + AP]
        values = turned[g * AP : g * AP + AP, :]
        s = dot(keys, q[:, h * AP : h * AP + AP], NT)
        band = slice(h * AP, h * AP + AP)
        if diagonal:
            s = jnp.where(allowed, s, -1e30)
            new = jnp.max(s, axis=0, keepdims=True)
            p = jnp.exp(s - new)
            total[h : h + 1, :] = jnp.sum(p, axis=0, keepdims=True)
            acc[band, :] = dot(values, p.astype(BF))
        else:
            old = top[h : h + 1, :]
            new = jnp.maximum(old, jnp.max(s, axis=0, keepdims=True))
            p = jnp.exp(s - new)
            fix = jnp.exp(old - new)
            total[h : h + 1, :] = total[h : h + 1, :] * fix + jnp.sum(p, axis=0, keepdims=True)
            acc[band, :] = acc[band, :] * fix + dot(values, p.astype(BF))
        top[h : h + 1, :] = new


def attend_back_block(q, kv, c, diagonal, lse, go, centre, dq_ref):
    block = q.shape[0]
    if diagonal:
        key_at = lax.broadcasted_iota(jnp.int32, (block, block), 0)
        allowed = key_at <= lax.broadcasted_iota(jnp.int32, (block, block), 1)
    turned = kv[c, :, : KVH * AP].astype(F32).T.astype(BF)
    sums = []
    for g in range(KVH):
        keys = kv[c, :, g * AP : g * AP + AP]
        values = kv[c, :, KVH * AP + g * AP : KVH * AP + g * AP + AP]
        dk = jnp.zeros((block, AP), F32)
        dv = jnp.zeros((block, AP), F32)
        for h in range(g * (QH // KVH), (g + 1) * (QH // KVH)):
            band = slice(h * AP, h * AP + AP)
            qh = q[:, band]
            gh = go[:, band]
            s = dot(keys, qh, NT) - lse[h : h + 1, :]
            p = jnp.exp(jnp.where(allowed, s, -1e30) if diagonal else s)
            dv = dv + dot(p.astype(BF), gh)
            dp = dot(values, gh, NT)
            ds = (p * (dp - centre[h : h + 1, :])).astype(BF)
            dk = dk + dot(ds, qh)
            part = dot(turned[g * AP : g * AP + AP, :], ds)
            dq_ref[band, :] = part if diagonal else dq_ref[band, :] + part
        sums.append((dk, dv))
    return (
        jnp.concatenate([sums[0][0], sums[1][0]], axis=1),
        jnp.concatenate([sums[0][1], sums[1][1]], axis=1),
    )


def finish_grads(dconv, ahead, taps, gate, dq, dkv, dsteps, out_ref, ext):
    length = dconv.shape[0]
    ext[0:length, :] = dconv[...]
    ext[length : length + 8, :] = ahead[...].astype(F32)
    du = taps[3:4, :] * ext[0:length, :]
    for lag in range(3):
        du = du + taps[lag : lag + 1, :] * ext[pl.ds(3 - lag, length), :]
    out_ref[:, :D_SSM] = gate[...]
    out_ref[:, D_SSM : D_SSM + XBC] = du.astype(BF)
    out_ref[:, 3328:3840] = dq[...]
    out_ref[:, 3840:4096] = dkv[...]
    out_ref[:, 4096:] = dsteps[...]


def call(kernel, outs, *args, scratch=(), limit=20):
    spec = pl.BlockSpec(memory_space=pltpu.VMEM)
    return pl.pallas_call(
        kernel,
        out_shape=[jax.ShapeDtypeStruct(shape, dtype) for shape, dtype in outs],
        in_specs=[spec] * len(args),
        out_specs=[spec] * len(outs),
        scratch_shapes=list(scratch),
        compiler_params=pltpu.CompilerParams(vmem_limit_bytes=limit << 20),
    )(*args)


def places():
    s, f = lax.axis_index("seq"), lax.axis_index("fsdp")
    return s // 2, s % 2, f // 4, (f // 2) % 2, f % 2


def at_place(y, x_lo, z, x_hi, core):
    return {"seq": y * 2 + x_lo, "fsdp": z * 4 + x_hi * 2 + core}


def greet(others):
    barrier = pltpu.get_barrier_semaphore()
    for other in others:
        pl.semaphore_signal(barrier, inc=1, device_id=other, device_id_type=pl.DeviceIdType.MESH)
    pl.semaphore_wait(barrier, len(others))


WIDTHS = (1024, 1024, 1024, 1152)


def reduce_kernel(chunks, *refs):
    n = len(chunks)
    count = max(chunk[0] for chunk in chunks) + 1
    inputs, outs, refs = refs[:count], refs[count : count + 7], refs[count + 7 :]
    groups = [refs[i * 10 : i * 10 + 10] for i in range(n)]
    refs = refs[n * 10 :]
    pieces, (send, recv, local) = refs[:count], refs[count:]
    y, x_lo, z, x_hi, core = places()
    yn, yp, yo = (y + 1) % 4, (y + 3) % 4, (y + 2) % 4
    zn, zp, zo = (z + 1) % 4, (z + 3) % 4, (z + 2) % 4
    y_next, y_prev = at_place(yn, x_lo, z, x_hi, core), at_place(yp, x_lo, z, x_hi, core)
    y_far = at_place(yo, x_lo, z, x_hi, core)
    z_next, z_prev = at_place(y, x_lo, zn, x_hi, core), at_place(y, x_lo, zp, x_hi, core)
    across = at_place(y, 1 - x_lo, z, 1 - x_hi, core)
    beside = at_place(y, 1 - x_lo, z, x_hi, core)
    twin = at_place(y, x_lo, z, x_hi, 1 - core)
    greet((y_next, y_prev, y_far, z_next, z_prev, across, beside, twin))

    def copy(c, slot, source, target, device):
        return pltpu.make_async_remote_copy(
            src_ref=source, dst_ref=target, send_sem=send.at[c, slot], recv_sem=recv.at[c, slot],
            device_id=device, device_id_type=pl.DeviceIdType.MESH,
        )

    started = []

    def go(c, slot, source, target, device):
        item = copy(c, slot, source, target, device)
        item.start()
        started.append(item)
        return item

    def lanes(c):
        return pl.ds(chunks[c][1], chunks[c][2])

    first = [[None] * 16 for _ in range(n)]
    loads = []
    for c in range(n):
        acc, twin_buf = groups[c][0], groups[c][1]
        g = inputs[chunks[c][0]]
        first[c][0] = go(c, 0, g.at[:, :, 1 - core, :, :, lanes(c)], twin_buf, twin)
        load = pltpu.make_async_copy(g.at[:, :, core, :, :, lanes(c)], acc, local.at[c])
        load.start()
        loads.append(load)

    def add(target, source):
        target[...] = target[...] + source[...]

    def stage(c, step):
        acc, twin_buf, p1, m1, p2, m2, q1, r1, q2, r2 = groups[c][:10]
        kept = first[c]
        gathered = pieces[chunks[c][0]]
        y_first = c % 2 == 0
        if step == 0:
            loads[c].wait()
            kept[0].wait_recv()

            def body(i, carry):
                a, b, d = i // 8, (i // 4) % 2, i % 4
                add(acc.at[a, b, d], twin_buf.at[a, b, d])
                return carry

            lax.fori_loop(0, 32, body, 0)
            if y_first:
                kept[1] = go(c, 1, acc.at[:, 0, yo], p1, y_next)
                kept[2] = go(c, 2, acc.at[:, 1, yo], m1, y_prev)
            else:
                kept[1] = go(c, 1, acc.at[zo, 0], p1, z_next)
                kept[2] = go(c, 2, acc.at[zo, 1], m1, z_prev)
        elif step == 1:
            kept[1].wait_recv()
            kept[2].wait_recv()

            def body(i, carry):
                if y_first:
                    add(acc.at[i, 0, yn], p1.at[i])
                    add(acc.at[i, 1, yp], m1.at[i])
                else:
                    add(acc.at[zn, 0, i], p1.at[i])
                    add(acc.at[zp, 1, i], m1.at[i])
                return carry

            lax.fori_loop(0, 4, body, 0)
            if y_first:
                kept[3] = go(c, 3, acc.at[:, :, yn], p2, y_next)
                kept[4] = go(c, 4, acc.at[:, :, yp], m2, y_prev)
            else:
                kept[3] = go(c, 3, acc.at[zn], p2, z_next)
                kept[4] = go(c, 4, acc.at[zp], m2, z_prev)
        elif step == 2:
            kept[3].wait_recv()
            kept[4].wait_recv()

            def body(i, carry):
                if y_first:
                    a, b = i // 2, i % 2
                    add(acc.at[a, b, y], p2.at[a, b])
                    add(acc.at[a, b, y], m2.at[a, b])
                else:
                    a, b = i // 4, i % 4
                    add(acc.at[z, a, b], p2.at[a, b])
                    add(acc.at[z, a, b], m2.at[a, b])
                return carry

            lax.fori_loop(0, 8, body, 0)
            if y_first:
                kept[5] = go(c, 5, acc.at[zo, 0, y], q1, z_next)
                kept[6] = go(c, 6, acc.at[zo, 1, y], r1, z_prev)
            else:
                kept[5] = go(c, 5, acc.at[z, 0, yo], q1, y_next)
                kept[6] = go(c, 6, acc.at[z, 1, yo], r1, y_prev)
        elif step == 3:
            kept[5].wait_recv()
            kept[6].wait_recv()
            if y_first:
                add(acc.at[zn, 0, y], q1)
                add(acc.at[zp, 1, y], r1)
                kept[7] = go(c, 7, acc.at[zn, :, y], q2, z_next)
                kept[8] = go(c, 8, acc.at[zp, :, y], r2, z_prev)
            else:
                add(acc.at[z, 0, yn], q1)
                add(acc.at[z, 1, yp], r1)
                kept[7] = go(c, 7, acc.at[z, :, yn], q2, y_next)
                kept[8] = go(c, 8, acc.at[z, :, yp], r2, y_prev)
        elif step == 4:
            kept[7].wait_recv()
            kept[8].wait_recv()
            for b in range(2):
                add(acc.at[z, b, y], q2.at[b])
                add(acc.at[z, b, y], r2.at[b])
            kept[9] = go(c, 9, acc.at[z, 1 - x_hi, y], gathered.at[4, :, lanes(c)], across)
        elif step == 5:
            kept[9].wait_recv()
            acc[z, x_hi, y] = acc[z, x_hi, y] + gathered[4, :, lanes(c)]
            kept[10] = go(c, 10, acc.at[z, x_hi, y], gathered.at[5, :, lanes(c)], beside)
        elif step == 6:
            kept[10].wait_recv()
            gathered[y, :, lanes(c)] = acc[z, x_hi, y] + gathered[5, :, lanes(c)]
            mine = gathered.at[y, :, lanes(c)]
            kept[11] = go(c, 11, mine, mine, y_next)
            kept[12] = go(c, 12, mine, mine, y_prev)
            kept[13] = go(c, 13, mine, mine, y_far)
        else:
            for slot in (11, 12, 13):
                kept[slot].wait_recv()

    for turn in range(n // 2 + 7):
        for c in reversed(range(n)):
            if 0 <= turn - c // 2 < 8:
                stage(c, turn - c // 2)
    mixer, attn, vector, gateup, mixed, attended, down = outs
    for i in range(4):
        mixer[i, :, : D_SSM + XBC] = pieces[0][i, :, : D_SSM + XBC].astype(F32)
        mixer[i, :, D_SSM + XBC :] = pieces[0][i, :, 4096:4120].astype(F32)
        attn[i] = pieces[0][i, :, 3328:4096].astype(F32)
        vector[i] = pieces[0][i, :, 4096:].astype(F32)
        gateup[i] = pieces[1][i].astype(F32)
        if i < 3:
            mixed[i] = pieces[2][i].astype(F32)
        else:
            attended[0] = pieces[2][i].astype(F32)
        down[i] = pieces[3][i].astype(F32)
    for item in started:
        item.wait_send()


def reduce_all(values, chunks):
    shapes = [(value.shape[0] // 64, value.shape[1]) for value in values]
    scratch = []
    for c, (which, _, w) in enumerate(chunks):
        r = shapes[which][0]
        scratch += [pltpu.VMEM((4, 2, 4, r, w), BF)] * 2 + [pltpu.VMEM((4, r, w), BF)] * 2
        scratch += [pltpu.VMEM((4, 2, r, w) if c % 2 == 0 else (2, 4, r, w), BF)] * 2
        scratch += [pltpu.VMEM((r, w), BF)] * 2 + [pltpu.VMEM((2, r, w), BF)] * 2
    n = len(chunks)
    scratch += [pltpu.VMEM((6,) + shape, BF) for shape in shapes]
    scratch += [pltpu.SemaphoreType.DMA((n, 14)), pltpu.SemaphoreType.DMA((n, 14)), pltpu.SemaphoreType.DMA((n,))]
    outs = [(4, 16, CIN), (4, 16, 768), (4, 16, 128), (4, 16, 2 * FF), (3, 32, 1024), (1, 32, 1024), (4, 32, 1024)]
    outs = pl.pallas_call(
        functools.partial(reduce_kernel, chunks),
        out_shape=[jax.ShapeDtypeStruct(shape, F32) for shape in outs],
        in_specs=[pl.BlockSpec(memory_space=pl.ANY)] * len(values),
        out_specs=[pl.BlockSpec(memory_space=pltpu.VMEM)] * len(outs),
        scratch_shapes=scratch,
        compiler_params=pltpu.CompilerParams(
            collective_id=1, has_side_effects=True, vmem_limit_bytes=60 << 20
        ),
        cost_estimate=pl.CostEstimate(flops=10**8, bytes_accessed=10**8, transcendentals=0),
    )(*[value.reshape((4, 2, 2, 4) + shape) for value, shape in zip(values, shapes)])
    return [out.reshape(-1, out.shape[2]) for out in outs]


REDUCED = (
    (2, 0, 1024), (3, 0, 1024), (1, 0, 1408), (1, 1408, 1408), (1, 2816, 1280), (0, 0, 1408), (0, 1408, 1408),
    (0, 2816, 1408),
)


def seq_group(s, send, recv):
    group = [{"seq": (s + d) % 8} for d in range(1, 8)]
    started = []

    def make(slot, d, source, target):
        return pltpu.make_async_remote_copy(
            src_ref=source, dst_ref=target, send_sem=send.at[slot, d % 8], recv_sem=recv.at[slot, d % 8],
            device_id={"seq": (s + d) % 8}, device_id_type=pl.DeviceIdType.MESH,
        )

    def go(slot, d, source, target):
        item = make(slot, d, source, target)
        item.start()
        started.append(item)
        return item

    return group, started, make, go


def fade_of(ends, c, head):
    lane = lax.broadcasted_iota(jnp.int32, (1, 128), 1)
    row = ends[c][7:8, :]
    return jnp.exp(jnp.sum(jnp.where(lane == head, row, 0.0), axis=1, keepdims=True))


def scan_states(ends, s, heads, got, made, order):
    for k in range(heads):
        rows = slice(k * AP, k * AP + AP)
        running = jnp.zeros((AP, NST), F32)
        for c in order:
            made[c, rows, :] = running.astype(BF)
            if c != order[-1]:
                running = running * fade_of(ends, c, s * heads + k) + got[c, rows, :].astype(F32)


def share_forward(
    fresh, last, kv, q, starts_out, kv_out, ends_out, o_ref, lse_ref,
    got, made, back, kv_all, ends, acc, top, total, send, recv,
):
    s = lax.axis_index("seq")
    group, started, make, go = seq_group(s, send, recv)
    kv_all[...] = jnp.zeros_like(kv_all)
    greet(group)
    waits = [[], []]
    for d in range(1, 8):
        waits[0].append(go(0, d, fresh.at[(s + d) % 8], got.at[s]))
        waits[0].append(go(1, d, last, ends.at[s]))
    for d in range(1, 8):
        pl.when(s + d < 8)(make(2, d, kv, kv_all.at[s]).start)
    got[s] = fresh[s]
    ends[s] = last[...]
    kv_all[s] = kv[...]
    attend_block(q, kv_all, s, True, acc, top, total)

    def step(d, carry):
        make(2, d, kv, kv_all.at[s]).wait_recv()
        attend_block(q, kv_all, s - d, False, acc, top, total)
        return carry

    half = (s + 1) // 2
    lax.fori_loop(1, half + 1, step, 0)
    for item in waits[0]:
        item.wait_recv()
    scan_states(ends, s, fresh.shape[1] // AP, got, made, list(range(8)))
    for d in range(1, 8):
        waits[1].append(go(3, d, made.at[(s + d) % 8], back.at[s]))
    back[s] = made[s]
    lax.fori_loop(half + 1, s + 1, step, 0)
    lse_ref[...] = top[...] + jnp.log(total[...])
    for pair in range(QH // 2):
        parts = []
        for h in (2 * pair, 2 * pair + 1):
            parts.append(acc[h * AP : h * AP + AP, :] / total[h : h + 1, :])
        o_ref[:, pair * 128 : pair * 128 + 128] = jnp.concatenate(parts, axis=0).T.astype(BF)
    for item in waits[1]:
        item.wait_recv()
    starts_out[...] = back[...]
    kv_out[...] = kv_all[...]
    ends_out[...] = ends[...]
    for d in range(1, 8):
        pl.when(s + d < 8)(make(2, d, kv, kv_all.at[s]).wait_send)
    for item in started:
        item.wait_send()


def share_backward(
    dstart, ends, q, kv, o, lse, go_ref, cosine, sine, dends_out, dq_out, dkv_out,
    got, made, back, kv_got, kv_made, dq, send, recv,
):
    s = lax.axis_index("seq")
    group, started, make, go = seq_group(s, send, recv)
    kv_got[...] = jnp.zeros_like(kv_got)
    greet(group)
    waits = [[], []]
    for d in range(1, 8):
        waits[0].append(go(0, d, dstart.at[(s + d) % 8], got.at[s]))
    got[s] = dstart[s]
    pick_h = lax.broadcasted_iota(jnp.int32, (8, QH * AP), 0)
    pick_c = lax.broadcasted_iota(jnp.int32, (8, QH * AP), 1)
    pick = jnp.where((pick_c >= pick_h * AP) & (pick_c < pick_h * AP + AP), 1.0, 0.0).astype(F32)
    centre = dot(pick, go_ref[...].astype(F32) * o[...].astype(F32), NT, precision=HIGHEST)
    own_k, own_v = attend_back_block(q, kv, s, True, lse, go_ref, centre, dq)
    for item in waits[0]:
        item.wait_recv()
    scan_states(ends, s, dstart.shape[1] // AP, got, made, list(range(7, -1, -1)))
    for d in range(1, 8):
        waits[1].append(go(2, d, made.at[(s + d) % 8], back.at[s]))
    back[s] = made[s]

    def sent(d):
        return make(1, 8 - d, kv_made.at[s - d], kv_got.at[s])

    def step(d, carry):
        dk, dv = attend_back_block(q, kv, s - d, False, lse, go_ref, centre, dq)
        kv_made[s - d, :, 0:128] = dk.astype(BF)
        kv_made[s - d, :, 128:256] = dv.astype(BF)
        sent(d).start()
        return carry

    lax.fori_loop(1, s + 1, step, 0)
    for pair in range(QH // 2):
        value = dq[pair * 128 : pair * 128 + 128, :].T * (1.0 / math.sqrt(AP))
        value = value * cosine[...] - swap_halves(value) * sine[...]
        dq_out[:, pair * 128 : pair * 128 + 128] = value.astype(BF)
    for d in range(1, 8):
        pl.when(s + d < 8)(make(1, 8 - d, kv_made.at[0], kv_got.at[s]).wait_recv)
    for c in range(8):
        own_k = own_k + kv_got[c, :, 0:128].astype(F32)
        own_v = own_v + kv_got[c, :, 128:256].astype(F32)
    dkv_out[:, 0:128] = (own_k * cosine[...] - swap_halves(own_k) * sine[...]).astype(BF)
    dkv_out[:, 128:256] = own_v.astype(BF)
    for item in waits[1]:
        item.wait_recv()
    dends_out[...] = back[...]
    for d in range(1, 8):
        pl.when(s - d >= 0)(make(1, 8 - d, kv_made.at[0], kv_got.at[s]).wait_send)
    for item in started:
        item.wait_send()


def share_call(kernel, collective, outs, scratch, slots, *args):
    spec = pl.BlockSpec(memory_space=pltpu.VMEM)
    return pl.pallas_call(
        kernel,
        out_shape=[jax.ShapeDtypeStruct(shape, dtype) for shape, dtype in outs],
        in_specs=[spec] * len(args),
        out_specs=[spec] * len(outs),
        scratch_shapes=[pltpu.VMEM(shape, dtype) for shape, dtype in scratch]
        + [pltpu.SemaphoreType.DMA((slots, 8))] * 2,
        compiler_params=pltpu.CompilerParams(
            collective_id=collective, has_side_effects=True, vmem_limit_bytes=32 << 20
        ),
        cost_estimate=pl.CostEstimate(flops=10**7, bytes_accessed=10**7, transcendentals=0),
    )(*args)


def gather_kernel(own, out, send, recv, local):
    n = len(WIDTHS)
    y, x_lo, z, x_hi, core = places()
    yn, yp, yo = (y + 1) % 4, (y + 3) % 4, (y + 2) % 4
    zn, zp, zo = (z + 1) % 4, (z + 3) % 4, (z + 2) % 4
    y_next, y_prev = at_place(yn, x_lo, z, x_hi, core), at_place(yp, x_lo, z, x_hi, core)
    z_next, z_prev = at_place(y, x_lo, zn, x_hi, core), at_place(y, x_lo, zp, x_hi, core)
    across = at_place(y, 1 - x_lo, z, 1 - x_hi, core)
    twin = at_place(y, x_lo, z, x_hi, 1 - core)
    greet((y_next, y_prev, z_next, z_prev, across, twin))
    started = []

    def lanes(c):
        return pl.ds(sum(WIDTHS[:c]), WIDTHS[c])

    def go(c, slot, source, target, device):
        item = pltpu.make_async_remote_copy(
            src_ref=source, dst_ref=target, send_sem=send.at[c, slot], recv_sem=recv.at[c, slot],
            device_id=device, device_id_type=pl.DeviceIdType.MESH,
        )
        item.start()
        started.append(item)
        return item

    held = [[None] * 10 for _ in range(n)]
    loads = []

    def stage(c, step):
        kept = held[c]
        cols = lanes(c)
        split = c % 2 == 0
        rows = pl.ds(y, 1) if split else pl.ds(0, 4)

        def part(a, b, d):
            return out.at[a, b, core, d, :, cols]

        def pass_on(slot, source, device):
            kept[slot] = go(c, slot, source, source, device)

        if step == 0:
            kept[0] = go(c, 0, own.at[rows, :, cols], part(z, x_hi, rows), across)
            load = pltpu.make_async_copy(own.at[rows, :, cols], part(z, x_hi, rows), local.at[c])
            load.start()
            loads.append(load)
        elif step == 1:
            loads[c].wait()
            kept[0].wait_recv()
            pass_on(1, part(z, slice(None), rows), z_next)
            pass_on(2, part(z, slice(None), rows), z_prev)
        elif step == 2:
            kept[1].wait_recv()
            kept[2].wait_recv()
            pass_on(3, part(zp, 0, rows), z_next)
            pass_on(4, part(zn, 1, rows), z_prev)
        elif step == 3:
            kept[3].wait_recv()
            kept[4].wait_recv()
            if split:
                pass_on(5, part(slice(None), slice(None), rows), y_next)
                pass_on(6, part(slice(None), slice(None), rows), y_prev)
            else:
                pass_on(9, part(slice(None), slice(None), rows), twin)
        elif step == 4 and split:
            kept[5].wait_recv()
            kept[6].wait_recv()
            pass_on(7, part(slice(None), 0, pl.ds(yp, 1)), y_next)
            pass_on(8, part(slice(None), 1, pl.ds(yn, 1)), y_prev)
        elif step == 5 and split:
            kept[7].wait_recv()
            kept[8].wait_recv()
            pass_on(9, part(slice(None), slice(None), slice(None)), twin)
        elif step == 6:
            kept[9].wait_recv()

    for step in range(7):
        for c in range(n):
            stage(c, step)
    for item in started:
        item.wait_send()


def gather_all(own):
    cols = own.shape[1]
    n = len(WIDTHS)
    out = pl.pallas_call(
        gather_kernel,
        out_shape=jax.ShapeDtypeStruct((4, 2, 2, 4, 16, cols), BF),
        in_specs=[pl.BlockSpec(memory_space=pl.ANY)],
        out_specs=pl.BlockSpec(memory_space=pl.ANY),
        scratch_shapes=[
            pltpu.SemaphoreType.DMA((n, 10)), pltpu.SemaphoreType.DMA((n, 10)), pltpu.SemaphoreType.DMA((n,))
        ],
        compiler_params=pltpu.CompilerParams(collective_id=2, has_side_effects=True),
        cost_estimate=pl.CostEstimate(flops=10**8, bytes_accessed=10**8, transcendentals=0),
    )(own.reshape(4, 16, cols))
    return out.reshape(1024, cols)


def rope_parts(length, start):
    half = AP // 2
    inverse = THETA ** (-2.0 * jnp.arange(half).astype(F32) / AP)
    angles = (start + jnp.arange(length)).astype(F32)[:, None] * inverse[None, :]
    cosine = jnp.cos(angles)
    sine = jnp.sin(angles)
    return jnp.concatenate([cosine] * 4, axis=1), jnp.concatenate([-sine, sine] * 2, axis=1)


def pad_lanes(value):
    return jnp.pad(value.astype(F32), (0, 128 - value.shape[0]))[None, :]


def per_device(
    seqs, hidden_in, norm_gain, mixer_proj, attn_proj, conv_kernel, conv_bias, step_bias, decay_log,
    skip_gain, gated_gain, mixer_out, attn_out, ffn_gain, gate_up, down_proj, out_grad,
):
    T = hidden_in.shape[1]
    width = norm_gain.shape[0]
    shards = 1024 // width
    me = lax.axis_index("seq")
    mix_rows, att_rows, down_rows = mixer_out.shape[0], attn_out.shape[0], down_proj.shape[0]

    small = jnp.concatenate(
        [norm_gain, ffn_gain, gated_gain, conv_bias, conv_kernel.T.reshape(-1)]
    )
    slots = width * 104
    small = jnp.pad(small, (0, slots - small.shape[0])).reshape(width, 104)
    front_shard = jnp.concatenate(
        [mixer_proj[:, : D_SSM + XBC], attn_proj, mixer_proj[:, D_SSM + XBC :], small], axis=1
    )
    front = gather_all(front_shard)
    tail_shard = jnp.concatenate(
        [
            gate_up[:, :FF],
            gate_up[:, FF:],
            jnp.concatenate([jnp.concatenate([mixer_out, attn_out], axis=0), down_proj], axis=1),
        ],
        axis=0,
    )
    tail = lax.all_gather(tail_shard, "fsdp", axis=0, tiled=False)
    smalls = front.reshape(shards, width, FRONT)[:, :, 4120:].reshape(shards, slots)
    cuts = []
    at = 0
    for size in (width, width, gated_gain.shape[0], conv_bias.shape[0]):
        cuts.append(smalls[:, at : at + size].reshape(1, -1).astype(F32))
        at += size
    gain_one, gain_ffn, gain_gated, bias_all = cuts
    kernel_size = conv_kernel.shape[0]
    taps = smalls[:, at : at + 4 * kernel_size].reshape(shards, 4, kernel_size)
    taps = taps.transpose(1, 0, 2).reshape(4, XBC).astype(F32)
    taps = jnp.pad(taps, ((0, 4), (0, 0)))

    resid = hidden_in[0].astype(F32)
    scale_one = rms_scale(resid)
    normed_one = resid * scale_one
    normed_in = (normed_one * gain_one).astype(BF)
    projection = dot(normed_in, front)
    gate_pre = projection[:, :D_SSM]
    cosine, sine = rope_parts(T, me * T)
    edge = projection[T - 8 :, D_SSM : D_SSM + XBC].astype(BF)
    halo = lax.ppermute(edge, "seq", [(i, i + 1) for i in range(seqs - 1)])
    sbias, dlog, skip = pad_lanes(step_bias), pad_lanes(decay_log), pad_lanes(skip_gain)
    act, dt, cum, fresh, xbc, steps, query_rot, kv_own = call(
        mamba_first,
        [
            ((T, XBC), F32), ((T, 128), F32), ((T, 128), F32), ((D_SSM, NST), BF), ((T, XBC), BF),
            ((T, 128), BF), ((T, QH * AP), BF), ((T, 2 * KVH * AP), BF),
        ],
        projection, halo, cosine, sine, taps, bias_all, sbias, dlog,
        scratch=[pltpu.VMEM((T + 8, XBC), F32)],
    )
    heads = MH // seqs
    states = ((seqs, heads * AP, NST), BF)
    pairs = ((seqs, T, 2 * KVH * AP), BF)
    tails = ((seqs, 8, 128), F32)
    heads_out = ((T, QH * AP), BF)
    starts, kv_all, ends, attn_tok, lse = share_call(
        share_forward, 3, [states, pairs, tails, heads_out, ((QH, T), F32)],
        [states, states, states, pairs, tails, ((QH * AP, T), F32), ((QH, T), F32), ((QH, T), F32)], 4,
        fresh.reshape(states[0]), cum[T - 8 :], kv_own, query_rot,
    )
    starts = starts.reshape(D_SSM, NST)
    (mixed_y,) = call(mamba_second, [((T, D_SSM), BF)], act, dt, cum, starts, skip)

    proj_gate = tail[:, :width].reshape(-1, FF)
    proj_up = tail[:, width : 2 * width].reshape(-1, FF)
    low_rows = 2 * width
    out_mixer = tail[:, low_rows : low_rows + mix_rows, :1024].reshape(-1, 1024)
    out_attn = tail[:, low_rows + mix_rows :, :1024].reshape(-1, 1024)
    proj_down = tail[:, low_rows:, 1024:].reshape(-1, 1024)
    mixed = mixed_y.astype(F32)
    gated = mixed * jax.nn.silu(gate_pre)
    scale_two = rms_scale(gated)
    normed_two = gated * scale_two
    normed_mix = (normed_two * gain_gated).astype(BF)
    middle = resid + dot(normed_mix, out_mixer) + dot(attn_tok, out_attn)
    scale_three = rms_scale(middle)
    normed_three = middle * scale_three
    normed_ffn = (normed_three * gain_ffn).astype(BF)
    gate_half = dot(normed_ffn, proj_gate)
    up_half = dot(normed_ffn, proj_up)
    activ = (jax.nn.silu(gate_half) * up_half).astype(BF)
    block_out = (middle + dot(activ, proj_down)).astype(BF)

    ograd = out_grad[0]
    grad_activ = dot(ograd, proj_down, NT)
    grad_down = dot(activ, ograd, TN).astype(BF)
    grad_g = (grad_activ * up_half * silu_slope(gate_half)).astype(BF)
    grad_u = (grad_activ * jax.nn.silu(gate_half)).astype(BF)
    grad_gateup = dot(normed_ffn, jnp.concatenate([grad_g, grad_u], axis=1), TN).astype(BF)
    grad_nffn = dot(grad_g, proj_gate, NT) + dot(grad_u, proj_up, NT)
    grad_ffn = jnp.sum(grad_nffn * normed_three, axis=0)
    grad_middle = ograd.astype(F32) + rms_back(grad_nffn * gain_ffn, normed_three, scale_three)
    middle_bf = grad_middle.astype(BF)
    grad_mixed = dot(normed_mix, middle_bf, TN).astype(BF)
    grad_attended = dot(attn_tok, middle_bf, TN).astype(BF)
    grad_nmix = dot(middle_bf, out_mixer, NT)
    grad_otok = dot(middle_bf, out_attn, NT).astype(BF)
    grad_gated = jnp.sum(grad_nmix * normed_two, axis=0)
    grad_gz = rms_back(grad_nmix * gain_gated, normed_two, scale_two)
    grad_ymix = (grad_gz * jax.nn.silu(gate_pre)).astype(BF)
    grad_gate = (grad_gz * mixed * silu_slope(gate_pre)).astype(BF)
    grad_outs = jnp.concatenate(
        [grad_mixed.reshape(shards, mix_rows, 1024), grad_attended.reshape(shards, att_rows, 1024)], axis=1
    ).reshape(-1, 1024)

    (dstart,) = call(mamba_back_first, [((D_SSM, NST), BF)], grad_ymix, act, cum)
    dends, qgrad, dkv = share_call(
        share_backward, 4, [states, heads_out, ((T, 2 * KVH * AP), BF)],
        [states, states, states, pairs, pairs, ((QH * AP, T), F32)], 3,
        dstart.reshape(states[0]), ends, query_rot, kv_all, attn_tok, lse, grad_otok, cosine, sine,
    )
    dends = dends.reshape(D_SSM, NST)
    dconv, dtaps, dbias, dsteps, dhead = call(
        mamba_back_second,
        [((T, XBC), F32), ((8, XBC), F32), ((8, XBC), F32), ((T, 128), BF), ((8, 128), F32)],
        grad_ymix, xbc, halo, act, dt, cum, starts, dends, steps, taps, bias_all, sbias, dlog, skip,
        scratch=[pltpu.VMEM((T + 8, XBC), F32), pltpu.VMEM((T, XBC), F32)],
        limit=32,
    )
    ahead = lax.ppermute(dconv[:8].astype(BF), "seq", [(i + 1, i) for i in range(seqs - 1)])
    (grad_proj,) = call(
        finish_grads, [((T, FRONT), BF)], dconv, ahead, taps, grad_gate, qgrad, dkv, dsteps,
        scratch=[pltpu.VMEM((T + 8, XBC), F32)],
    )

    grad_front = dot(normed_in, grad_proj, TN).astype(BF)
    grad_nin = dot(grad_proj, front, NT)
    grad_norm = jnp.sum(grad_nin * normed_one, axis=0)
    input_grad = grad_middle + rms_back(grad_nin * gain_one, normed_one, scale_one)
    vectors = [grad_norm, grad_ffn, grad_gated, dbias[0]] + [dtaps[lag] for lag in range(4)]
    vectors = [value.reshape(shards, -1) for value in vectors]
    vectors.append(jnp.broadcast_to(dhead[:3, :MH].reshape(1, 3 * MH), (shards, 3 * MH)))
    vectors = jnp.concatenate(vectors, axis=1)
    vectors = jnp.pad(vectors, ((0, 0), (0, slots - vectors.shape[1]))).astype(BF)
    last = jnp.concatenate([grad_front[:, 4096:4120], vectors.reshape(-1, 104)], axis=1)
    mixer_sum, attn_sum, vectors, gateup_sum, mixed_sum, attended_sum, down_sum = reduce_all(
        [lax.dynamic_update_slice(grad_front, last, (0, 4096)), grad_gateup, grad_outs, grad_down], REDUCED
    )
    vectors = vectors[:, 24:].reshape(-1)
    owned = []
    at = 0
    for size in [width, width, gated_gain.shape[0], kernel_size] + [kernel_size] * 4 + [MH] * 3:
        owned.append(vectors[at : at + size])
        at += size
    own_taps = jnp.stack(owned[4:8], axis=1)
    return (
        block_out[None],
        input_grad[None],
        owned[0],
        mixer_sum,
        attn_sum,
        own_taps,
        owned[3],
        owned[8],
        owned[9],
        owned[10],
        owned[2],
        mixed_sum,
        attended_sum,
        owned[1],
        gateup_sum,
        down_sum,
    )


def solution(mesh):
    tokens = P("fsdp", "seq", None)
    vector = P("fsdp")
    matrix = P("fsdp", None)
    in_specs = (
        tokens, vector, matrix, matrix, matrix, vector, P(), P(), P(), vector, matrix, matrix, vector,
        matrix, matrix, tokens,
    )
    out_specs = (
        tokens, tokens, vector, matrix, matrix, matrix, vector, P(), P(), P(), vector, matrix, matrix,
        vector, matrix, matrix,
    )
    return jax.shard_map(
        functools.partial(per_device, mesh.shape["seq"]),
        mesh=mesh, in_specs=in_specs, out_specs=out_specs, check_vma=False,
    )
```
